256 devices in a mesh: level: 2 (over core), blk: 128 (over z, x, y).
Axes of the slice: x: 4, y: 4, z: 8, core: 2. Of those that a mesh axis runs over, the one named last changes fastest.
Arguments:
- fluid_state: float32 [2, 2048, 5, 16, 256], P('level', 'blk'), may hold values from -0.5 to 4, as said below
- neighbours: int32 [2048, 6], replicated, may hold values from 0 to 2047, as said below
- parents: int32 [2048, 2], replicated, may hold values from 0 to 2047, as said below
Outputs:
- updated: float32 [2, 2048, 5, 16, 256], P('level', 'blk')
The draws below stay inside these ranges and needn't reach their ends.
Inputs may be any that keep to these rules, and one draw needn't show every extreme that they name: Row b lists the coarse blocks beyond block b's low and high face along x, then y, then z; the relation is symmetric (the block beyond b's high face along an axis has b beyond its low face along it); block g is held by blk index g // 16, never by the same device as its neighbours; among the (block, face) pairs of one device at most 2 have their neighbour on any one other device, and some pairs of devices reach 2; no block beside a parent is a parent. `parents`: row g gives the coarse parent of refined block g and g's octant in it (4 x half + 2 y half + z half); the parent is held by the same blk index as g; every parent has one child of each octant, so each device's refined blocks are the children of 2 of its coarse blocks. `fluid_state`: components are density, x, y, z momentum and total energy of states with density 0.6 to 1.6, velocity components -0.3 to 0.3 and pressure 0.7 to 1.4, gamma 1.4.
All inputs are finite; a program needn't handle non-finite values.
Results may differ from the reference program's by a relative error of at most 0.0003.
Values sent between devices are 32-bit elements; how exact they have to be, the bound alone decides.
A program may use at most 192 MiB of HBM per device.

```python
import math
import jax
import jax.numpy as jnp
from jax import lax

EDGE = 16
BLK_DEV = 16
BLOCKS = 2048


GAS_GAMMA = 1.4


def layout_of(key):
    device_count = BLOCKS // BLK_DEV
    span_size = device_count // 2
    parent_count = BLK_DEV // 8
    base_key = jax.random.fold_in(key, 1013)
    key_list = jax.random.split(base_key, 4)
    relabel = jax.random.permutation(key_list[0], BLK_DEV)
    offsets = (1 + (jax.random.permutation(key_list[1], 3 * BLK_DEV) + span_size - 1) % span_size).reshape(3, BLK_DEV)
    turn_sizes = jax.random.randint(key_list[2], (3,), parent_count, BLK_DEV - parent_count + 1)
    fine_order = jax.random.permutation(key_list[3], BLK_DEV)
    return (relabel, offsets, turn_sizes, fine_order)


def draw_neighbours(key, part):
    relabel, offsets, turn_sizes, fine_order = layout_of(key)
    device_count = BLOCKS // BLK_DEV
    canonical = jnp.argsort(relabel, stable=True)
    devices = jnp.arange(device_count)[:, None]
    canon_slots = jnp.broadcast_to(canonical[None, :], (device_count, BLK_DEV))
    columns = []
    for direction in range(3):
        upward = (canon_slots + turn_sizes[direction]) % BLK_DEV
        downward = (canon_slots - turn_sizes[direction]) % BLK_DEV
        high_device = (devices + offsets[direction][canon_slots]) % device_count
        low_device = (devices - offsets[direction][downward]) % device_count
        columns.append(low_device * BLK_DEV + relabel[downward])
        columns.append(high_device * BLK_DEV + relabel[upward])
    return jnp.stack(columns, axis=-1).reshape(BLOCKS, 6).astype(jnp.int32)


def draw_parents(key, part):
    relabel, offsets, turn_sizes, fine_order = layout_of(key)
    device_count = BLOCKS // BLK_DEV
    devices = jnp.arange(device_count)[:, None]
    child_ids = jnp.broadcast_to(fine_order[None, :], (device_count, BLK_DEV))
    parent = devices * BLK_DEV + relabel[child_ids // 8]
    octant = child_ids % 8
    return jnp.stack([parent, octant], axis=-1).reshape(BLOCKS, 2).astype(jnp.int32)


def draw_fluid_state(key, part):
    key_list = jax.random.split(jax.random.fold_in(key, 2027), 10)
    cell_shape = (2, BLOCKS, EDGE, EDGE * EDGE)

    def mixed(key_cell, key_block):
        return jax.random.uniform(key_cell, cell_shape)
    density = 0.6 + 1.0 * mixed(key_list[0], key_list[1])
    velocity = [-0.3 + 0.6 * mixed(key_list[2 + 2 * component], key_list[3 + 2 * component]) for component in range(3)]
    pressure = 0.7 + 0.7 * mixed(key_list[8], key_list[9])
    kinetic = velocity[0] * velocity[0] + velocity[1] * velocity[1] + velocity[2] * velocity[2]
    energy = pressure / (GAS_GAMMA - 1.0) + 0.5 * density * kinetic
    momenta = [density * velocity[component] for component in range(3)]
    return jnp.stack([density] + momenta + [energy], axis=2).astype(jnp.float32)


def setup_inputs(seed: int = 0) -> dict:
    seeds = jax.random.split(jax.random.key(seed), 4)
    fluid_state = draw_fluid_state(jax.random.fold_in(seeds[3], 71), 0)
    neighbours = draw_neighbours(jax.random.fold_in(seeds[3], 71), 0)
    parents = draw_parents(jax.random.fold_in(seeds[3], 71), 0)
    return {"fluid_state": fluid_state, "neighbours": neighbours, "parents": parents}


GAS_GAMMA = 1.4
STEP_RATIO = 0.12
OPPOSITE = (1, 0, 3, 2, 5, 4)
FACE_SIGNS = (-1.0, 1.0, -1.0, 1.0, -1.0, 1.0)
BIT_OF = (4, 2, 1)
TANGENT = ((2, 1), (4, 1), (4, 2))

def primitive(state_vec):
    density = state_vec[0]
    velocity = state_vec[1:4] / density
    pressure = (GAS_GAMMA - 1.0) * (state_vec[4] - 0.5 * lax.optimization_barrier(jnp.sum(state_vec[1:4] * velocity, axis=0)))
    return (density, velocity, pressure)

def physical_flux(state_vec, normal, density, velocity, pressure):
    normal_speed = velocity[normal]
    pieces = [state_vec[component] * normal_speed for component in range(4)]
    pieces.append((state_vec[4] + pressure) * normal_speed)
    pieces[1 + normal] = pieces[1 + normal] + pressure
    return jnp.stack(pieces)

def contact_flux(low_state, high_state, normal):
    density_low, velocity_low, pressure_low = primitive(low_state)
    density_high, velocity_high, pressure_high = primitive(high_state)
    sound_low = jnp.sqrt(GAS_GAMMA * pressure_low / density_low)
    sound_high = jnp.sqrt(GAS_GAMMA * pressure_high / density_high)
    speed_low = velocity_low[normal]
    speed_high = velocity_high[normal]
    slowest = jnp.minimum(speed_low - sound_low, speed_high - sound_high)
    fastest = jnp.maximum(speed_low + sound_low, speed_high + sound_high)
    mass_low = density_low * (slowest - speed_low)
    mass_high = density_high * (fastest - speed_high)
    contact = (pressure_high - pressure_low + speed_low * mass_low - speed_high * mass_high) / (mass_low - mass_high)
    flux_low = physical_flux(low_state, normal, density_low, velocity_low, pressure_low)
    flux_high = physical_flux(high_state, normal, density_high, velocity_high, pressure_high)

    def star_flux(state_vec, density, velocity, pressure, mass_flow, wave_speed, flux_here):
        factor = mass_flow / (wave_speed - contact)
        momenta = [factor * velocity[component] for component in range(3)]
        momenta[normal] = factor * contact
        energy = factor * (state_vec[4] / density + (contact - velocity[normal]) * (contact + pressure / mass_flow))
        star_state = jnp.stack([factor] + momenta + [energy])
        return flux_here + wave_speed * (star_state - state_vec)
    star_low = star_flux(low_state, density_low, velocity_low, pressure_low, mass_low, slowest, flux_low)
    star_high = star_flux(high_state, density_high, velocity_high, pressure_high, mass_high, fastest, flux_high)
    return jnp.where(slowest >= 0.0, flux_low, jnp.where(contact >= 0.0, star_low, jnp.where(fastest > 0.0, star_high, flux_high)))

def face_fluxes(padded, normal):
    step_below = padded[:, :, 1:-1] - padded[:, :, :-2]
    step_above = padded[:, :, 2:] - padded[:, :, 1:-1]
    limited = jnp.where(step_below * step_above > 0.0, jnp.sign(step_below) * jnp.minimum(jnp.abs(step_below), jnp.abs(step_above)), 0.0)
    centre = padded[:, :, 1:-1]
    low_face = centre - 0.5 * limited
    high_face = centre + 0.5 * limited
    change = 0.5 * STEP_RATIO * (physical_flux(low_face, normal, *primitive(low_face)) - physical_flux(high_face, normal, *primitive(high_face)))
    low_face = low_face + change
    high_face = high_face + change
    return contact_flux(high_face[:, :, :-1], low_face[:, :, 1:], normal)

def oriented(block_cells, direction):
    leading = block_cells.shape[:2]
    edge_cells = block_cells.shape[2]
    cube_cells = block_cells.reshape(leading + (edge_cells, edge_cells, edge_cells))
    if direction == 1:
        cube_cells = cube_cells.transpose(0, 1, 3, 2, 4)
    elif direction == 2:
        cube_cells = cube_cells.transpose(0, 1, 4, 2, 3)
    return cube_cells.reshape(leading + (edge_cells, edge_cells * edge_cells))

def restored(block_cells, direction):
    leading = block_cells.shape[:2]
    edge_cells = block_cells.shape[2]
    cube_cells = block_cells.reshape(leading + (edge_cells, edge_cells, edge_cells))
    if direction == 1:
        cube_cells = cube_cells.transpose(0, 1, 3, 2, 4)
    elif direction == 2:
        cube_cells = cube_cells.transpose(0, 1, 3, 4, 2)
    return cube_cells.reshape(leading + (edge_cells, edge_cells * edge_cells))

def advance(block_cells, ghosts):
    divergence = jnp.zeros_like(block_cells)
    boundary = []
    for direction in range(3):
        padded = jnp.concatenate([ghosts[2 * direction], oriented(block_cells, direction), ghosts[2 * direction + 1]], axis=2)
        fluxes = face_fluxes(padded, direction)
        divergence = divergence + restored(fluxes[:, :, 1:] - fluxes[:, :, :-1], direction)
        boundary.append(fluxes[:, :, 0])
        boundary.append(fluxes[:, :, -1])
    return (block_cells - STEP_RATIO * divergence, jnp.stack(boundary))

def face_slabs(block_cells, layers):
    edge_cells = block_cells.shape[2]
    pieces = []
    for direction in range(3):
        view_cells = oriented(block_cells, direction)
        pieces.append(view_cells[:, :, :layers])
        pieces.append(view_cells[:, :, edge_cells - layers:])
    return jnp.stack(pieces).transpose(2, 0, 1, 3, 4)

def inner_rim(ghost_slabs):
    return jnp.stack([ghost_slabs[:, face_id, :, 1 - face_id % 2] for face_id in range(6)], axis=1)

def flipped_octant(octants, mask_bit):
    return octants + mask_bit - 2 * mask_bit * (octants // mask_bit % 2)

def fine_ghosts(face_set, rims, octants, siblings):
    block_count = face_set.shape[0]
    edge_sq = face_set.shape[-1]
    half_edge = math.isqrt(edge_sq) // 2
    row_ids = jnp.arange(block_count)
    result = []
    for face_id in range(6):
        direction = face_id // 2
        side_id = face_id % 2
        outward = octants // BIT_OF[direction] % 2 == side_id
        first_bit = octants // TANGENT[direction][0] % 2
        second_bit = octants // TANGENT[direction][1] % 2
        coarse_rim = rims[:, face_id].reshape(block_count, 5, 2, half_edge, 2, half_edge)
        quarter = coarse_rim[row_ids, :, first_bit, :, second_bit, :]
        widened = jnp.repeat(jnp.repeat(quarter, 2, axis=2), 2, axis=3).reshape(block_count, 5, 1, edge_sq)
        from_coarse = jnp.concatenate([widened, widened], axis=2)
        from_sibling = face_set[siblings[:, direction], OPPOSITE[face_id]]
        result.append(jnp.where(outward[:, None, None, None], from_coarse, from_sibling))
    return jnp.stack(result).transpose(0, 2, 1, 3, 4)

def restricted(block_cells, flux_total, octants):
    block_count = block_cells.shape[1]
    half_edge = block_cells.shape[2] // 2
    averages = block_cells.reshape(5, block_count, half_edge, 2, half_edge, 2, half_edge, 2).sum(axis=(3, 5, 7)) * 0.125
    averages = averages.transpose(1, 0, 2, 3, 4)
    quarters = []
    for direction in range(3):
        outward_high = octants // BIT_OF[direction] % 2 == 1
        chosen = jnp.where(outward_high[None, :, None], flux_total[2 * direction + 1], flux_total[2 * direction])
        summed = chosen.reshape(5, block_count, half_edge, 2, half_edge, 2).sum(axis=(3, 5))
        quarters.append(summed.transpose(1, 0, 2, 3) * 0.125)
    return (averages, jnp.stack(quarters, axis=1))

def assemble(averages, quarters, children, coarse_faces):
    block_count = children.shape[0]
    half_edge = averages.shape[-1]
    edge_cells = 2 * half_edge
    picked = averages[children].reshape(block_count, 2, 2, 2, 5, half_edge, half_edge, half_edge)
    new_cells = picked.transpose(4, 0, 1, 5, 2, 6, 3, 7).reshape(5, block_count, edge_cells, edge_cells * edge_cells)
    deltas = []
    for face_id in range(6):
        direction = face_id // 2
        side_id = face_id % 2
        octant_list = []
        for first_bit in (0, 1):
            for second_bit in (0, 1):
                octant_list.append(side_id * BIT_OF[direction] + first_bit * TANGENT[direction][0] + second_bit * TANGENT[direction][1])
        chosen = quarters[children[:, jnp.array(octant_list, jnp.int32)]][:, :, direction]
        fine_face = chosen.reshape(block_count, 2, 2, 5, half_edge, half_edge).transpose(0, 3, 1, 4, 2, 5).reshape(block_count, 5, edge_cells * edge_cells)
        deltas.append(coarse_faces[face_id].transpose(1, 0, 2) - fine_face)
    return (new_cells, jnp.stack(deltas, axis=1))

def apply_corrections(block_cells, corrections):
    edge_cells = block_cells.shape[2]
    for direction in range(3):
        view_cells = oriented(block_cells, direction)
        view_cells = view_cells.at[:, :, 0].add(corrections[:, 2 * direction].transpose(1, 0, 2))
        view_cells = view_cells.at[:, :, edge_cells - 1].add(corrections[:, 2 * direction + 1].transpose(1, 0, 2))
        block_cells = restored(view_cells, direction)
    return block_cells

def stepped(block_cells, ghosts):
    total_blocks = block_cells.shape[1]
    groups = total_blocks // BLK_DEV
    edge_cells = block_cells.shape[2]
    edge_sq = block_cells.shape[3]
    grouped = block_cells.reshape(5, groups, BLK_DEV, edge_cells, edge_sq).transpose(1, 0, 2, 3, 4)
    grouped_ghosts = ghosts.reshape(6, 5, groups, BLK_DEV, 2, edge_sq).transpose(2, 0, 1, 3, 4, 5)
    new_cells, boundary = lax.map(lambda operands: advance(operands[0], operands[1]), (grouped, grouped_ghosts))
    new_cells = new_cells.transpose(1, 0, 2, 3, 4).reshape(5, total_blocks, edge_cells, edge_sq)
    boundary = boundary.transpose(1, 2, 0, 3, 4).reshape(6, 5, total_blocks, edge_sq)
    return (new_cells, boundary)

def reference(fluid_state, neighbours, parents):
    coarse = fluid_state[0].transpose(1, 0, 2, 3)
    refined_cells = fluid_state[1].transpose(1, 0, 2, 3)
    opposite = jnp.array(OPPOSITE, jnp.int32)

    def ghosts_of(face_set):
        return face_set[neighbours, opposite[None, :]]
    early_ghosts = ghosts_of(face_slabs(coarse, 2))
    coarse_new, coarse_faces = stepped(coarse, early_ghosts.transpose(1, 2, 0, 3, 4))
    late_ghosts = ghosts_of(face_slabs(coarse_new, 2))
    parent = parents[:, 0]
    octants = parents[:, 1]
    total_blocks = parents.shape[0]
    children = jnp.zeros((total_blocks, 8), jnp.int32).at[parent, octants].set(jnp.arange(total_blocks, dtype=jnp.int32))
    siblings = jnp.stack([children[parent, flipped_octant(octants, BIT_OF[direction])] for direction in range(3)], axis=1)
    early_rims = inner_rim(early_ghosts)[parent]
    late_rims = inner_rim(late_ghosts)[parent]
    fine_half, first_faces = stepped(refined_cells, fine_ghosts(face_slabs(refined_cells, 2), early_rims, octants, siblings))
    fine_out, second_faces = stepped(fine_half, fine_ghosts(face_slabs(fine_half, 2), 0.5 * (early_rims + late_rims), octants, siblings))
    averages, quarters = restricted(fine_out, first_faces + second_faces, octants)
    refined = jnp.zeros((total_blocks,), jnp.float32).at[parent].set(1.0)
    parent_cells, deltas = assemble(averages, quarters, children, coarse_faces)
    coarse_mixed = jnp.where(refined[None, :, None, None] > 0.0, parent_cells, coarse_new)
    deltas = deltas * refined[:, None, None, None]
    face_signs = jnp.array(FACE_SIGNS, jnp.float32)
    corrections = deltas[neighbours, opposite[None, :]] * face_signs[None, :, None, None] * STEP_RATIO
    coarse_out = apply_corrections(coarse_mixed, corrections)
    return jnp.stack([coarse_out, fine_out]).transpose(0, 2, 1, 3, 4)
```

```python
import jax
import jax.numpy as jnp
from jax import lax
from jax.experimental import pallas as pl
from jax.experimental.pallas import tpu as pltpu
from jax.sharding import PartitionSpec as P

GAMMA = 1.4
RATIO = 0.12
MESH = pl.DeviceIdType.MESH
ORDER = ((0, 1, 2, 3, 4), (0, 2, 1, 3, 4), (0, 3, 1, 2, 4))
BIT_OF = (4, 2, 1)
TANGENT = ((2, 1), (4, 1), (4, 2))
F32 = jnp.float32


def iota(axis):
    return lax.broadcasted_iota(jnp.int32, (8, 128), axis)


def take(tile, index):
    return jnp.take_along_axis(tile, index, axis=1, mode="promise_in_bounds")


def flip8(tiles):
    return jnp.swapaxes(jnp.stack(tiles), 0, 1)


def swap_groups(tiles):
    tiles = list(tiles)
    lane = iota(1)
    for step in (1, 2, 4):
        upper = (lane // 16) % (2 * step) >= step
        for i in range(8):
            if i & step == 0:
                a, b = tiles[i], tiles[i + step]
                tiles[i] = jnp.where(upper, pltpu.roll(b, 16 * step, 1), a)
                tiles[i + step] = jnp.where(upper, b, pltpu.roll(a, 128 - 16 * step, 1))
    return tiles


def swap_lanes(low, high, part):
    lane = iota(1)
    index = (lane % 8) * 16 + 8 * part + lane // 16
    return jnp.where(lane % 16 < 8, take(low, index), take(high, index))


def prim(q):
    inverse = 1.0 / q[0]
    speed = q[1] * inverse
    kinetic = (q[1] * q[1] + q[2] * q[2] + q[3] * q[3]) * inverse
    return inverse, speed, (GAMMA - 1.0) * (q[4] - 0.5 * kinetic)


def flux_of(q, speed, pressure):
    return [q[1], q[1] * speed + pressure, q[2] * speed, q[3] * speed, (q[4] + pressure) * speed]


def half_step(below, here, above, low_wanted=True, high_wanted=True):
    low, high = [], []
    for u0, u1, u2 in zip(below, here, above):
        a = u1 - u0
        b = u2 - u1
        slope = jnp.maximum(jnp.minimum(a, b), 0.0) + jnp.minimum(jnp.maximum(a, b), 0.0)
        low.append(u1 - 0.5 * slope)
        high.append(u1 + 0.5 * slope)
    _, speed, pressure = prim(low)
    flux_low = flux_of(low, speed, pressure)
    _, speed, pressure = prim(high)
    flux_high = flux_of(high, speed, pressure)
    change = [0.5 * RATIO * (a - b) for a, b in zip(flux_low, flux_high)]
    low = [a + b for a, b in zip(low, change)] if low_wanted else None
    high = [a + b for a, b in zip(high, change)] if high_wanted else None
    return low, high


def with_sound(q):
    inverse, speed, pressure = prim(q)
    return q, inverse, speed, pressure, jnp.sqrt(GAMMA * pressure * inverse)


def contact_flux(low, high):
    ql, il, ul, pl_, cl = with_sound(low)
    qh, ih, uh, ph, ch = with_sound(high)
    slowest = jnp.minimum(ul - cl, uh - ch)
    fastest = jnp.maximum(ul + cl, uh + ch)
    mass_l = ql[0] * (slowest - ul)
    mass_h = qh[0] * (fastest - uh)
    contact = (ph - pl_ + ul * mass_l - uh * mass_h) / (mass_l - mass_h)
    lower = jnp.logical_or(slowest >= 0.0, contact >= 0.0)
    q = [jnp.where(lower, a, b) for a, b in zip(ql, qh)]
    inverse = jnp.where(lower, il, ih)
    speed = jnp.where(lower, ul, uh)
    pressure = jnp.where(lower, pl_, ph)
    mass = jnp.where(lower, mass_l, mass_h)
    wave = jnp.where(lower, slowest, fastest)
    outside = jnp.logical_or(slowest >= 0.0, jnp.logical_and(contact < 0.0, fastest <= 0.0))
    flux = flux_of(q, speed, pressure)
    over = 1.0 / (wave - contact)
    factor = mass * over
    scaled = factor * inverse
    gap = contact - speed
    star = [
        factor,
        factor * contact,
        scaled * q[2],
        scaled * q[3],
        scaled * q[4] + gap * (factor * contact + pressure * over),
    ]
    return [jnp.where(outside, f, f + wave * (s - u)) for f, s, u in zip(flux, star, q)]


def cells(V, a, i, ch):
    return [V[a, c, i, ch] for c in range(5)]


def ghost(G, a, s, layer, ch):
    return [G[2 * a + s, c, layer, ch] for c in range(5)]


def inner_sweep(V, D):
    def body(n, carry):
        a = n // 4
        ch = n % 4
        states = [cells(V, a, i, ch) for i in range(3)]
        _, high = half_step(*states)
        previous = None
        for i in range(2, 15):
            states = [states[1], states[2], cells(V, a, i + 1, ch)]
            low, next_high = half_step(*states)
            flux = contact_flux(high, low)
            for c in range(5):
                D[a, c, i - 1, ch] = flux[c] if previous is None else flux[c] - previous[c]
            high, previous = next_high, flux
        for c in range(5):
            D[a, c, 14, ch] = -previous[c]
        return carry

    lax.fori_loop(0, 12, body, 0)


def outer_sweep(V, G, D, FC, first):
    def body(n, carry):
        a = n // 4
        ch = n % 4
        u = [cells(V, a, i, ch) for i in range(3)]
        g = [ghost(G, a, 0, layer, ch) for layer in range(2)]
        _, r_ghost = half_step(g[0], g[1], u[0], low_wanted=False)
        l0, r0 = half_step(g[1], u[0], u[1])
        l1, _ = half_step(u[0], u[1], u[2], high_wanted=False)
        f0 = contact_flux(r_ghost, l0)
        f1 = contact_flux(r0, l1)
        for c in range(5):
            D[a, c, 0, ch] = f1[c] - f0[c]
            D[a, c, 1, ch] = D[a, c, 1, ch] - f1[c]
            FC[2 * a, c, ch] = f0[c] if first else FC[2 * a, c, ch] + f0[c]
        u = [cells(V, a, i, ch) for i in (13, 14, 15)]
        g = [ghost(G, a, 1, layer, ch) for layer in range(2)]
        _, r0 = half_step(u[0], u[1], u[2], low_wanted=False)
        l1, r1 = half_step(u[1], u[2], g[0])
        l2, _ = half_step(u[2], g[0], g[1], high_wanted=False)
        f0 = contact_flux(r0, l1)
        f1 = contact_flux(r1, l2)
        for c in range(5):
            D[a, c, 14, ch] = D[a, c, 14, ch] + f0[c]
            D[a, c, 15, ch] = f1[c] - f0[c]
            FC[2 * a + 1, c, ch] = f1[c] if first else FC[2 * a + 1, c, ch] + f1[c]
        return carry

    lax.fori_loop(0, 12, body, 0)


def update(V, D):
    def body(n, carry):
        t = n % 2
        X = n // 2
        for c in range(5):
            ys = [
                swap_groups([D[1, ORDER[1].index(c), 8 * Y + j, 2 * X + t] for j in range(8)])
                for Y in range(2)
            ]
            zs = [
                swap_groups([D[2, ORDER[2].index(c), 8 * Z + j, 2 * X + t] for j in range(8)])
                for Z in range(2)
            ]
            for i in range(8):
                for Y in range(2):
                    total = D[0, c, 8 * X + i, 2 * Y + t] + ys[Y][i]
                    total = total + swap_lanes(zs[0][i], zs[1][i], Y)
                    V[0, c, 8 * X + i, 2 * Y + t] = V[0, c, 8 * X + i, 2 * Y + t] - RATIO * total
        return carry

    lax.fori_loop(0, 4, body, 0)


def make_views(V):
    def body(n, carry):
        t = n % 2
        X = n // 2
        for c in range(5):
            for Y in range(2):
                tiles = swap_groups([V[0, c, 8 * X + i, 2 * Y + t] for i in range(8)])
                for j in range(8):
                    V[1, ORDER[1].index(c), 8 * Y + j, 2 * X + t] = tiles[j]
            for Z in range(2):
                tiles = swap_groups(
                    [
                        swap_lanes(V[0, c, 8 * X + i, t], V[0, c, 8 * X + i, 2 + t], Z)
                        for i in range(8)
                    ]
                )
                for j in range(8):
                    V[2, ORDER[2].index(c), 8 * Z + j, 2 * X + t] = tiles[j]
        return carry

    lax.fori_loop(0, 4, body, 0)


def load_state(fluid, perm, V):
    def body(c, carry):
        for t in range(2):
            for X in range(2):
                for h in range(2):
                    rows = flip8(
                        [
                            fluid[0, perm[8 * t + j], c, 8 * X : 8 * X + 8, 128 * h : 128 * h + 128]
                            for j in range(8)
                        ]
                    )
                    for i in range(8):
                        V[0, c, 8 * X + i, 2 * h + t] = rows[i]
        return carry

    lax.fori_loop(0, 5, body, 0)


def store_state(V, out):
    def body(c, carry):
        for t in range(2):
            for X in range(2):
                for h in range(2):
                    rows = flip8([V[0, c, 8 * X + i, 2 * h + t] for i in range(8)])
                    for j in range(8):
                        out[8 * t + j, c, 8 * X : 8 * X + 8, 128 * h : 128 * h + 128] = rows[j]
        return carry

    lax.fori_loop(0, 5, body, 0)


def make_slabs(V, items):
    def body(n, carry):
        f = n // 2
        t = n % 2
        a = f // 2
        first = (f % 2) * 14
        for c in range(5):
            four = [V[a, c, first + layer, 2 * h + t] for layer in range(2) for h in range(2)]
            rows = flip8(four + four)
            for j in range(8):
                items[f * 16 + 8 * t + j, c] = rows[j]
        return carry

    lax.fori_loop(0, 12, body, 0)


def make_rims(V, items):
    def body(n, carry):
        f = n // 2
        t = n % 2
        a = f // 2
        layer = (f % 2) * 15
        for c in range(5):
            two = [V[a, c, layer, 2 * h + t] for h in range(2)]
            rows = flip8(two * 4)
            for j in range(8):
                items[f * 16 + 8 * t + j, c] = rows[j, 0:4]
        return carry

    lax.fori_loop(0, 12, body, 0)


def pack(items, slots, send, rows):
    first = lax.broadcasted_iota(jnp.int32, (rows, 128), 0) < rows // 2

    def body(d, carry):
        i0 = slots[2 * d]
        i1 = slots[2 * d + 1]
        for c in range(5):
            send[d, c] = jnp.where(first, items[i0, c], items[i1, c])
        return carry

    lax.fori_loop(0, send.shape[0], body, 0)


def collect_slabs(recv, where, slot_mask, G):
    def body(n, carry):
        f = n // 2
        t = n % 2
        second = slot_mask[n] > 0.5
        for c in range(5):
            rows = flip8([recv[where[f * 16 + 8 * t + j], c] for j in range(8)])
            for layer in range(2):
                for h in range(2):
                    r = 2 * layer + h
                    G[f, c, layer, 2 * h + t] = jnp.where(second, rows[4 + r], rows[r])
        return carry

    lax.fori_loop(0, 12, body, 0)


def fine_ghosts(V, rims, G, late=None):
    lane = iota(1)
    sub = iota(0)
    for f in range(6):
        a, s = f // 2, f % 2
        bit = BIT_OF[a]
        outer = (sub // bit) % 2 == s
        first = (sub // TANGENT[a][0]) % 2 == 1
        second = (sub // TANGENT[a][1]) % 2

        def body(n, carry):
            t = n % 2
            c = n // 2

            def row(h):
                value = rims[f, c, pl.ds(2 * t + h, 1), :]
                if late is not None:
                    value = 0.5 * (value + late[f, c, pl.ds(2 * t + h, 1), :])
                return jnp.broadcast_to(value, (8, 128))

            source = jnp.where(first, row(1), row(0))
            for h in range(2):
                index = (4 * h + lane // 32) * 16 + 8 * second + (lane % 16) // 2
                coarse = take(source, index)
                for layer in range(2):
                    near = V[a, c, (layer if s else 14 + layer), 2 * h + t]
                    near = pltpu.roll(near, (8 - bit) if s else bit, 0)
                    G[f, c, layer, 2 * h + t] = jnp.where(outer, coarse, near)
            return carry

        lax.fori_loop(0, 10, body, 0)


def pair_sums(low, high, bit):
    lane = iota(1)
    index = (lane // 16 % 4) * 32 + 2 * (lane % 8)
    sums = []
    for tile in (low, high):
        tile = tile + pltpu.roll(tile, 127, 1)
        sums.append(take(tile + pltpu.roll(tile, 112, 1), index))
    merged = jnp.where(lane < 64, sums[0], sums[1])
    return jnp.where(lane % 16 < 8, merged, pltpu.roll(merged, 8 - bit, 0))


def restrict(V, FC, mixed, means):
    def body(n, carry):
        t = n % 2
        c = n // 2
        merged = []
        for x in range(8):
            low, high = [
                V[0, c, 2 * x, 2 * h + t] + V[0, c, 2 * x + 1, 2 * h + t] for h in range(2)
            ]
            merged.append(pair_sums(low, high, 1) * 0.125)
        rows = flip8(merged)
        for X in range(2):
            for h in range(2):
                mixed[t, c, X, h] = rows[4 * X + 2 * h]
        return carry

    lax.fori_loop(0, 10, body, 0)

    for f in range(6):
        a, s = f // 2, f % 2

        def face_body(c, carry):
            for t in range(2):
                merged = pair_sums(FC[f, c, t], FC[f, c, 2 + t], TANGENT[a][1]) * 0.125
                for h in range(2):
                    o = s * BIT_OF[a] + h * TANGENT[a][0]
                    means[f, c, 2 * t + h : 2 * t + h + 1, :] = merged[o : o + 1]
            return carry

        lax.fori_loop(0, 5, face_body, 0)


def take_mixed(V, mixed):
    top = iota(0) == 0

    def body(n, carry):
        t = n % 2
        c = n // 2
        for x in range(16):
            for h in range(2):
                row = jnp.broadcast_to(mixed[t, c, x // 8, h, x % 8 : x % 8 + 1, :], (8, 128))
                V[0, c, x, 2 * h + t] = jnp.where(top, row, V[0, c, x, 2 * h + t])
        return carry

    lax.fori_loop(0, 10, body, 0)


def apply_corrections(recv, where, slot_mask, V):
    lane = iota(1)

    for f in range(6):
        a, s = f // 2, f % 2
        scale = RATIO if s else -RATIO

        def body(t, carry):
            second = slot_mask[2 * f + t] > 0.5
            for k in range(5):
                c = ORDER[a][k]
                tiles = [recv[where[f * 16 + 8 * t + j], k] for j in range(8)]
                rows = flip8([jnp.concatenate([tile, tile], axis=0) for tile in tiles])
                change = [scale * jnp.where(second, rows[2 + h], rows[h]) for h in range(2)]
                if a == 0:
                    for h in range(2):
                        V[0, c, 15 * s, 2 * h + t] = V[0, c, 15 * s, 2 * h + t] + change[h]
                    continue
                for x in range(16):
                    source = change[x // 8]
                    i = x % 8
                    if a == 1:
                        group = 7 * s
                        moved = pltpu.roll(source, (16 * (group - i)) % 128, 1)
                        moved = jnp.where(lane // 16 == group, moved, 0.0)
                        V[0, c, x, 2 * s + t] = V[0, c, x, 2 * s + t] + moved
                    else:
                        for h in range(2):
                            moved = take(source, i * 16 + 8 * h + lane // 16)
                            moved = jnp.where(lane % 16 == 15 * s, moved, 0.0)
                            V[0, c, x, 2 * h + t] = V[0, c, x, 2 * h + t] + moved
            return carry

        lax.fori_loop(0, 2, body, 0)


def step_kernel(
    devices,
    perm,
    slots,
    where,
    which,
    fluid,
    slot_mask,
    out,
    V,
    D,
    G,
    FC,
    items1,
    items2,
    items3,
    send1,
    recv1,
    send2,
    recv2,
    send3,
    recv3,
    early_out,
    early_in,
    late_out,
    late_in,
    mixed_out,
    mixed_in,
    means_out,
    means_in,
    send_sems,
    recv_sems,
    pair_send,
    pair_recv,
):
    level = lax.axis_index("level")
    me = lax.axis_index("blk")
    other = 1 - level
    barrier = pltpu.get_barrier_semaphore()

    def start_all(send, recv, n):
        def body(d, carry):
            pltpu.make_async_remote_copy(
                src_ref=send.at[d],
                dst_ref=recv.at[d],
                send_sem=send_sems.at[n],
                recv_sem=recv_sems.at[n],
                device_id=(level, lax.rem(me + d + 1, devices)),
                device_id_type=MESH,
            ).start()
            return carry

        lax.fori_loop(0, devices - 1, body, 0)

    def whole(send, recv, n):
        return pltpu.make_async_remote_copy(
            src_ref=send,
            dst_ref=recv,
            send_sem=send_sems.at[n],
            recv_sem=recv_sems.at[n],
            device_id=(level, lax.rem(me + 1, devices)),
            device_id_type=MESH,
        )

    def to_pair(source, target, n):
        return pltpu.make_async_remote_copy(
            src_ref=source,
            dst_ref=target,
            send_sem=pair_send.at[n],
            recv_sem=pair_recv.at[n],
            device_id=(other, me),
            device_id_type=MESH,
        )

    pl.semaphore_signal(barrier, inc=1, device_id=(other, me), device_id_type=MESH)

    @pl.when(level == 0)
    def _():
        def greet(d, carry):
            pl.semaphore_signal(
                barrier,
                inc=1,
                device_id=(level, lax.rem(me + d + 1, devices)),
                device_id_type=MESH,
            )
            return carry

        lax.fori_loop(0, devices - 1, greet, 0)
        pl.semaphore_wait(barrier, devices)

    @pl.when(level == 1)
    def _():
        pl.semaphore_wait(barrier, 1)

    load_state(fluid, perm, V)
    make_views(V)

    @pl.when(level == 0)
    def _():
        make_slabs(V, items1)
        pack(items1, slots, send1, 8)
        start_all(send1, recv1, 0)

        def clear(n, carry):
            for c in range(5):
                items3[n, c] = jnp.zeros((4, 128), F32)
            return carry

        lax.fori_loop(0, 96, clear, 0)

    inner_sweep(V, D)

    @pl.when(level == 0)
    def _():
        whole(send1, recv1, 0).wait_recv()
        collect_slabs(recv1, where, slot_mask, G)
        for f in range(6):
            for c in range(5):
                for t in range(2):
                    for h in range(2):
                        early_out[f, c, 2 * t + h : 2 * t + h + 1, :] = G[
                            f, c, 1 - f % 2, 2 * h + t, 0:1, :
                        ]
        to_pair(early_out, early_in, 0).start()

    @pl.when(level == 1)
    def _():
        to_pair(early_out, early_in, 0).wait_recv()
        fine_ghosts(V, early_in, G)

    outer_sweep(V, G, D, FC, True)
    update(V, D)
    make_views(V)

    @pl.when(level == 0)
    def _():
        make_rims(V, items2)
        pack(items2, slots, send2, 4)
        start_all(send2, recv2, 1)
        whole(send2, recv2, 1).wait_recv()
        for f in range(6):
            for t in range(2):
                item = f * 16 + 8 * t
                for c in range(5):
                    tile = recv2[where[item], c]
                    late_out[f, c, 2 * t : 2 * t + 2, :] = jnp.where(
                        which[item] == 1, tile[2:4], tile[0:2]
                    )
        to_pair(late_out, late_in, 1).start()

        to_pair(mixed_out, mixed_in, 2).wait_recv()
        to_pair(means_out, means_in, 3).wait_recv()
        for f in range(6):
            for t in range(2):
                for c in range(5):
                    for h in range(2):
                        delta = (
                            FC[f, c, 2 * h + t, 0:1, :]
                            - means_in[f, c, 2 * t + h : 2 * t + h + 1, :]
                        )
                        for k in range(2):
                            items3[f * 16 + 8 * t, c, 2 * k + h : 2 * k + h + 1, :] = delta
        pack(items3, slots, send3, 4)
        start_all(send3, recv3, 2)
        take_mixed(V, mixed_in)
        whole(send3, recv3, 2).wait_recv()
        apply_corrections(recv3, where, slot_mask, V)

    @pl.when(level == 1)
    def _():
        inner_sweep(V, D)
        to_pair(late_out, late_in, 1).wait_recv()
        fine_ghosts(V, early_in, G, late_in)
        outer_sweep(V, G, D, FC, False)
        update(V, D)
        restrict(V, FC, mixed_out, means_out)
        to_pair(mixed_out, mixed_in, 2).start()
        to_pair(means_out, means_in, 3).start()

    store_state(V, out)

    @pl.when(level == 0)
    def _():
        whole(send1, recv1, 0).wait_send()
        whole(send2, recv2, 1).wait_send()
        whole(send3, recv3, 2).wait_send()
        to_pair(early_out, early_in, 0).wait_send()
        to_pair(late_out, late_in, 1).wait_send()

    @pl.when(level == 1)
    def _():
        to_pair(mixed_out, mixed_in, 2).wait_send()
        to_pair(means_out, means_in, 3).wait_send()


def place_kernel(back, source, out):
    def body(b, carry):
        out[0, b] = source[back[b]]
        return carry

    lax.fori_loop(0, out.shape[1], body, 0)


def tables(neighbours, parents, level, me, count, devices):
    rows = lax.dynamic_slice_in_dim(neighbours, me * count, count, 0)
    family = lax.dynamic_slice_in_dim(parents, me * count, count, 0)
    ids = jnp.arange(count, dtype=jnp.int32)
    owner = family[:, 0] - me * count
    owns = owner[:, None] == ids[None, :]
    is_parent = jnp.any(owns, axis=0)
    earlier = ids[None, :] < ids[:, None]
    parent_rank = jnp.sum(is_parent[None, :] & earlier, axis=1, dtype=jnp.int32)
    rest_rank = ids - parent_rank
    coarse_place = jnp.where(
        is_parent, 8 * parent_rank, jnp.where(rest_rank < 7, 1 + rest_rank, 2 + rest_rank)
    )
    fine_place = 8 * jnp.sum(jnp.where(owns, parent_rank[None, :], 0), axis=1) + family[:, 1]
    place = jnp.where(level == 0, coarse_place, fine_place).astype(jnp.int32)

    def inverse(position):
        return jnp.sum(
            jnp.where(position[None, :] == ids[:, None], ids[None, :], 0), axis=1, dtype=jnp.int32
        )

    coarse_perm = inverse(coarse_place)
    chosen = coarse_perm[:, None] == ids[None, :]
    ordered = jnp.sum(jnp.where(chosen[:, :, None], rows[None], 0), axis=1, dtype=jnp.int32)
    ordered = ordered.T.reshape(-1)
    faces = jnp.repeat(jnp.arange(6, dtype=jnp.int32), count)
    target = ordered // count
    own_id = jnp.tile(coarse_perm, 6) * 6 + faces
    their_id = ordered % count * 6 + faces + 1 - 2 * (faces % 2)
    key = jnp.where(me < target, own_id, their_id)
    which = jnp.sum(
        (target[:, None] == target[None, :]) & (key[None, :] < key[:, None]),
        axis=1,
        dtype=jnp.int32,
    )
    to = (target - me + devices - 1) % devices
    come = (me - target + devices - 1) % devices
    item_ids = jnp.arange(6 * count, dtype=jnp.int32)
    slot_ids = jnp.arange(2 * devices, dtype=jnp.int32)
    slots = jnp.sum(
        jnp.where((2 * to + which)[None, :] == slot_ids[:, None], item_ids[None, :], 0),
        axis=1,
        dtype=jnp.int32,
    )
    mask = jnp.broadcast_to(which.astype(F32).reshape(12, 8, 1), (12, 8, 128))
    return inverse(place), place, slots, come, which, mask


def local(fluid_state, neighbours, parents):
    level = lax.axis_index("level")
    me = lax.axis_index("blk")
    devices = lax.axis_size("blk")
    count = fluid_state.shape[1]
    perm, place, slots, where, which, mask = tables(
        neighbours, parents, level, me, count, devices
    )
    smem = pl.BlockSpec(memory_space=pltpu.SMEM)
    vmem = pl.BlockSpec(memory_space=pltpu.VMEM)
    peers = devices - 1

    def step(*refs):
        step_kernel(devices, *refs)

    result = pl.pallas_call(
        step,
        out_shape=jax.ShapeDtypeStruct(fluid_state.shape[1:], F32),
        in_specs=[smem] * 4 + [vmem] * 2,
        out_specs=vmem,
        scratch_shapes=[
            pltpu.VMEM((3, 5, 16, 4, 8, 128), F32),
            pltpu.VMEM((3, 5, 16, 4, 8, 128), F32),
            pltpu.VMEM((6, 5, 2, 4, 8, 128), F32),
            pltpu.VMEM((6, 5, 4, 8, 128), F32),
            pltpu.VMEM((96, 5, 8, 128), F32),
            pltpu.VMEM((96, 5, 4, 128), F32),
            pltpu.VMEM((96, 5, 4, 128), F32),
            pltpu.VMEM((peers, 5, 8, 128), F32),
            pltpu.VMEM((peers, 5, 8, 128), F32),
            pltpu.VMEM((peers, 5, 4, 128), F32),
            pltpu.VMEM((peers, 5, 4, 128), F32),
            pltpu.VMEM((peers, 5, 4, 128), F32),
            pltpu.VMEM((peers, 5, 4, 128), F32),
            pltpu.VMEM((6, 5, 4, 128), F32),
            pltpu.VMEM((6, 5, 4, 128), F32),
            pltpu.VMEM((6, 5, 4, 128), F32),
            pltpu.VMEM((6, 5, 4, 128), F32),
            pltpu.VMEM((2, 5, 2, 2, 8, 128), F32),
            pltpu.VMEM((2, 5, 2, 2, 8, 128), F32),
            pltpu.VMEM((6, 5, 4, 128), F32),
            pltpu.VMEM((6, 5, 4, 128), F32),
            pltpu.SemaphoreType.DMA((3,)),
            pltpu.SemaphoreType.DMA((3,)),
            pltpu.SemaphoreType.DMA((4,)),
            pltpu.SemaphoreType.DMA((4,)),
        ],
        compiler_params=pltpu.CompilerParams(
            collective_id=0, has_side_effects=True, vmem_limit_bytes=60 * 1024 * 1024
        ),
    )(perm, slots, where, which, fluid_state, mask)
    return pl.pallas_call(
        place_kernel,
        out_shape=jax.ShapeDtypeStruct(fluid_state.shape, F32),
        in_specs=[smem, vmem],
        out_specs=vmem,
    )(place, result)


def solution(mesh):
    return jax.shard_map(
        local,
        mesh=mesh,
        in_specs=(P("level", "blk", None, None, None), P(), P()),
        out_specs=P("level", "blk", None, None, None),
        check_vma=False,
    )
```

```python
import jax
import jax.numpy as jnp
from jax import lax
from jax.experimental import pallas as pl
from jax.experimental.pallas import tpu as pltpu
from jax.sharding import PartitionSpec as P

GAMMA = 1.4
RATIO = 0.12
MESH = pl.DeviceIdType.MESH
ORDER = ((0, 1, 2, 3, 4), (0, 2, 1, 3, 4), (0, 3, 1, 2, 4))
BIT_OF = (4, 2, 1)
TANGENT = ((2, 1), (1, 4), (2, 4))
F32 = jnp.float32


def iota(axis):
    return lax.broadcasted_iota(jnp.int32, (8, 128), axis)


def take(tile, index):
    return jnp.take_along_axis(tile, index, axis=1, mode="promise_in_bounds")


def flip8(tiles):
    return jnp.swapaxes(jnp.stack(tiles), 0, 1)


def turn(tiles):
    whole = jnp.concatenate(tiles, axis=0).T
    return [whole[8 * i : 8 * i + 8] for i in range(16)]


def halves(tile):
    lane = iota(1)
    other = pltpu.roll(tile, 64, 1)
    return jnp.where(lane < 64, tile, other), jnp.where(lane < 64, other, tile)


def join(low, high, second):
    lane = iota(1)
    low = jnp.where(second, pltpu.roll(low, 64, 1), low)
    high = jnp.where(second, high, pltpu.roll(high, 64, 1))
    return jnp.where(lane < 64, low, high)


def prim(q):
    inverse = 1.0 / q[0]
    speed = q[1] * inverse
    kinetic = (q[1] * q[1] + q[2] * q[2] + q[3] * q[3]) * inverse
    return inverse, speed, (GAMMA - 1.0) * (q[4] - 0.5 * kinetic)


def flux_of(q, speed, pressure):
    return [q[1], q[1] * speed + pressure, q[2] * speed, q[3] * speed, (q[4] + pressure) * speed]


def half_step(below, here, above, low_wanted=True, high_wanted=True):
    low, high = [], []
    for u0, u1, u2 in zip(below, here, above):
        a = u1 - u0
        b = u2 - u1
        slope = jnp.maximum(jnp.minimum(a, b), 0.0) + jnp.minimum(jnp.maximum(a, b), 0.0)
        low.append(u1 - 0.5 * slope)
        high.append(u1 + 0.5 * slope)
    _, speed, pressure = prim(low)
    flux_low = flux_of(low, speed, pressure)
    _, speed, pressure = prim(high)
    flux_high = flux_of(high, speed, pressure)
    change = [0.5 * RATIO * (a - b) for a, b in zip(flux_low, flux_high)]
    low = [a + b for a, b in zip(low, change)] if low_wanted else None
    high = [a + b for a, b in zip(high, change)] if high_wanted else None
    return low, high


def with_sound(q):
    inverse, speed, pressure = prim(q)
    return q, inverse, speed, pressure, jnp.sqrt(GAMMA * pressure * inverse)


def contact_flux(low, high):
    ql, il, ul, pl_, cl = with_sound(low)
    qh, ih, uh, ph, ch = with_sound(high)
    slowest = jnp.minimum(ul - cl, uh - ch)
    fastest = jnp.maximum(ul + cl, uh + ch)
    mass_l = ql[0] * (slowest - ul)
    mass_h = qh[0] * (fastest - uh)
    contact = (ph - pl_ + ul * mass_l - uh * mass_h) / (mass_l - mass_h)
    lower = jnp.logical_or(slowest >= 0.0, contact >= 0.0)
    q = [jnp.where(lower, a, b) for a, b in zip(ql, qh)]
    inverse = jnp.where(lower, il, ih)
    speed = jnp.where(lower, ul, uh)
    pressure = jnp.where(lower, pl_, ph)
    mass = jnp.where(lower, mass_l, mass_h)
    wave = jnp.where(lower, slowest, fastest)
    outside = jnp.logical_or(slowest >= 0.0, jnp.logical_and(contact < 0.0, fastest <= 0.0))
    flux = flux_of(q, speed, pressure)
    over = 1.0 / (wave - contact)
    factor = mass * over
    scaled = factor * inverse
    gap = contact - speed
    star = [
        factor,
        factor * contact,
        scaled * q[2],
        scaled * q[3],
        scaled * q[4] + gap * (factor * contact + pressure * over),
    ]
    return [jnp.where(outside, f, f + wave * (s - u)) for f, s, u in zip(flux, star, q)]


def cells(V, a, i, ch):
    return [V[a, c, i, ch] for c in range(5)]


def ghost(G, a, s, layer, ch):
    return [G[2 * a + s, c, layer, ch] for c in range(5)]


def inner_sweep(V, D):
    def body(n, carry):
        a = n // 4
        ch = n % 4
        states = [cells(V, a, i, ch) for i in range(3)]
        _, high = half_step(*states)
        previous = None
        for i in range(2, 15):
            states = [states[1], states[2], cells(V, a, i + 1, ch)]
            low, next_high = half_step(*states)
            flux = contact_flux(high, low)
            for c in range(5):
                D[a, c, i - 1, ch] = flux[c] if previous is None else flux[c] - previous[c]
            high, previous = next_high, flux
        for c in range(5):
            D[a, c, 14, ch] = -previous[c]
        return carry

    lax.fori_loop(0, 12, body, 0)


def outer_sweep(V, G, D, FC, first):
    def body(n, carry):
        a = n // 4
        ch = n % 4
        u = [cells(V, a, i, ch) for i in range(3)]
        g = [ghost(G, a, 0, layer, ch) for layer in range(2)]
        _, r_ghost = half_step(g[0], g[1], u[0], low_wanted=False)
        l0, r0 = half_step(g[1], u[0], u[1])
        l1, _ = half_step(u[0], u[1], u[2], high_wanted=False)
        f0 = contact_flux(r_ghost, l0)
        f1 = contact_flux(r0, l1)
        for c in range(5):
            D[a, c, 0, ch] = f1[c] - f0[c]
            D[a, c, 1, ch] = D[a, c, 1, ch] - f1[c]
            FC[2 * a, c, ch] = f0[c] if first else FC[2 * a, c, ch] + f0[c]
        u = [cells(V, a, i, ch) for i in (13, 14, 15)]
        g = [ghost(G, a, 1, layer, ch) for layer in range(2)]
        _, r0 = half_step(u[0], u[1], u[2], low_wanted=False)
        l1, r1 = half_step(u[1], u[2], g[0])
        l2, _ = half_step(u[2], g[0], g[1], high_wanted=False)
        f0 = contact_flux(r0, l1)
        f1 = contact_flux(r1, l2)
        for c in range(5):
            D[a, c, 14, ch] = D[a, c, 14, ch] + f0[c]
            D[a, c, 15, ch] = f1[c] - f0[c]
            FC[2 * a + 1, c, ch] = f1[c] if first else FC[2 * a + 1, c, ch] + f1[c]
        return carry

    lax.fori_loop(0, 12, body, 0)


def update(N, D):
    def body(n, carry):
        X = n // 2
        h = n % 2
        for c in range(5):
            c1, c2 = ORDER[1].index(c), ORDER[2].index(c)
            tiles = [None] * 16
            for z in range(2):
                rows = flip8([D[2, c2, 8 * z + i, 2 * h + X] for i in range(8)])
                for y in range(8):
                    tiles[2 * y + z] = D[1, c1, 8 * h + y, 2 * z + X] + rows[y]
            tiles = turn(tiles)
            for t in range(2):
                rows = flip8([D[0, c, 8 * X + i, 2 * h + t] for i in range(8)])
                for j in range(8):
                    q = 8 * t + j
                    N[q, c, X, h] = N[q, c, X, h] - RATIO * (tiles[q] + rows[j])
        return carry

    lax.fori_loop(0, 4, body, 0)


def make_views(N, V, fluid=None, perm=None):
    def body(n, carry):
        X = n // 2
        h = n % 2
        for c in range(5):
            c1, c2 = ORDER[1].index(c), ORDER[2].index(c)
            tiles = []
            for q in range(16):
                if fluid is None:
                    tiles.append(N[q, c, X, h])
                else:
                    rows = pl.ds(pl.multiple_of(8 * X, 8), 8)
                    lanes = pl.ds(pl.multiple_of(128 * h, 128), 128)
                    tiles.append(fluid[0, perm[q], c, rows, lanes])
                    N[q, c, X, h] = tiles[q]
            for t in range(2):
                rows = flip8(tiles[8 * t : 8 * t + 8])
                for i in range(8):
                    V[0, c, 8 * X + i, 2 * h + t] = rows[i]
            tiles = turn(tiles)
            for z in range(2):
                for y in range(8):
                    V[1, c1, 8 * h + y, 2 * z + X] = tiles[2 * y + z]
                rows = flip8([tiles[2 * y + z] for y in range(8)])
                for i in range(8):
                    V[2, c2, 8 * z + i, 2 * h + X] = rows[i]
        return carry

    lax.fori_loop(0, 4, body, 0)


def store_state(N, out):
    def body(q, carry):
        for c in range(5):
            for X in range(2):
                for h in range(2):
                    out[q, c, 8 * X : 8 * X + 8, 128 * h : 128 * h + 128] = N[q, c, X, h]
        return carry

    lax.fori_loop(0, 16, body, 0)


def make_slabs(V, items):
    def x_body(n, carry):
        s = n // 2
        t = n % 2
        codes = [
            [V[0, c, 14 * s + layer, 2 * h + t] for layer in range(2) for h in range(2)]
            for c in range(5)
        ]
        last = [half for tile in codes[4] for half in halves(tile)]
        for g, tiles in enumerate((codes[0] + codes[1], codes[2] + codes[3], last)):
            rows = flip8(tiles)
            for j in range(8):
                items[s * 16 + 8 * t + j, g] = rows[j]
        return carry

    def body(n, carry):
        a = 1 + n // 2
        s = n % 2
        codes = [
            [V[a, c, 14 * s + layer, k] for layer in range(2) for k in range(4)] for c in range(5)
        ]
        for g, tiles in enumerate((codes[0] + codes[1], codes[2] + codes[3], codes[4] * 2)):
            tiles = turn(tiles)
            for q in range(16):
                items[(2 + n) * 16 + q, g] = tiles[q]
        return carry

    lax.fori_loop(0, 4, x_body, 0)
    lax.fori_loop(0, 4, body, 0)


def make_rims(V, items):
    def x_body(n, carry):
        s = n // 2
        t = n % 2
        codes = [[V[0, c, 15 * s, 2 * h + t] for h in range(2)] for c in range(5)]
        last = [half for tile in codes[4] for half in halves(tile)]
        for g, tiles in enumerate((codes[0] + codes[1] + codes[2] + codes[3], last * 2)):
            rows = flip8(tiles)
            for j in range(8):
                items[s * 16 + 8 * t + j, g] = rows[j]
        return carry

    def body(n, carry):
        a = 1 + n // 2
        s = n % 2
        codes = [[V[a, c, 15 * s, k] for k in range(4)] for c in range(5)]
        for g, tiles in enumerate((codes[0] + codes[1] + codes[2] + codes[3], codes[4] * 4)):
            tiles = turn(tiles)
            for q in range(16):
                items[(2 + n) * 16 + q, g] = tiles[q]
        return carry

    lax.fori_loop(0, 4, x_body, 0)
    lax.fori_loop(0, 4, body, 0)


def pack(items, slots, send):
    whole = items.shape[1] - 1

    def body(d, carry):
        lane = iota(1)
        i0 = slots[2 * d]
        i1 = slots[2 * d + 1]
        for g in range(whole):
            send[d, g] = items[i0, g]
            send[d, whole + g] = items[i1, g]
        send[d, 2 * whole] = jnp.where(lane < 64, items[i0, whole], items[i1, whole])
        return carry

    lax.fori_loop(0, send.shape[0], body, 0)


def collect_slabs(recv, where, which, row_mask, lane_mask, G):
    def x_body(n, carry):
        s = n // 2
        t = n % 2
        second = row_mask[n] > 0.5
        first = s * 16 + 8 * t
        for g in range(2):
            rows = flip8([recv[where[first + j], 2 * which[first + j] + g] for j in range(8)])
            for m in range(8):
                c, layer, h = 2 * g + m // 4, m // 2 % 2, m % 2
                G[s, c, layer, 2 * h + t] = rows[m]
        rows = flip8([recv[where[first + j], 4] for j in range(8)])
        for layer in range(2):
            for h in range(2):
                m = 2 * layer + h
                G[s, 4, layer, 2 * h + t] = join(rows[2 * m], rows[2 * m + 1], second)
        return carry

    def body(n, carry):
        second = lane_mask[n] > 0.5
        first = (2 + n) * 16
        for g in range(2):
            tiles = turn([recv[where[first + q], 2 * which[first + q] + g] for q in range(16)])
            for m in range(16):
                G[2 + n, 2 * g + m // 8, m // 4 % 2, m % 4] = tiles[m]
        tiles = turn([recv[where[first + q], 4] for q in range(16)])
        for m in range(8):
            G[2 + n, 4, m // 4, m % 4] = jnp.where(second, tiles[8 + m], tiles[m])
        return carry

    lax.fori_loop(0, 4, x_body, 0)
    lax.fori_loop(0, 4, body, 0)


def early_rims(G, rims):
    face = iota(1) // 8 % 8

    def body(c, carry):
        for k in range(4):
            tile = G[2, c, 1, k]
            for n in range(1, 4):
                tile = jnp.where(face == n, pltpu.roll(G[2 + n, c, 1 - n % 2, k], 8 * n, 1), tile)
            rims[4 * c + k] = tile
        for f in range(2):
            for t in range(2):
                for h in range(2):
                    r = 4 * f + 2 * t + h
                    rims[20 + c, r : r + 1, :] = G[f, c, 1 - f, 2 * h + t, 0:1, :]
        return carry

    lax.fori_loop(0, 5, body, 0)


def late_rims(recv, where, which, lane_mask, rims):
    for f in range(2):
        for t in range(2):
            item = f * 16 + 8 * t
            r = 4 * f + 2 * t
            tile = recv[where[item], which[item]]
            for c in range(4):
                rims[20 + c, r : r + 2, :] = tile[2 * c : 2 * c + 2]
            tile = recv[where[item], 2]
            joined = join(tile, pltpu.roll(tile, 7, 0), which[item] == 1)
            for h in range(2):
                rims[24, r + h : r + h + 1, :] = joined[2 * h : 2 * h + 1]
    items = [f * 16 + 8 * t for t in range(2) for _ in range(2) for f in range(2, 6)]
    tiles = turn([recv[where[i], which[i]] for i in items])
    for m in range(16):
        rims[m] = tiles[m]
    tiles = turn([recv[where[i], 2] for i in items])
    for m in range(4):
        rims[16 + m] = jnp.where(lane_mask[4] > 0.5, tiles[8 + m], tiles[m])


def spread_rows(tile, u):
    sub = iota(0)
    result = pltpu.roll(tile, 4, 0) if u else tile
    base = result
    for r in range(1, 5):
        result = jnp.where((sub + 1) // 2 == r, pltpu.roll(base, r, 0), result)
    return result


def fine_ghosts(V, rims, G, late=None):
    lane = iota(1)
    sub = iota(0)

    def rim(*index):
        value = rims[index]
        return value if late is None else 0.5 * (value + late[index])

    for f in range(2):
        outer = (sub // 4) % 2 == f
        first = (sub // 2) % 2 == 1
        second = sub % 2

        def x_body(c, carry):
            for t in range(2):
                r = 4 * f + 2 * t
                row = [
                    jnp.broadcast_to(rim(20 + c, pl.ds(r + h, 1), slice(None)), (8, 128))
                    for h in range(2)
                ]
                source = jnp.where(first, row[1], row[0])
                for h in range(2):
                    index = (4 * h + lane // 32) * 16 + 8 * second + (lane % 16) // 2
                    coarse = take(source, index)
                    for layer in range(2):
                        near = V[0, c, (layer if f else 14 + layer), 2 * h + t]
                        near = pltpu.roll(near, 4, 0)
                        G[f, c, layer, 2 * h + t] = jnp.where(outer, coarse, near)
            return carry

        lax.fori_loop(0, 5, x_body, 0)

    octant = lane // 8 % 8
    for f in range(2, 6):
        a, s = f // 2, f % 2
        bit = BIT_OF[a]
        outer = octant // bit % 2 == s
        first = octant // TANGENT[a][0] % 2 == 1
        second = octant // 4 == 1

        def body(c, carry):
            source = [rim(4 * c + k) for k in range(4)]
            for X in range(2):
                index = (lane // 64 * 8 + f - 2) * 8 + 4 * X + lane % 8 // 2
                four = [take(tile, index) for tile in source]
                low = jnp.where(second, four[1], four[0])
                high = jnp.where(second, four[3], four[2])
                chosen = jnp.where(first, high, low)
                for u in range(2):
                    coarse = spread_rows(chosen, u)
                    for layer in range(2):
                        near = V[a, c, (layer if s else 14 + layer), 2 * u + X]
                        near = pltpu.roll(near, (128 - 8 * bit) if s else 8 * bit, 1)
                        G[f, c, layer, 2 * u + X] = jnp.where(outer, coarse, near)
            return carry

        lax.fori_loop(0, 5, body, 0)


def pair_sums(low, high):
    lane = iota(1)
    index = (lane // 16 % 4) * 32 + 2 * (lane % 8)
    sums = []
    for tile in (low, high):
        tile = tile + pltpu.roll(tile, 127, 1)
        sums.append(take(tile + pltpu.roll(tile, 112, 1), index))
    merged = jnp.where(lane < 64, sums[0], sums[1])
    return jnp.where(lane % 16 < 8, merged, pltpu.roll(merged, 7, 0))


def restrict_cells(N, mixed):
    def body(n, carry):
        t = n % 2
        c = n // 2
        merged = []
        for X in range(2):
            rows = [flip8([N[8 * t + j, c, X, h] for j in range(8)]) for h in range(2)]
            for x in range(4):
                low, high = [rows[h][2 * x] + rows[h][2 * x + 1] for h in range(2)]
                merged.append(pair_sums(low, high) * 0.125)
        rows = flip8(merged)
        for X in range(2):
            for h in range(2):
                mixed[t, c, X, h] = rows[4 * X + 2 * h]
        return carry

    lax.fori_loop(0, 10, body, 0)


def restrict_faces(FC, means):
    lane = iota(1)
    sub = iota(0)

    def x_body(c, carry):
        for f in range(2):
            for t in range(2):
                merged = pair_sums(FC[f, c, t], FC[f, c, 2 + t]) * 0.125
                for h in range(2):
                    o = 4 * f + 2 * h
                    r = 4 * f + 2 * t + h
                    means[20 + c, r : r + 1, :] = merged[o : o + 1]
        return carry

    def body(c, carry):
        index = lane // 8 * 8 + 2 * (lane % 4)
        for n in range(4):
            result = None
            for u in range(2):
                sums = []
                for X in range(2):
                    tile = FC[2 + n, c, 2 * u + X]
                    tile = tile + pltpu.roll(tile, 127, 1)
                    sums.append(take(tile + pltpu.roll(tile, 7, 0), index))
                merged = jnp.where(lane % 8 < 4, sums[0], sums[1])
                for i in range(4):
                    moved = pltpu.roll(merged, (8 - i) % 8, 0) if u == 0 else pltpu.roll(merged, 4 - i, 0)
                    if result is None:
                        result = moved
                    else:
                        result = jnp.where(sub == 4 * u + i, moved, result)
            means[5 * n + c] = result * 0.125
        return carry

    lax.fori_loop(0, 5, x_body, 0)
    lax.fori_loop(0, 5, body, 0)


def make_deltas(FC, means, items):
    lane = lax.broadcasted_iota(jnp.int32, (1, 128), 1)
    for f in range(2):
        for t in range(2):
            item = f * 16 + 8 * t
            for c in range(5):
                for h in range(2):
                    r = 4 * f + 2 * t + h
                    delta = FC[f, c, 2 * h + t, 0:1, :] - means[20 + c, r : r + 1, :]
                    if c < 4:
                        items[item, 0, 2 * c + h : 2 * c + h + 1, :] = delta
                    else:
                        other = pltpu.roll(delta, 64, 1)
                        items[item, 1, 2 * h : 2 * h + 1, :] = jnp.where(lane < 64, delta, other)
                        items[item, 1, 2 * h + 1 : 2 * h + 2, :] = jnp.where(
                            lane < 64, other, delta
                        )
    for n in range(4):
        a, s = 1 + n // 2, n % 2
        codes = []
        for c in range(5):
            fine = means[5 * n + c]
            for k in range(4):
                o = s * BIT_OF[a] + (k // 2) * TANGENT[a][0] + (k % 2) * 4
                codes.append(FC[2 + n, c, k] - pltpu.roll(fine, (128 - 8 * o) % 128, 1))
        for g, tiles in enumerate((codes[:16], codes[16:] * 4)):
            tiles = turn(tiles)
            for t in range(2):
                items[(2 + n) * 16 + 8 * t, g] = tiles[8 * t]


def take_mixed(N, mixed):
    def body(c, carry):
        for t in range(2):
            for X in range(2):
                for h in range(2):
                    N[8 * t, c, X, h] = mixed[t, c, X, h]
        return carry

    lax.fori_loop(0, 5, body, 0)


def apply_corrections(recv, where, which, lane_mask, change, N):
    sub = iota(0)

    def x_body(q, carry):
        for s in range(2):
            scale = RATIO if s else -RATIO
            item = s * 16 + q
            e = where[item]
            k = which[item]
            tile = recv[e, 2]
            joined = join(tile, pltpu.roll(tile, 7, 0), k == 1)
            tile = recv[e, k]
            for c in range(5):
                for h in range(2):
                    row = tile[2 * c + h : 2 * c + h + 1] if c < 4 else joined[2 * h : 2 * h + 1]
                    row = jnp.broadcast_to(scale * row, (8, 128))
                    N[q, c, s, h] = N[q, c, s, h] + jnp.where(sub == 7 * s, row, 0.0)
        return carry

    lax.fori_loop(0, 16, x_body, 0)

    for n in range(4):
        scale = RATIO if n % 2 else -RATIO
        first = (2 + n) * 16
        tiles = turn([recv[where[first + q], which[first + q]] for q in range(16)])
        for m in range(16):
            change[n, m // 4, m % 4] = scale * tiles[m]
        tiles = turn([recv[where[first + q], 2] for q in range(16)])
        for m in range(4):
            change[n, 4, m] = scale * jnp.where(lane_mask[n] > 0.5, tiles[8 + m], tiles[m])

    def body(X, carry):
        for c in range(5):
            c1, c2 = ORDER[1].index(c), ORDER[2].index(c)
            for h in range(2):
                tiles = []
                for y in range(8):
                    for z in range(2):
                        row = jnp.broadcast_to(
                            change[2 + z, c2, 2 * h + X, y : y + 1, :], (8, 128)
                        )
                        tile = jnp.where(sub == 7 * z, row, 0.0)
                        if y == 7 * h:
                            tile = tile + change[h, c1, 2 * z + X]
                        tiles.append(tile)
                tiles = turn(tiles)
                for q in range(16):
                    N[q, c, X, h] = N[q, c, X, h] + tiles[q]
        return carry

    lax.fori_loop(0, 2, body, 0)


def step_kernel(
    devices,
    perm,
    slots,
    where,
    which,
    fluid,
    row_mask,
    lane_mask,
    out,
    N,
    V,
    D,
    G,
    FC,
    change,
    items1,
    items2,
    items3,
    send1,
    recv1,
    send2,
    recv2,
    send3,
    recv3,
    early_out,
    early_in,
    late_out,
    late_in,
    mixed_out,
    mixed_in,
    means_out,
    means_in,
    send_sems,
    recv_sems,
    pair_send,
    pair_recv,
    ready,
):
    level = lax.axis_index("level")
    me = lax.axis_index("blk")
    other = 1 - level
    barrier = pltpu.get_barrier_semaphore()

    def start_all(send, recv, n):
        def body(k, carry):
            d = lax.rem(k * 53 + 26, devices - 1)
            pltpu.make_async_remote_copy(
                src_ref=send.at[d],
                dst_ref=recv.at[d],
                send_sem=send_sems.at[n],
                recv_sem=recv_sems.at[n],
                device_id=(level, lax.rem(me + d + 1, devices)),
                device_id_type=MESH,
            ).start()
            return carry

        lax.fori_loop(0, devices - 1, body, 0)

    def whole(send, recv, n):
        return pltpu.make_async_remote_copy(
            src_ref=send,
            dst_ref=recv,
            send_sem=send_sems.at[n],
            recv_sem=recv_sems.at[n],
            device_id=(level, lax.rem(me + 1, devices)),
            device_id_type=MESH,
        )

    def to_pair(source, target, n):
        return pltpu.make_async_remote_copy(
            src_ref=source,
            dst_ref=target,
            send_sem=pair_send.at[n],
            recv_sem=pair_recv.at[n],
            device_id=(other, me),
            device_id_type=MESH,
        )

    def greet(semaphore, peers):
        for peer in peers:
            pl.semaphore_signal(
                semaphore, inc=1, device_id=(level, peer), device_id_type=MESH
            )

    plane = devices // 8
    far, mid, near = me // plane, me // 4 % 4, me % 4
    line_far = [lax.rem(far + i, 8) * plane + me % plane for i in range(1, 8)]
    line_mid = [far * plane + lax.rem(mid + i, 4) * 4 + near for i in range(1, 4)]
    line_near = [far * plane + mid * 4 + lax.rem(near + i, 4) for i in range(1, 4)]

    pl.semaphore_signal(barrier, inc=1, device_id=(other, me), device_id_type=MESH)

    @pl.when(level == 0)
    def _():
        greet(barrier, line_far + line_mid + line_near)

    make_views(N, V, fluid, perm)

    @pl.when(level == 0)
    def _():
        pl.semaphore_wait(barrier, 14)
        greet(ready.at[0], line_far)
        make_slabs(V, items1)
        pl.semaphore_wait(ready.at[0], 7)
        greet(ready.at[1], line_mid)
        pack(items1, slots, send1)
        pl.semaphore_wait(ready.at[1], 3)
        start_all(send1, recv1, 0)

        def clear(n, carry):
            for g in range(2):
                items3[n, g] = jnp.zeros((8, 128), F32)
            return carry

        lax.fori_loop(0, 96, clear, 0)

    @pl.when(level == 1)
    def _():
        pl.semaphore_wait(barrier, 1)

    inner_sweep(V, D)

    @pl.when(level == 0)
    def _():
        whole(send1, recv1, 0).wait_recv()
        collect_slabs(recv1, where, which, row_mask, lane_mask, G)
        early_rims(G, early_out)
        to_pair(early_out, early_in, 0).start()

    @pl.when(level == 1)
    def _():
        to_pair(early_out, early_in, 0).wait_recv()
        fine_ghosts(V, early_in, G)

    outer_sweep(V, G, D, FC, True)
    update(N, D)
    make_views(N, V)

    @pl.when(level == 0)
    def _():
        make_rims(V, items2)
        pack(items2, slots, send2)
        start_all(send2, recv2, 1)
        whole(send2, recv2, 1).wait_recv()
        late_rims(recv2, where, which, lane_mask, late_out)
        to_pair(late_out, late_in, 1).start()

        to_pair(means_out, means_in, 3).wait_recv()
        make_deltas(FC, means_in, items3)
        pack(items3, slots, send3)
        start_all(send3, recv3, 2)
        to_pair(mixed_out, mixed_in, 2).wait_recv()
        take_mixed(N, mixed_in)
        whole(send3, recv3, 2).wait_recv()
        apply_corrections(recv3, where, which, lane_mask, change, N)

    @pl.when(level == 1)
    def _():
        inner_sweep(V, D)
        to_pair(late_out, late_in, 1).wait_recv()
        fine_ghosts(V, early_in, G, late_in)
        outer_sweep(V, G, D, FC, False)
        restrict_faces(FC, means_out)
        to_pair(means_out, means_in, 3).start()
        update(N, D)
        restrict_cells(N, mixed_out)
        to_pair(mixed_out, mixed_in, 2).start()

    store_state(N, out)

    @pl.when(level == 0)
    def _():
        whole(send1, recv1, 0).wait_send()
        whole(send2, recv2, 1).wait_send()
        whole(send3, recv3, 2).wait_send()
        to_pair(early_out, early_in, 0).wait_send()
        to_pair(late_out, late_in, 1).wait_send()

    @pl.when(level == 1)
    def _():
        to_pair(mixed_out, mixed_in, 2).wait_send()
        to_pair(means_out, means_in, 3).wait_send()


def place_kernel(back, source, out):
    def body(b, carry):
        out[0, b] = source[back[b]]
        return carry

    lax.fori_loop(0, out.shape[1], body, 0)


def tables(neighbours, parents, level, me, count, devices):
    rows = lax.dynamic_slice_in_dim(neighbours, me * count, count, 0)
    family = lax.dynamic_slice_in_dim(parents, me * count, count, 0)
    ids = jnp.arange(count, dtype=jnp.int32)
    owner = family[:, 0] - me * count
    owns = owner[:, None] == ids[None, :]
    is_parent = jnp.any(owns, axis=0)
    earlier = ids[None, :] < ids[:, None]
    parent_rank = jnp.sum(is_parent[None, :] & earlier, axis=1, dtype=jnp.int32)
    rest_rank = ids - parent_rank
    coarse_place = jnp.where(
        is_parent, 8 * parent_rank, jnp.where(rest_rank < 7, 1 + rest_rank, 2 + rest_rank)
    )
    fine_place = 8 * jnp.sum(jnp.where(owns, parent_rank[None, :], 0), axis=1) + family[:, 1]
    place = jnp.where(level == 0, coarse_place, fine_place).astype(jnp.int32)

    def inverse(position):
        return jnp.sum(
            jnp.where(position[None, :] == ids[:, None], ids[None, :], 0), axis=1, dtype=jnp.int32
        )

    coarse_perm = inverse(coarse_place)
    chosen = coarse_perm[:, None] == ids[None, :]
    ordered = jnp.sum(jnp.where(chosen[:, :, None], rows[None], 0), axis=1, dtype=jnp.int32)
    ordered = ordered.T.reshape(-1)
    faces = jnp.repeat(jnp.arange(6, dtype=jnp.int32), count)
    target = ordered // count
    own_id = jnp.tile(coarse_perm, 6) * 6 + faces
    their_id = ordered % count * 6 + faces + 1 - 2 * (faces % 2)
    key = jnp.where(me < target, own_id, their_id)
    which = jnp.sum(
        (target[:, None] == target[None, :]) & (key[None, :] < key[:, None]),
        axis=1,
        dtype=jnp.int32,
    )
    to = (target - me + devices - 1) % devices
    come = (me - target + devices - 1) % devices
    item_ids = jnp.arange(6 * count, dtype=jnp.int32)
    slot_ids = jnp.arange(2 * devices, dtype=jnp.int32)
    slots = jnp.sum(
        jnp.where((2 * to + which)[None, :] == slot_ids[:, None], item_ids[None, :], 0),
        axis=1,
        dtype=jnp.int32,
    )
    second = which.astype(F32).reshape(6, count)
    row_mask = jnp.broadcast_to(second[:2].reshape(4, 8, 1), (4, 8, 128))
    late = jnp.concatenate([second[2:, 0], second[2:, 0], second[2:, 8], second[2:, 8]])
    lanes = jnp.concatenate([second[2:], late[None]])
    lane_mask = jnp.broadcast_to(jnp.repeat(lanes, 8, axis=1)[:, None, :], (5, 8, 128))
    return inverse(place), place, slots, come, which, row_mask, lane_mask


def local(fluid_state, neighbours, parents):
    level = lax.axis_index("level")
    me = lax.axis_index("blk")
    devices = lax.axis_size("blk")
    count = fluid_state.shape[1]
    perm, place, slots, where, which, row_mask, lane_mask = tables(
        neighbours, parents, level, me, count, devices
    )
    smem = pl.BlockSpec(memory_space=pltpu.SMEM)
    vmem = pl.BlockSpec(memory_space=pltpu.VMEM)
    peers = devices - 1

    def step(*refs):
        step_kernel(devices, *refs)

    result = pl.pallas_call(
        step,
        out_shape=jax.ShapeDtypeStruct(fluid_state.shape[1:], F32),
        in_specs=[smem] * 4 + [vmem] * 3,
        out_specs=vmem,
        scratch_shapes=[
            pltpu.VMEM((16, 5, 2, 2, 8, 128), F32),
            pltpu.VMEM((3, 5, 16, 4, 8, 128), F32),
            pltpu.VMEM((3, 5, 16, 4, 8, 128), F32),
            pltpu.VMEM((6, 5, 2, 4, 8, 128), F32),
            pltpu.VMEM((6, 5, 4, 8, 128), F32),
            pltpu.VMEM((4, 5, 4, 8, 128), F32),
            pltpu.VMEM((96, 3, 8, 128), F32),
            pltpu.VMEM((96, 2, 8, 128), F32),
            pltpu.VMEM((96, 2, 8, 128), F32),
            pltpu.VMEM((peers, 5, 8, 128), F32),
            pltpu.VMEM((peers, 5, 8, 128), F32),
            pltpu.VMEM((peers, 3, 8, 128), F32),
            pltpu.VMEM((peers, 3, 8, 128), F32),
            pltpu.VMEM((peers, 3, 8, 128), F32),
            pltpu.VMEM((peers, 3, 8, 128), F32),
            pltpu.VMEM((25, 8, 128), F32),
            pltpu.VMEM((25, 8, 128), F32),
            pltpu.VMEM((25, 8, 128), F32),
            pltpu.VMEM((25, 8, 128), F32),
            pltpu.VMEM((2, 5, 2, 2, 8, 128), F32),
            pltpu.VMEM((2, 5, 2, 2, 8, 128), F32),
            pltpu.VMEM((25, 8, 128), F32),
            pltpu.VMEM((25, 8, 128), F32),
            pltpu.SemaphoreType.DMA((3,)),
            pltpu.SemaphoreType.DMA((3,)),
            pltpu.SemaphoreType.DMA((4,)),
            pltpu.SemaphoreType.DMA((4,)),
            pltpu.SemaphoreType.REGULAR((2,)),
        ],
        compiler_params=pltpu.CompilerParams(
            collective_id=0, has_side_effects=True, vmem_limit_bytes=60 * 1024 * 1024
        ),
    )(perm, slots, where, which, fluid_state, row_mask, lane_mask)
    return pl.pallas_call(
        place_kernel,
        out_shape=jax.ShapeDtypeStruct(fluid_state.shape, F32),
        in_specs=[smem, vmem],
        out_specs=vmem,
    )(place, result)


def solution(mesh):
    return jax.shard_map(
        local,
        mesh=mesh,
        in_specs=(P("level", "blk", None, None, None), P(), P()),
        out_specs=P("level", "blk", None, None, None),
        check_vma=False,
    )
```

```python
import jax
import jax.numpy as jnp
from jax import lax
from jax.experimental import pallas as pl
from jax.experimental.pallas import tpu as pltpu
from jax.sharding import PartitionSpec as P

GAMMA = 1.4
RATIO = 0.12
MESH = pl.DeviceIdType.MESH
ORDER = ((0, 1, 2, 3, 4), (0, 2, 1, 3, 4), (0, 3, 1, 2, 4))
BIT_OF = (4, 2, 1)
TANGENT = ((2, 1), (1, 4), (2, 4))
F32 = jnp.float32


def send_order():
    offsets = [(z, x, y) for z in range(8) for x in range(4) for y in range(4)][1:]
    mixed = [offsets[(53 * k + 26) % 127] for k in range(127)]
    return sorted(mixed, key=lambda o: -(min(o[0], 8 - o[0]) + min(o[1], 4 - o[1]) + min(o[2], 4 - o[2])))


def iota(axis):
    return lax.broadcasted_iota(jnp.int32, (8, 128), axis)


def take(tile, index):
    return jnp.take_along_axis(tile, index, axis=1, mode="promise_in_bounds")


def flip8(tiles):
    return jnp.swapaxes(jnp.stack(tiles), 0, 1)


def turn(tiles):
    whole = jnp.concatenate(tiles, axis=0).T
    return [whole[8 * i : 8 * i + 8] for i in range(16)]


def halves(tile):
    lane = iota(1)
    other = pltpu.roll(tile, 64, 1)
    return jnp.where(lane < 64, tile, other), jnp.where(lane < 64, other, tile)


def join(low, high, second):
    lane = iota(1)
    low = jnp.where(second, pltpu.roll(low, 64, 1), low)
    high = jnp.where(second, high, pltpu.roll(high, 64, 1))
    return jnp.where(lane < 64, low, high)


def prim(q):
    inverse = 1.0 / q[0]
    speed = q[1] * inverse
    kinetic = (q[1] * q[1] + q[2] * q[2] + q[3] * q[3]) * inverse
    return inverse, speed, (GAMMA - 1.0) * (q[4] - 0.5 * kinetic)


def flux_of(q, speed, pressure):
    return [q[1], q[1] * speed + pressure, q[2] * speed, q[3] * speed, (q[4] + pressure) * speed]


def half_step(below, here, above, low_wanted=True, high_wanted=True):
    low, high = [], []
    for u0, u1, u2 in zip(below, here, above):
        a = u1 - u0
        b = u2 - u1
        slope = jnp.maximum(jnp.minimum(a, b), 0.0) + jnp.minimum(jnp.maximum(a, b), 0.0)
        low.append(u1 - 0.5 * slope)
        high.append(u1 + 0.5 * slope)
    _, speed, pressure = prim(low)
    flux_low = flux_of(low, speed, pressure)
    _, speed, pressure = prim(high)
    flux_high = flux_of(high, speed, pressure)
    change = [0.5 * RATIO * (a - b) for a, b in zip(flux_low, flux_high)]
    low = [a + b for a, b in zip(low, change)] if low_wanted else None
    high = [a + b for a, b in zip(high, change)] if high_wanted else None
    return low, high


def with_sound(q):
    inverse, speed, pressure = prim(q)
    return q, inverse, speed, pressure, jnp.sqrt(GAMMA * pressure * inverse)


def contact_flux(low, high):
    ql, il, ul, pl_, cl = with_sound(low)
    qh, ih, uh, ph, ch = with_sound(high)
    slowest = jnp.minimum(ul - cl, uh - ch)
    fastest = jnp.maximum(ul + cl, uh + ch)
    mass_l = ql[0] * (slowest - ul)
    mass_h = qh[0] * (fastest - uh)
    contact = (ph - pl_ + ul * mass_l - uh * mass_h) / (mass_l - mass_h)
    lower = jnp.logical_or(slowest >= 0.0, contact >= 0.0)
    q = [jnp.where(lower, a, b) for a, b in zip(ql, qh)]
    inverse = jnp.where(lower, il, ih)
    speed = jnp.where(lower, ul, uh)
    pressure = jnp.where(lower, pl_, ph)
    mass = jnp.where(lower, mass_l, mass_h)
    wave = jnp.where(lower, slowest, fastest)
    outside = jnp.logical_or(slowest >= 0.0, jnp.logical_and(contact < 0.0, fastest <= 0.0))
    flux = flux_of(q, speed, pressure)
    over = 1.0 / (wave - contact)
    factor = mass * over
    scaled = factor * inverse
    gap = contact - speed
    star = [
        factor,
        factor * contact,
        scaled * q[2],
        scaled * q[3],
        scaled * q[4] + gap * (factor * contact + pressure * over),
    ]
    return [jnp.where(outside, f, f + wave * (s - u)) for f, s, u in zip(flux, star, q)]


def cells(V, a, i, ch):
    return [V[a, c, i, ch] for c in range(5)]


def ghost(G, a, s, layer, ch):
    return [G[2 * a + s, c, layer, ch] for c in range(5)]


def inner_sweep(V, D):
    def body(n, carry):
        a = n // 4
        ch = n % 4
        states = [cells(V, a, i, ch) for i in range(3)]
        _, high = half_step(*states)
        previous = None
        for i in range(2, 15):
            states = [states[1], states[2], cells(V, a, i + 1, ch)]
            low, next_high = half_step(*states)
            flux = contact_flux(high, low)
            for c in range(5):
                D[a, c, i - 1, ch] = flux[c] if previous is None else flux[c] - previous[c]
            high, previous = next_high, flux
        for c in range(5):
            D[a, c, 14, ch] = -previous[c]
        return carry

    lax.fori_loop(0, 12, body, 0)


def outer_sweep(V, G, D, FC, first):
    def body(n, carry):
        a = n // 4
        ch = n % 4
        u = [cells(V, a, i, ch) for i in range(3)]
        g = [ghost(G, a, 0, layer, ch) for layer in range(2)]
        _, r_ghost = half_step(g[0], g[1], u[0], low_wanted=False)
        l0, r0 = half_step(g[1], u[0], u[1])
        l1, _ = half_step(u[0], u[1], u[2], high_wanted=False)
        f0 = contact_flux(r_ghost, l0)
        f1 = contact_flux(r0, l1)
        for c in range(5):
            D[a, c, 0, ch] = f1[c] - f0[c]
            D[a, c, 1, ch] = D[a, c, 1, ch] - f1[c]
            FC[2 * a, c, ch] = f0[c] if first else FC[2 * a, c, ch] + f0[c]
        u = [cells(V, a, i, ch) for i in (13, 14, 15)]
        g = [ghost(G, a, 1, layer, ch) for layer in range(2)]
        _, r0 = half_step(u[0], u[1], u[2], low_wanted=False)
        l1, r1 = half_step(u[1], u[2], g[0])
        l2, _ = half_step(u[2], g[0], g[1], high_wanted=False)
        f0 = contact_flux(r0, l1)
        f1 = contact_flux(r1, l2)
        for c in range(5):
            D[a, c, 14, ch] = D[a, c, 14, ch] + f0[c]
            D[a, c, 15, ch] = f1[c] - f0[c]
            FC[2 * a + 1, c, ch] = f1[c] if first else FC[2 * a + 1, c, ch] + f1[c]
        return carry

    lax.fori_loop(0, 12, body, 0)


def update(N, D):
    def body(n, carry):
        X = n // 2
        h = n % 2
        for c in range(5):
            c1, c2 = ORDER[1].index(c), ORDER[2].index(c)
            tiles = [None] * 16
            for z in range(2):
                rows = flip8([D[2, c2, 8 * z + i, 2 * h + X] for i in range(8)])
                for y in range(8):
                    tiles[2 * y + z] = D[1, c1, 8 * h + y, 2 * z + X] + rows[y]
            tiles = turn(tiles)
            for t in range(2):
                rows = flip8([D[0, c, 8 * X + i, 2 * h + t] for i in range(8)])
                for j in range(8):
                    q = 8 * t + j
                    N[q, c, X, h] = N[q, c, X, h] - RATIO * (tiles[q] + rows[j])
        return carry

    lax.fori_loop(0, 4, body, 0)


def make_views(N, V, fluid=None, perm=None):
    def body(n, carry):
        X = n // 2
        h = n % 2
        for c in range(5):
            c1, c2 = ORDER[1].index(c), ORDER[2].index(c)
            tiles = []
            for q in range(16):
                if fluid is None:
                    tiles.append(N[q, c, X, h])
                else:
                    rows = pl.ds(pl.multiple_of(8 * X, 8), 8)
                    lanes = pl.ds(pl.multiple_of(128 * h, 128), 128)
                    tiles.append(fluid[0, perm[q], c, rows, lanes])
                    N[q, c, X, h] = tiles[q]
            for t in range(2):
                rows = flip8(tiles[8 * t : 8 * t + 8])
                for i in range(8):
                    V[0, c, 8 * X + i, 2 * h + t] = rows[i]
            tiles = turn(tiles)
            for z in range(2):
                for y in range(8):
                    V[1, c1, 8 * h + y, 2 * z + X] = tiles[2 * y + z]
                rows = flip8([tiles[2 * y + z] for y in range(8)])
                for i in range(8):
                    V[2, c2, 8 * z + i, 2 * h + X] = rows[i]
        return carry

    lax.fori_loop(0, 4, body, 0)


def store_state(N, out):
    def body(q, carry):
        for c in range(5):
            for X in range(2):
                for h in range(2):
                    out[q, c, 8 * X : 8 * X + 8, 128 * h : 128 * h + 128] = N[q, c, X, h]
        return carry

    lax.fori_loop(0, 16, body, 0)


def make_slabs(V, items):
    def x_body(n, carry):
        s = n // 2
        t = n % 2
        codes = [
            [V[0, c, 14 * s + layer, 2 * h + t] for layer in range(2) for h in range(2)]
            for c in range(5)
        ]
        last = [half for tile in codes[4] for half in halves(tile)]
        for g, tiles in enumerate((codes[0] + codes[1], codes[2] + codes[3], last)):
            rows = flip8(tiles)
            for j in range(8):
                items[s * 16 + 8 * t + j, g] = rows[j]
        return carry

    def body(n, carry):
        a = 1 + n // 2
        s = n % 2
        codes = [
            [V[a, c, 14 * s + layer, k] for layer in range(2) for k in range(4)] for c in range(5)
        ]
        for g, tiles in enumerate((codes[0] + codes[1], codes[2] + codes[3], codes[4] * 2)):
            tiles = turn(tiles)
            for q in range(16):
                items[(2 + n) * 16 + q, g] = tiles[q]
        return carry

    lax.fori_loop(0, 4, x_body, 0)
    lax.fori_loop(0, 4, body, 0)


def squeeze(tiles):
    group = iota(1) // 32
    rows = flip8(tiles)
    pair = []
    for r in range(2):
        row = rows[4 * r]
        for g in range(1, 4):
            row = jnp.where(group == g, rows[4 * r + g], row)
        pair.append(row)
    return flip8(pair * 4)


def unsqueeze(tiles, second):
    rows = flip8([jnp.concatenate([tile, tile], axis=0) for tile in tiles])
    pair = [jnp.where(second, rows[2 + r], rows[r]) for r in range(2)]
    return flip8([pair[0]] * 4 + [pair[1]] * 4)


def last_tiles(tiles):
    lane = iota(1)
    result = tiles[0:4]
    for g in range(1, 4):
        result = [jnp.where(lane % 4 == g, tiles[4 * g + m], result[m]) for m in range(4)]
    return result


def make_rims(V, items):
    def x_body(n, carry):
        s = n // 2
        t = n % 2
        codes = [V[0, c, 15 * s, 2 * h + t] for c in range(5) for h in range(2)]
        rows = flip8(codes[:8])
        last = flip8(codes[8:] * 4)
        for j in range(8):
            item = s * 16 + 8 * t + j
            items[item, 0] = rows[j, 0:4]
            items[item, 1] = rows[j, 4:8]
            items[item, 2] = last[j, 0:4]
        return carry

    def body(n, carry):
        a = 1 + n // 2
        s = n % 2
        codes = [[V[a, c, 15 * s, k] for k in range(4)] for c in range(5)]
        store_rims(items, (2 + n) * 16, codes, range(16))
        return carry

    lax.fori_loop(0, 4, x_body, 0)
    lax.fori_loop(0, 4, body, 0)


def store_rims(items, first, codes, blocks):
    tiles = turn(codes[0] + codes[1] + codes[2] + codes[3])
    last = turn(codes[4] * 4)
    for t in range(2):
        pairs = squeeze(last[8 * t : 8 * t + 8])
        for j in range(8):
            q = 8 * t + j
            if q in blocks:
                items[first + q, 0] = tiles[q][0:4]
                items[first + q, 1] = tiles[q][4:8]
                items[first + q, 2] = pairs[j, 0:4]


def rim_tile(recv, e, k):
    return jnp.concatenate([recv[e, 2 * k], recv[e, 2 * k + 1]], axis=0)


def pack_slabs(items, slots, send):
    def body(d, carry):
        lane = iota(1)
        i0 = slots[2 * d]
        i1 = slots[2 * d + 1]
        for g in range(2):
            send[d, g] = items[i0, g]
            send[d, 2 + g] = items[i1, g]
        send[d, 4] = jnp.where(lane < 64, items[i0, 2], items[i1, 2])
        return carry

    lax.fori_loop(0, send.shape[0], body, 0)


def pack_rims(items, slots, send):
    def body(d, carry):
        first = lax.broadcasted_iota(jnp.int32, (4, 128), 0) < 2
        i0 = slots[2 * d]
        i1 = slots[2 * d + 1]
        for g in range(2):
            send[d, g] = items[i0, g]
            send[d, 2 + g] = items[i1, g]
        send[d, 4] = jnp.where(first, items[i0, 2], items[i1, 2])
        return carry

    lax.fori_loop(0, send.shape[0], body, 0)


def collect_slabs(recv, where, which, row_mask, lane_mask, G):
    def x_body(n, carry):
        s = n // 2
        t = n % 2
        second = row_mask[n] > 0.5
        first = s * 16 + 8 * t
        for g in range(2):
            rows = flip8([recv[where[first + j], 2 * which[first + j] + g] for j in range(8)])
            for m in range(8):
                c, layer, h = 2 * g + m // 4, m // 2 % 2, m % 2
                G[s, c, layer, 2 * h + t] = rows[m]
        rows = flip8([recv[where[first + j], 4] for j in range(8)])
        for layer in range(2):
            for h in range(2):
                m = 2 * layer + h
                G[s, 4, layer, 2 * h + t] = join(rows[2 * m], rows[2 * m + 1], second)
        return carry

    def body(n, carry):
        second = lane_mask[n] > 0.5
        first = (2 + n) * 16
        for g in range(2):
            tiles = turn([recv[where[first + q], 2 * which[first + q] + g] for q in range(16)])
            for m in range(16):
                G[2 + n, 2 * g + m // 8, m // 4 % 2, m % 4] = tiles[m]
        tiles = turn([recv[where[first + q], 4] for q in range(16)])
        for m in range(8):
            G[2 + n, 4, m // 4, m % 4] = jnp.where(second, tiles[8 + m], tiles[m])
        return carry

    lax.fori_loop(0, 4, x_body, 0)
    lax.fori_loop(0, 4, body, 0)


def early_rims(G, rims):
    face = iota(1) // 8 % 8

    def body(c, carry):
        for k in range(4):
            tile = G[2, c, 1, k]
            for n in range(1, 4):
                tile = jnp.where(face == n, pltpu.roll(G[2 + n, c, 1 - n % 2, k], 8 * n, 1), tile)
            rims[4 * c + k] = tile
        for f in range(2):
            for t in range(2):
                for h in range(2):
                    r = 4 * f + 2 * t + h
                    rims[20 + c, r : r + 1, :] = G[f, c, 1 - f, 2 * h + t, 0:1, :]
        return carry

    lax.fori_loop(0, 5, body, 0)


def late_rims(recv, where, which, row_mask, rims):
    for f in range(2):
        for t in range(2):
            item = f * 16 + 8 * t
            r = 4 * f + 2 * t
            tile = rim_tile(recv, where[item], which[item])
            for c in range(4):
                rims[20 + c, r : r + 2, :] = tile[2 * c : 2 * c + 2]
            tile = recv[where[item], 4]
            rims[24, r : r + 2, :] = jnp.where(which[item] == 1, tile[2:4], tile[0:2])
    items = [f * 16 + 8 * t for t in range(2) for _ in range(2) for f in range(2, 6)]
    tiles = turn([rim_tile(recv, where[i], which[i]) for i in items])
    for m in range(16):
        rims[m] = tiles[m]
    tiles = []
    for t in range(2):
        rows = unsqueeze(
            [recv[where[i], 4] for i in items[8 * t : 8 * t + 8]], row_mask[12 + t] > 0.5
        )
        tiles += [rows[j] for j in range(8)]
    tiles = last_tiles(turn(tiles))
    for m in range(4):
        rims[16 + m] = tiles[m]


def spread_rows(tile, u):
    sub = iota(0)
    result = pltpu.roll(tile, 4, 0) if u else tile
    base = result
    for r in range(1, 5):
        result = jnp.where((sub + 1) // 2 == r, pltpu.roll(base, r, 0), result)
    return result


def sibling_ghosts(V, G):
    def x_body(c, carry):
        for f in range(2):
            for layer in range(2):
                for k in range(4):
                    near = V[0, c, (layer if f else 14 + layer), k]
                    G[f, c, layer, k] = pltpu.roll(near, 4, 0)
        return carry

    def body(c, carry):
        for f in range(2, 6):
            a, s = f // 2, f % 2
            by = (128 - 8 * BIT_OF[a]) if s else 8 * BIT_OF[a]
            for layer in range(2):
                for k in range(4):
                    near = V[a, c, (layer if s else 14 + layer), k]
                    G[f, c, layer, k] = pltpu.roll(near, by, 1)
        return carry

    lax.fori_loop(0, 5, x_body, 0)
    lax.fori_loop(0, 5, body, 0)


def coarse_ghosts(rims, G, late=None):
    lane = iota(1)
    sub = iota(0)

    def rim(*index):
        value = rims[index]
        return value if late is None else 0.5 * (value + late[index])

    def x_body(c, carry):
        first = (sub // 2) % 2 == 1
        second = sub % 2
        for f in range(2):
            outer = (sub // 4) % 2 == f
            for t in range(2):
                r = 4 * f + 2 * t
                row = [
                    jnp.broadcast_to(rim(20 + c, pl.ds(r + h, 1), slice(None)), (8, 128))
                    for h in range(2)
                ]
                source = jnp.where(first, row[1], row[0])
                for h in range(2):
                    index = (4 * h + lane // 32) * 16 + 8 * second + (lane % 16) // 2
                    coarse = take(source, index)
                    for layer in range(2):
                        k = 2 * h + t
                        G[f, c, layer, k] = jnp.where(outer, coarse, G[f, c, layer, k])
        return carry

    octant = lane // 8 % 8

    def body(c, carry):
        source = [rim(4 * c + k) for k in range(4)]
        second = octant // 4 == 1
        for f in range(2, 6):
            a, s = f // 2, f % 2
            outer = octant // BIT_OF[a] % 2 == s
            first = octant // TANGENT[a][0] % 2 == 1
            for X in range(2):
                index = (lane // 64 * 8 + f - 2) * 8 + 4 * X + lane % 8 // 2
                four = [take(tile, index) for tile in source]
                low = jnp.where(second, four[1], four[0])
                high = jnp.where(second, four[3], four[2])
                chosen = jnp.where(first, high, low)
                for u in range(2):
                    coarse = spread_rows(chosen, u)
                    for layer in range(2):
                        k = 2 * u + X
                        G[f, c, layer, k] = jnp.where(outer, coarse, G[f, c, layer, k])
        return carry

    lax.fori_loop(0, 5, x_body, 0)
    lax.fori_loop(0, 5, body, 0)


def pair_sums(low, high):
    lane = iota(1)
    index = (lane // 16 % 4) * 32 + 2 * (lane % 8)
    sums = []
    for tile in (low, high):
        tile = tile + pltpu.roll(tile, 127, 1)
        sums.append(take(tile + pltpu.roll(tile, 112, 1), index))
    merged = jnp.where(lane < 64, sums[0], sums[1])
    return jnp.where(lane % 16 < 8, merged, pltpu.roll(merged, 7, 0))


def restrict_cells(N, mixed):
    def body(n, carry):
        t = n % 2
        c = n // 2
        merged = []
        for X in range(2):
            rows = [flip8([N[8 * t + j, c, X, h] for j in range(8)]) for h in range(2)]
            for x in range(4):
                low, high = [rows[h][2 * x] + rows[h][2 * x + 1] for h in range(2)]
                merged.append(pair_sums(low, high) * 0.125)
        rows = flip8(merged)
        for X in range(2):
            for h in range(2):
                mixed[t, c, X, h] = rows[4 * X + 2 * h]
        return carry

    lax.fori_loop(0, 10, body, 0)


def restrict_faces(FC, means):
    lane = iota(1)
    sub = iota(0)

    def x_body(c, carry):
        for f in range(2):
            for t in range(2):
                merged = pair_sums(FC[f, c, t], FC[f, c, 2 + t]) * 0.125
                for h in range(2):
                    o = 4 * f + 2 * h
                    r = 4 * f + 2 * t + h
                    means[20 + c, r : r + 1, :] = merged[o : o + 1]
        return carry

    def body(c, carry):
        index = lane // 8 * 8 + 2 * (lane % 4)
        for n in range(4):
            result = None
            for u in range(2):
                sums = []
                for X in range(2):
                    tile = FC[2 + n, c, 2 * u + X]
                    tile = tile + pltpu.roll(tile, 127, 1)
                    sums.append(take(tile + pltpu.roll(tile, 7, 0), index))
                merged = jnp.where(lane % 8 < 4, sums[0], sums[1])
                for i in range(4):
                    moved = pltpu.roll(merged, (8 - i) % 8, 0) if u == 0 else pltpu.roll(merged, 4 - i, 0)
                    if result is None:
                        result = moved
                    else:
                        result = jnp.where(sub == 4 * u + i, moved, result)
            means[5 * n + c] = result * 0.125
        return carry

    lax.fori_loop(0, 5, x_body, 0)
    lax.fori_loop(0, 5, body, 0)


def make_deltas(FC, means, items):
    for f in range(2):
        for t in range(2):
            item = f * 16 + 8 * t
            for c in range(5):
                for h in range(2):
                    r = 4 * f + 2 * t + h
                    delta = FC[f, c, 2 * h + t, 0:1, :] - means[20 + c, r : r + 1, :]
                    if c < 4:
                        row = 2 * (c % 2) + h
                        items[item, c // 2, row : row + 1, :] = delta
                    else:
                        items[item, 2, h : h + 1, :] = delta
                        items[item, 2, 2 + h : 3 + h, :] = delta
    for n in range(4):
        a, s = 1 + n // 2, n % 2
        codes = []
        for c in range(5):
            fine = means[5 * n + c]
            codes.append([])
            for k in range(4):
                o = s * BIT_OF[a] + (k // 2) * TANGENT[a][0] + (k % 2) * 4
                moved = pltpu.roll(fine, (128 - 8 * o) % 128, 1)
                codes[c].append(FC[2 + n, c, k] - moved)
        store_rims(items, (2 + n) * 16, codes, (0, 8))


def take_mixed(N, mixed):
    def body(c, carry):
        for t in range(2):
            for X in range(2):
                for h in range(2):
                    N[8 * t, c, X, h] = mixed[t, c, X, h]
        return carry

    lax.fori_loop(0, 5, body, 0)


def apply_corrections(recv, where, which, row_mask, change, N):
    sub = iota(0)

    def x_body(q, carry):
        for s in range(2):
            scale = RATIO if s else -RATIO
            item = s * 16 + q
            e = where[item]
            k = which[item]
            tile = recv[e, 4]
            last = jnp.where(k == 1, tile[2:4], tile[0:2])
            tile = rim_tile(recv, e, k)
            for c in range(5):
                for h in range(2):
                    row = tile[2 * c + h : 2 * c + h + 1] if c < 4 else last[h : h + 1]
                    row = jnp.broadcast_to(scale * row, (8, 128))
                    N[q, c, s, h] = N[q, c, s, h] + jnp.where(sub == 7 * s, row, 0.0)
        return carry

    lax.fori_loop(0, 16, x_body, 0)

    for n in range(4):
        scale = RATIO if n % 2 else -RATIO
        first = (2 + n) * 16
        tiles = turn([rim_tile(recv, where[first + q], which[first + q]) for q in range(16)])
        for m in range(16):
            change[n, m // 4, m % 4] = scale * tiles[m]
        tiles = []
        for t in range(2):
            rows = unsqueeze(
                [recv[where[first + 8 * t + j], 4] for j in range(8)],
                row_mask[4 + 2 * n + t] > 0.5,
            )
            tiles += [rows[j] for j in range(8)]
        tiles = last_tiles(turn(tiles))
        for m in range(4):
            change[n, 4, m] = scale * tiles[m]

    def body(X, carry):
        for c in range(5):
            c1, c2 = ORDER[1].index(c), ORDER[2].index(c)
            for h in range(2):
                tiles = []
                for y in range(8):
                    for z in range(2):
                        row = jnp.broadcast_to(
                            change[2 + z, c2, 2 * h + X, y : y + 1, :], (8, 128)
                        )
                        tile = jnp.where(sub == 7 * z, row, 0.0)
                        if y == 7 * h:
                            tile = tile + change[h, c1, 2 * z + X]
                        tiles.append(tile)
                tiles = turn(tiles)
                for q in range(16):
                    N[q, c, X, h] = N[q, c, X, h] + tiles[q]
        return carry

    lax.fori_loop(0, 2, body, 0)


def step_kernel(
    devices,
    perm,
    slots,
    where,
    which,
    fluid_hbm,
    row_mask,
    lane_mask,
    out,
    N,
    V,
    D,
    G,
    FC,
    change,
    items1,
    items2,
    items3,
    send1,
    recv1,
    send2,
    recv2,
    send3,
    recv3,
    early_out,
    early_in,
    late_out,
    late_in,
    mixed_out,
    mixed_in,
    means_out,
    means_in,
    send_sems,
    recv_sems,
    pair_send,
    pair_recv,
    ready,
    fluid,
    load_sem,
):
    level = lax.axis_index("level")
    me = lax.axis_index("blk")
    other = 1 - level
    barrier = pltpu.get_barrier_semaphore()

    def start_all(send, recv, n):
        for dz, dx, dy in send_order():
            d = dz * 16 + dx * 4 + dy - 1
            pltpu.make_async_remote_copy(
                src_ref=send.at[d],
                dst_ref=recv.at[d],
                send_sem=send_sems.at[n],
                recv_sem=recv_sems.at[n],
                device_id=(level, far[dz] + mid[dx] + near[dy]),
                device_id_type=MESH,
            ).start()

    def whole(send, recv, n):
        return pltpu.make_async_remote_copy(
            src_ref=send,
            dst_ref=recv,
            send_sem=send_sems.at[n],
            recv_sem=recv_sems.at[n],
            device_id=(level, lax.rem(me + 1, devices)),
            device_id_type=MESH,
        )

    def to_pair(source, target, n):
        return pltpu.make_async_remote_copy(
            src_ref=source,
            dst_ref=target,
            send_sem=pair_send.at[n],
            recv_sem=pair_recv.at[n],
            device_id=(other, me),
            device_id_type=MESH,
        )

    def greet(semaphore, peers):
        for peer in peers:
            pl.semaphore_signal(
                semaphore, inc=1, device_id=(level, peer), device_id_type=MESH
            )

    far = [lax.rem(me // 16 + i, 8) * 16 for i in range(8)]
    mid = [lax.rem(me // 4 % 4 + i, 4) * 4 for i in range(4)]
    near = [lax.rem(me % 4 + i, 4) for i in range(4)]
    line = [far[i] + mid[0] + near[0] for i in range(1, 8)]
    plane = [far[0] + mid[i] + near[j] for i in range(4) for j in range(4) if i or j]

    pl.semaphore_signal(barrier, inc=1, device_id=(other, me), device_id_type=MESH)

    @pl.when(level == 0)
    def _():
        greet(barrier, line + plane)

    copy = pltpu.make_async_copy(fluid_hbm, fluid, load_sem)
    copy.start()
    copy.wait()
    make_views(N, V, fluid, perm)

    @pl.when(level == 0)
    def _():
        pl.semaphore_wait(barrier, 23)
        greet(ready, line)
        make_slabs(V, items1)
        pack_slabs(items1, slots, send1)
        pl.semaphore_wait(ready, 7)
        start_all(send1, recv1, 0)

        def clear(n, carry):
            for g in range(3):
                items3[n, g] = jnp.zeros((4, 128), F32)
            return carry

        lax.fori_loop(0, 96, clear, 0)

    @pl.when(level == 1)
    def _():
        pl.semaphore_wait(barrier, 1)

    inner_sweep(V, D)

    @pl.when(level == 0)
    def _():
        whole(send1, recv1, 0).wait_recv()
        collect_slabs(recv1, where, which, row_mask, lane_mask, G)
        early_rims(G, early_out)
        to_pair(early_out, early_in, 0).start()

    @pl.when(level == 1)
    def _():
        sibling_ghosts(V, G)
        to_pair(early_out, early_in, 0).wait_recv()
        coarse_ghosts(early_in, G)

    outer_sweep(V, G, D, FC, True)
    update(N, D)
    make_views(N, V)

    @pl.when(level == 0)
    def _():
        make_rims(V, items2)
        pack_rims(items2, slots, send2)
        start_all(send2, recv2, 1)
        whole(send2, recv2, 1).wait_recv()
        late_rims(recv2, where, which, row_mask, late_out)
        to_pair(late_out, late_in, 1).start()

        to_pair(means_out, means_in, 3).wait_recv()
        make_deltas(FC, means_in, items3)
        pack_rims(items3, slots, send3)
        start_all(send3, recv3, 2)
        to_pair(mixed_out, mixed_in, 2).wait_recv()
        take_mixed(N, mixed_in)
        whole(send3, recv3, 2).wait_recv()
        apply_corrections(recv3, where, which, row_mask, change, N)

    @pl.when(level == 1)
    def _():
        inner_sweep(V, D)
        sibling_ghosts(V, G)
        to_pair(late_out, late_in, 1).wait_recv()
        coarse_ghosts(early_in, G, late_in)
        outer_sweep(V, G, D, FC, False)
        restrict_faces(FC, means_out)
        to_pair(means_out, means_in, 3).start()
        update(N, D)
        restrict_cells(N, mixed_out)
        to_pair(mixed_out, mixed_in, 2).start()

    store_state(N, out)

    @pl.when(level == 0)
    def _():
        whole(send1, recv1, 0).wait_send()
        whole(send2, recv2, 1).wait_send()
        whole(send3, recv3, 2).wait_send()
        to_pair(early_out, early_in, 0).wait_send()
        to_pair(late_out, late_in, 1).wait_send()

    @pl.when(level == 1)
    def _():
        to_pair(mixed_out, mixed_in, 2).wait_send()
        to_pair(means_out, means_in, 3).wait_send()


def place_kernel(back, source, out):
    def body(b, carry):
        out[0, b] = source[back[b]]
        return carry

    lax.fori_loop(0, out.shape[1], body, 0)


def tables(neighbours, parents, level, me, count, devices):
    rows = lax.dynamic_slice_in_dim(neighbours, me * count, count, 0)
    family = lax.dynamic_slice_in_dim(parents, me * count, count, 0)
    ids = jnp.arange(count, dtype=jnp.int32)
    owner = family[:, 0] - me * count
    owns = owner[:, None] == ids[None, :]
    is_parent = jnp.any(owns, axis=0)
    earlier = ids[None, :] < ids[:, None]
    parent_rank = jnp.sum(is_parent[None, :] & earlier, axis=1, dtype=jnp.int32)
    rest_rank = ids - parent_rank
    coarse_place = jnp.where(
        is_parent, 8 * parent_rank, jnp.where(rest_rank < 7, 1 + rest_rank, 2 + rest_rank)
    )
    fine_place = 8 * jnp.sum(jnp.where(owns, parent_rank[None, :], 0), axis=1) + family[:, 1]
    place = jnp.where(level == 0, coarse_place, fine_place).astype(jnp.int32)

    def inverse(position):
        return jnp.sum(
            jnp.where(position[None, :] == ids[:, None], ids[None, :], 0), axis=1, dtype=jnp.int32
        )

    coarse_perm = inverse(coarse_place)
    chosen = coarse_perm[:, None] == ids[None, :]
    ordered = jnp.sum(jnp.where(chosen[:, :, None], rows[None], 0), axis=1, dtype=jnp.int32)
    ordered = ordered.T.reshape(-1)
    faces = jnp.repeat(jnp.arange(6, dtype=jnp.int32), count)
    target = ordered // count
    own_id = jnp.tile(coarse_perm, 6) * 6 + faces
    their_id = ordered % count * 6 + faces + 1 - 2 * (faces % 2)
    key = jnp.where(me < target, own_id, their_id)
    which = jnp.sum(
        (target[:, None] == target[None, :]) & (key[None, :] < key[:, None]),
        axis=1,
        dtype=jnp.int32,
    )
    far, mid, near = target // 16 - me // 16, target // 4 % 4 - me // 4 % 4, target % 4 - me % 4
    to = (far % 8) * 16 + (mid % 4) * 4 + near % 4 - 1
    come = (-far % 8) * 16 + (-mid % 4) * 4 + (-near) % 4 - 1
    item_ids = jnp.arange(6 * count, dtype=jnp.int32)
    slot_ids = jnp.arange(2 * devices, dtype=jnp.int32)
    slots = jnp.sum(
        jnp.where((2 * to + which)[None, :] == slot_ids[:, None], item_ids[None, :], 0),
        axis=1,
        dtype=jnp.int32,
    )
    second = which.astype(F32).reshape(6, count)
    late = jnp.stack([second[2:, 0], second[2:, 0], second[2:, 8], second[2:, 8]])
    rows = jnp.concatenate([second.reshape(12, 8), late.reshape(2, 8)])
    row_mask = jnp.broadcast_to(rows[:, :, None], (14, 8, 128))
    lane_mask = jnp.broadcast_to(jnp.repeat(second[2:], 8, axis=1)[:, None, :], (4, 8, 128))
    return inverse(place), place, slots, come, which, row_mask, lane_mask


def local(fluid_state, neighbours, parents):
    level = lax.axis_index("level")
    me = lax.axis_index("blk")
    devices = lax.axis_size("blk")
    count = fluid_state.shape[1]
    perm, place, slots, where, which, row_mask, lane_mask = tables(
        neighbours, parents, level, me, count, devices
    )
    smem = pl.BlockSpec(memory_space=pltpu.SMEM)
    vmem = pl.BlockSpec(memory_space=pltpu.VMEM)
    peers = devices - 1

    def step(*refs):
        step_kernel(devices, *refs)

    result = pl.pallas_call(
        step,
        out_shape=jax.ShapeDtypeStruct(fluid_state.shape[1:], F32),
        in_specs=[smem] * 4 + [pl.BlockSpec(memory_space=pl.ANY)] + [vmem] * 2,
        out_specs=vmem,
        scratch_shapes=[
            pltpu.VMEM((16, 5, 2, 2, 8, 128), F32),
            pltpu.VMEM((3, 5, 16, 4, 8, 128), F32),
            pltpu.VMEM((3, 5, 16, 4, 8, 128), F32),
            pltpu.VMEM((6, 5, 2, 4, 8, 128), F32),
            pltpu.VMEM((6, 5, 4, 8, 128), F32),
            pltpu.VMEM((4, 5, 4, 8, 128), F32),
            pltpu.VMEM((96, 3, 8, 128), F32),
            pltpu.VMEM((96, 3, 4, 128), F32),
            pltpu.VMEM((96, 3, 4, 128), F32),
            pltpu.VMEM((peers, 5, 8, 128), F32),
            pltpu.VMEM((peers, 5, 8, 128), F32),
            pltpu.VMEM((peers, 5, 4, 128), F32),
            pltpu.VMEM((peers, 5, 4, 128), F32),
            pltpu.VMEM((peers, 5, 4, 128), F32),
            pltpu.VMEM((peers, 5, 4, 128), F32),
            pltpu.VMEM((25, 8, 128), F32),
            pltpu.VMEM((25, 8, 128), F32),
            pltpu.VMEM((25, 8, 128), F32),
            pltpu.VMEM((25, 8, 128), F32),
            pltpu.VMEM((2, 5, 2, 2, 8, 128), F32),
            pltpu.VMEM((2, 5, 2, 2, 8, 128), F32),
            pltpu.VMEM((25, 8, 128), F32),
            pltpu.VMEM((25, 8, 128), F32),
            pltpu.SemaphoreType.DMA((3,)),
            pltpu.SemaphoreType.DMA((3,)),
            pltpu.SemaphoreType.DMA((4,)),
            pltpu.SemaphoreType.DMA((4,)),
            pltpu.SemaphoreType.REGULAR,
            pltpu.VMEM(fluid_state.shape, F32),
            pltpu.SemaphoreType.DMA,
        ],
        compiler_params=pltpu.CompilerParams(
            collective_id=0, has_side_effects=True, vmem_limit_bytes=60 * 1024 * 1024
        ),
    )(perm, slots, where, which, fluid_state, row_mask, lane_mask)
    return pl.pallas_call(
        place_kernel,
        out_shape=jax.ShapeDtypeStruct(fluid_state.shape, F32),
        in_specs=[smem, vmem],
        out_specs=vmem,
    )(place, result)


def solution(mesh):
    return jax.shard_map(
        local,
        mesh=mesh,
        in_specs=(P("level", "blk", None, None, None), P(), P()),
        out_specs=P("level", "blk", None, None, None),
        check_vma=False,
    )
```

```python
import jax
import jax.numpy as jnp
from jax import lax
from jax.experimental import pallas as pl
from jax.experimental.pallas import tpu as pltpu
from jax.sharding import PartitionSpec as P

GAMMA = 1.4
RATIO = 0.12
MESH = pl.DeviceIdType.MESH
ORDER = ((0, 1, 2, 3, 4), (0, 2, 1, 3, 4), (0, 3, 1, 2, 4))
BIT_OF = (4, 2, 1)
TANGENT = ((2, 1), (1, 4), (2, 4))
F32 = jnp.float32


def send_order():
    offsets = [(z, x, y) for z in range(8) for x in range(4) for y in range(4)][1:]
    mixed = [offsets[(53 * k + 26) % 127] for k in range(127)]
    return sorted(mixed, key=lambda o: -(min(o[0], 8 - o[0]) + min(o[1], 4 - o[1]) + min(o[2], 4 - o[2])))


def iota(axis):
    return lax.broadcasted_iota(jnp.int32, (8, 128), axis)


def take(tile, index):
    return jnp.take_along_axis(tile, index, axis=1, mode="promise_in_bounds")


def flip8(tiles):
    return jnp.swapaxes(jnp.stack(tiles), 0, 1)


def turn(tiles):
    whole = jnp.concatenate(tiles, axis=0).T
    return [whole[8 * i : 8 * i + 8] for i in range(16)]


def halves(tile):
    lane = iota(1)
    other = pltpu.roll(tile, 64, 1)
    return jnp.where(lane < 64, tile, other), jnp.where(lane < 64, other, tile)


def join(low, high, second):
    lane = iota(1)
    low = jnp.where(second, pltpu.roll(low, 64, 1), low)
    high = jnp.where(second, high, pltpu.roll(high, 64, 1))
    return jnp.where(lane < 64, low, high)


def prim(q):
    inverse = 1.0 / q[0]
    speed = q[1] * inverse
    kinetic = (q[1] * q[1] + q[2] * q[2] + q[3] * q[3]) * inverse
    return inverse, speed, (GAMMA - 1.0) * (q[4] - 0.5 * kinetic)


def flux_of(q, speed, pressure):
    return [q[1], q[1] * speed + pressure, q[2] * speed, q[3] * speed, (q[4] + pressure) * speed]


def half_step(below, here, above, low_wanted=True, high_wanted=True):
    low, high = [], []
    for u0, u1, u2 in zip(below, here, above):
        a = u1 - u0
        b = u2 - u1
        slope = jnp.maximum(jnp.minimum(a, b), 0.0) + jnp.minimum(jnp.maximum(a, b), 0.0)
        low.append(u1 - 0.5 * slope)
        high.append(u1 + 0.5 * slope)
    _, speed, pressure = prim(low)
    flux_low = flux_of(low, speed, pressure)
    _, speed, pressure = prim(high)
    flux_high = flux_of(high, speed, pressure)
    change = [0.5 * RATIO * (a - b) for a, b in zip(flux_low, flux_high)]
    low = [a + b for a, b in zip(low, change)] if low_wanted else None
    high = [a + b for a, b in zip(high, change)] if high_wanted else None
    return low, high


def with_sound(q):
    inverse, speed, pressure = prim(q)
    return q, inverse, speed, pressure, jnp.sqrt(GAMMA * pressure * inverse)


def contact_flux(low, high):
    ql, il, ul, pl_, cl = with_sound(low)
    qh, ih, uh, ph, ch = with_sound(high)
    slowest = jnp.minimum(ul - cl, uh - ch)
    fastest = jnp.maximum(ul + cl, uh + ch)
    mass_l = ql[0] * (slowest - ul)
    mass_h = qh[0] * (fastest - uh)
    contact = (ph - pl_ + ul * mass_l - uh * mass_h) / (mass_l - mass_h)
    lower = jnp.logical_or(slowest >= 0.0, contact >= 0.0)
    q = [jnp.where(lower, a, b) for a, b in zip(ql, qh)]
    inverse = jnp.where(lower, il, ih)
    speed = jnp.where(lower, ul, uh)
    pressure = jnp.where(lower, pl_, ph)
    mass = jnp.where(lower, mass_l, mass_h)
    wave = jnp.where(lower, slowest, fastest)
    outside = jnp.logical_or(slowest >= 0.0, jnp.logical_and(contact < 0.0, fastest <= 0.0))
    flux = flux_of(q, speed, pressure)
    over = 1.0 / (wave - contact)
    factor = mass * over
    scaled = factor * inverse
    gap = contact - speed
    star = [
        factor,
        factor * contact,
        scaled * q[2],
        scaled * q[3],
        scaled * q[4] + gap * (factor * contact + pressure * over),
    ]
    return [jnp.where(outside, f, f + wave * (s - u)) for f, s, u in zip(flux, star, q)]


def cells(V, a, i, ch):
    return [V[a, c, i, ch] for c in range(5)]


def ghost(G, a, s, layer, ch):
    return [G[2 * a + s, c, layer, ch] for c in range(5)]


def inner_sweep(V, D):
    def body(n, carry):
        a = n // 4
        ch = n % 4
        states = [cells(V, a, i, ch) for i in range(3)]
        _, high = half_step(*states)
        previous = None
        for i in range(2, 15):
            states = [states[1], states[2], cells(V, a, i + 1, ch)]
            low, next_high = half_step(*states)
            flux = contact_flux(high, low)
            for c in range(5):
                D[a, c, i - 1, ch] = flux[c] if previous is None else flux[c] - previous[c]
            high, previous = next_high, flux
        for c in range(5):
            D[a, c, 14, ch] = -previous[c]
        return carry

    lax.fori_loop(0, 12, body, 0)


def outer_sweep(V, G, D, FC, first):
    def body(n, carry):
        a = n // 4
        ch = n % 4
        u = [cells(V, a, i, ch) for i in range(3)]
        g = [ghost(G, a, 0, layer, ch) for layer in range(2)]
        _, r_ghost = half_step(g[0], g[1], u[0], low_wanted=False)
        l0, r0 = half_step(g[1], u[0], u[1])
        l1, _ = half_step(u[0], u[1], u[2], high_wanted=False)
        f0 = contact_flux(r_ghost, l0)
        f1 = contact_flux(r0, l1)
        for c in range(5):
            D[a, c, 0, ch] = f1[c] - f0[c]
            D[a, c, 1, ch] = D[a, c, 1, ch] - f1[c]
            FC[2 * a, c, ch] = f0[c] if first else FC[2 * a, c, ch] + f0[c]
        u = [cells(V, a, i, ch) for i in (13, 14, 15)]
        g = [ghost(G, a, 1, layer, ch) for layer in range(2)]
        _, r0 = half_step(u[0], u[1], u[2], low_wanted=False)
        l1, r1 = half_step(u[1], u[2], g[0])
        l2, _ = half_step(u[2], g[0], g[1], high_wanted=False)
        f0 = contact_flux(r0, l1)
        f1 = contact_flux(r1, l2)
        for c in range(5):
            D[a, c, 14, ch] = D[a, c, 14, ch] + f0[c]
            D[a, c, 15, ch] = f1[c] - f0[c]
            FC[2 * a + 1, c, ch] = f1[c] if first else FC[2 * a + 1, c, ch] + f1[c]
        return carry

    lax.fori_loop(0, 12, body, 0)


def update(N, D):
    def body(n, carry):
        X = n // 2
        h = n % 2
        for c in range(5):
            c1, c2 = ORDER[1].index(c), ORDER[2].index(c)
            tiles = [None] * 16
            for z in range(2):
                rows = flip8([D[2, c2, 8 * z + i, 2 * h + X] for i in range(8)])
                for y in range(8):
                    tiles[2 * y + z] = D[1, c1, 8 * h + y, 2 * z + X] + rows[y]
            tiles = turn(tiles)
            for t in range(2):
                rows = flip8([D[0, c, 8 * X + i, 2 * h + t] for i in range(8)])
                for j in range(8):
                    q = 8 * t + j
                    N[q, c, X, h] = N[q, c, X, h] - RATIO * (tiles[q] + rows[j])
        return carry

    lax.fori_loop(0, 4, body, 0)


def make_views(N, V, fluid=None, perm=None):
    def body(n, carry):
        X = n // 2
        h = n % 2
        for c in range(5):
            c1, c2 = ORDER[1].index(c), ORDER[2].index(c)
            tiles = []
            for q in range(16):
                if fluid is None:
                    tiles.append(N[q, c, X, h])
                else:
                    rows = pl.ds(pl.multiple_of(8 * X, 8), 8)
                    lanes = pl.ds(pl.multiple_of(128 * h, 128), 128)
                    tiles.append(fluid[0, perm[q], c, rows, lanes])
                    N[q, c, X, h] = tiles[q]
            for t in range(2):
                rows = flip8(tiles[8 * t : 8 * t + 8])
                for i in range(8):
                    V[0, c, 8 * X + i, 2 * h + t] = rows[i]
            tiles = turn(tiles)
            for z in range(2):
                for y in range(8):
                    V[1, c1, 8 * h + y, 2 * z + X] = tiles[2 * y + z]
                rows = flip8([tiles[2 * y + z] for y in range(8)])
                for i in range(8):
                    V[2, c2, 8 * z + i, 2 * h + X] = rows[i]
        return carry

    lax.fori_loop(0, 4, body, 0)


def store_state(N, out):
    def body(q, carry):
        for c in range(5):
            for X in range(2):
                for h in range(2):
                    out[q, c, 8 * X : 8 * X + 8, 128 * h : 128 * h + 128] = N[q, c, X, h]
        return carry

    lax.fori_loop(0, 16, body, 0)


def make_slabs(V, items):
    def x_body(n, carry):
        s = n // 2
        t = n % 2
        codes = [
            [V[0, c, 14 * s + layer, 2 * h + t] for layer in range(2) for h in range(2)]
            for c in range(5)
        ]
        last = [half for tile in codes[4] for half in halves(tile)]
        for g, tiles in enumerate((codes[0] + codes[1], codes[2] + codes[3], last)):
            rows = flip8(tiles)
            for j in range(8):
                items[s * 16 + 8 * t + j, g] = rows[j]
        return carry

    def body(n, carry):
        a = 1 + n // 2
        s = n % 2
        codes = [
            [V[a, c, 14 * s + layer, k] for layer in range(2) for k in range(4)] for c in range(5)
        ]
        for g, tiles in enumerate((codes[0] + codes[1], codes[2] + codes[3], codes[4] * 2)):
            tiles = turn(tiles)
            for q in range(16):
                items[(2 + n) * 16 + q, g] = tiles[q]
        return carry

    lax.fori_loop(0, 4, x_body, 0)
    lax.fori_loop(0, 4, body, 0)


def squeeze(tiles):
    group = iota(1) // 32
    rows = flip8(tiles)
    pair = []
    for r in range(2):
        row = rows[4 * r]
        for g in range(1, 4):
            row = jnp.where(group == g, rows[4 * r + g], row)
        pair.append(row)
    return flip8(pair * 4)


def unsqueeze(tiles, second):
    rows = flip8([jnp.concatenate([tile, tile], axis=0) for tile in tiles])
    pair = [jnp.where(second, rows[2 + r], rows[r]) for r in range(2)]
    return flip8([pair[0]] * 4 + [pair[1]] * 4)


def last_tiles(tiles):
    lane = iota(1)
    result = tiles[0:4]
    for g in range(1, 4):
        result = [jnp.where(lane % 4 == g, tiles[4 * g + m], result[m]) for m in range(4)]
    return result


def make_rims(V, items):
    def x_body(n, carry):
        s = n // 2
        t = n % 2
        codes = [V[0, c, 15 * s, 2 * h + t] for c in range(5) for h in range(2)]
        rows = flip8(codes[:8])
        last = flip8(codes[8:] * 4)
        for j in range(8):
            item = s * 16 + 8 * t + j
            items[item, 0] = rows[j, 0:4]
            items[item, 1] = rows[j, 4:8]
            items[item, 2] = last[j, 0:4]
        return carry

    def body(n, carry):
        a = 1 + n // 2
        s = n % 2
        codes = [[V[a, c, 15 * s, k] for k in range(4)] for c in range(5)]
        store_rims(items, (2 + n) * 16, codes, range(16))
        return carry

    lax.fori_loop(0, 4, x_body, 0)
    lax.fori_loop(0, 4, body, 0)


def store_rims(items, first, codes, blocks):
    tiles = turn(codes[0] + codes[1] + codes[2] + codes[3])
    last = turn(codes[4] * 4)
    for t in range(2):
        pairs = squeeze(last[8 * t : 8 * t + 8])
        for j in range(8):
            q = 8 * t + j
            if q in blocks:
                items[first + q, 0] = tiles[q][0:4]
                items[first + q, 1] = tiles[q][4:8]
                items[first + q, 2] = pairs[j, 0:4]


def rim_tile(recv, e, k):
    return jnp.concatenate([recv[e, 2 * k], recv[e, 2 * k + 1]], axis=0)


def pack_slabs(items, slots, send):
    def body(d, carry):
        lane = iota(1)
        i0 = slots[2 * d]
        i1 = slots[2 * d + 1]
        for g in range(2):
            send[d, g] = items[i0, g]
            send[d, 2 + g] = items[i1, g]
        send[d, 4] = jnp.where(lane < 64, items[i0, 2], items[i1, 2])
        return carry

    lax.fori_loop(0, send.shape[0], body, 0)


def pack_rims(items, slots, send):
    def body(d, carry):
        first = lax.broadcasted_iota(jnp.int32, (4, 128), 0) < 2
        i0 = slots[2 * d]
        i1 = slots[2 * d + 1]
        for g in range(2):
            send[d, g] = items[i0, g]
            send[d, 2 + g] = items[i1, g]
        send[d, 4] = jnp.where(first, items[i0, 2], items[i1, 2])
        return carry

    lax.fori_loop(0, send.shape[0], body, 0)


def collect_slabs(recv, where, which, row_mask, lane_mask, G):
    def x_body(n, carry):
        s = n // 2
        t = n % 2
        second = row_mask[n] > 0.5
        first = s * 16 + 8 * t
        for g in range(2):
            rows = flip8([recv[where[first + j], 2 * which[first + j] + g] for j in range(8)])
            for m in range(8):
                c, layer, h = 2 * g + m // 4, m // 2 % 2, m % 2
                G[s, c, layer, 2 * h + t] = rows[m]
        rows = flip8([recv[where[first + j], 4] for j in range(8)])
        for layer in range(2):
            for h in range(2):
                m = 2 * layer + h
                G[s, 4, layer, 2 * h + t] = join(rows[2 * m], rows[2 * m + 1], second)
        return carry

    def body(n, carry):
        second = lane_mask[n] > 0.5
        first = (2 + n) * 16
        for g in range(2):
            tiles = turn([recv[where[first + q], 2 * which[first + q] + g] for q in range(16)])
            for m in range(16):
                G[2 + n, 2 * g + m // 8, m // 4 % 2, m % 4] = tiles[m]
        tiles = turn([recv[where[first + q], 4] for q in range(16)])
        for m in range(8):
            G[2 + n, 4, m // 4, m % 4] = jnp.where(second, tiles[8 + m], tiles[m])
        return carry

    lax.fori_loop(0, 4, x_body, 0)
    lax.fori_loop(0, 4, body, 0)


def parent_layers(read, out):
    face = iota(1) // 8 % 8

    def body(c, carry):
        for k in range(4):
            tile = read(2, c, k)
            for n in range(1, 4):
                tile = jnp.where(face == n, pltpu.roll(read(2 + n, c, k), 8 * n, 1), tile)
            out[4 * c + k] = tile
        for f in range(2):
            for t in range(2):
                for h in range(2):
                    r = 4 * f + 2 * t + h
                    out[20 + c, r : r + 1, :] = read(f, c, 2 * h + t)[0:1]
        return carry

    lax.fori_loop(0, 5, body, 0)


def part_layers(layers, out):
    def body(c, carry):
        for n in range(4):
            for k in range(4):
                out[n, c, k] = pltpu.roll(layers[4 * c + k], (128 - 8 * n) % 128, 1)
        return carry

    lax.fori_loop(0, 5, body, 0)


def late_rims(recv, where, which, row_mask, rims):
    for f in range(2):
        for t in range(2):
            item = f * 16 + 8 * t
            r = 4 * f + 2 * t
            tile = rim_tile(recv, where[item], which[item])
            for c in range(4):
                rims[20 + c, r : r + 2, :] = tile[2 * c : 2 * c + 2]
            tile = recv[where[item], 4]
            rims[24, r : r + 2, :] = jnp.where(which[item] == 1, tile[2:4], tile[0:2])
    items = [f * 16 + 8 * t for t in range(2) for _ in range(2) for f in range(2, 6)]
    tiles = turn([rim_tile(recv, where[i], which[i]) for i in items])
    for m in range(16):
        rims[m] = tiles[m]
    tiles = []
    for t in range(2):
        rows = unsqueeze(
            [recv[where[i], 4] for i in items[8 * t : 8 * t + 8]], row_mask[12 + t] > 0.5
        )
        tiles += [rows[j] for j in range(8)]
    tiles = last_tiles(turn(tiles))
    for m in range(4):
        rims[16 + m] = tiles[m]


def spread_rows(tile, u):
    sub = iota(0)
    result = pltpu.roll(tile, 4, 0) if u else tile
    base = result
    for r in range(1, 5):
        result = jnp.where((sub + 1) // 2 == r, pltpu.roll(base, r, 0), result)
    return result


def sibling_ghosts(V, G):
    def x_body(c, carry):
        for f in range(2):
            for layer in range(2):
                for k in range(4):
                    near = V[0, c, (layer if f else 14 + layer), k]
                    G[f, c, layer, k] = pltpu.roll(near, 4, 0)
        return carry

    def body(c, carry):
        for f in range(2, 6):
            a, s = f // 2, f % 2
            by = (128 - 8 * BIT_OF[a]) if s else 8 * BIT_OF[a]
            for layer in range(2):
                for k in range(4):
                    near = V[a, c, (layer if s else 14 + layer), k]
                    G[f, c, layer, k] = pltpu.roll(near, by, 1)
        return carry

    lax.fori_loop(0, 5, x_body, 0)
    lax.fori_loop(0, 5, body, 0)


def coarse_ghosts(rims, G, late=None):
    lane = iota(1)
    sub = iota(0)

    def rim(*index):
        value = rims[index]
        return value if late is None else 0.5 * (value + late[index])

    def x_body(c, carry):
        first = (sub // 2) % 2 == 1
        second = sub % 2
        for f in range(2):
            outer = (sub // 4) % 2 == f
            for t in range(2):
                r = 4 * f + 2 * t
                row = [
                    jnp.broadcast_to(rim(20 + c, pl.ds(r + h, 1), slice(None)), (8, 128))
                    for h in range(2)
                ]
                source = jnp.where(first, row[1], row[0])
                for h in range(2):
                    index = (4 * h + lane // 32) * 16 + 8 * second + (lane % 16) // 2
                    coarse = take(source, index)
                    for layer in range(2):
                        k = 2 * h + t
                        G[f, c, layer, k] = jnp.where(outer, coarse, G[f, c, layer, k])
        return carry

    octant = lane // 8 % 8

    def body(c, carry):
        source = [rim(4 * c + k) for k in range(4)]
        second = octant // 4 == 1
        for f in range(2, 6):
            a, s = f // 2, f % 2
            outer = octant // BIT_OF[a] % 2 == s
            first = octant // TANGENT[a][0] % 2 == 1
            for X in range(2):
                index = (lane // 64 * 8 + f - 2) * 8 + 4 * X + lane % 8 // 2
                four = [take(tile, index) for tile in source]
                low = jnp.where(second, four[1], four[0])
                high = jnp.where(second, four[3], four[2])
                chosen = jnp.where(first, high, low)
                for u in range(2):
                    coarse = spread_rows(chosen, u)
                    for layer in range(2):
                        k = 2 * u + X
                        G[f, c, layer, k] = jnp.where(outer, coarse, G[f, c, layer, k])
        return carry

    lax.fori_loop(0, 5, x_body, 0)
    lax.fori_loop(0, 5, body, 0)


def pair_sums(low, high):
    lane = iota(1)
    index = (lane // 16 % 4) * 32 + 2 * (lane % 8)
    sums = []
    for tile in (low, high):
        tile = tile + pltpu.roll(tile, 127, 1)
        sums.append(take(tile + pltpu.roll(tile, 112, 1), index))
    merged = jnp.where(lane < 64, sums[0], sums[1])
    return jnp.where(lane % 16 < 8, merged, pltpu.roll(merged, 7, 0))


def restrict_cells(N, mixed):
    def body(n, carry):
        t = n % 2
        c = n // 2
        merged = []
        for X in range(2):
            rows = [flip8([N[8 * t + j, c, X, h] for j in range(8)]) for h in range(2)]
            for x in range(4):
                low, high = [rows[h][2 * x] + rows[h][2 * x + 1] for h in range(2)]
                merged.append(pair_sums(low, high) * 0.125)
        rows = flip8(merged)
        for X in range(2):
            for h in range(2):
                mixed[t, c, X, h] = rows[4 * X + 2 * h]
        return carry

    lax.fori_loop(0, 10, body, 0)


def restrict_faces(FC, means):
    lane = iota(1)
    sub = iota(0)

    def x_body(c, carry):
        for f in range(2):
            for t in range(2):
                merged = pair_sums(FC[f, c, t], FC[f, c, 2 + t]) * 0.125
                for h in range(2):
                    o = 4 * f + 2 * h
                    r = 4 * f + 2 * t + h
                    means[20 + c, r : r + 1, :] = merged[o : o + 1]
        return carry

    def body(c, carry):
        index = lane // 8 * 8 + 2 * (lane % 4)
        for n in range(4):
            result = None
            for u in range(2):
                sums = []
                for X in range(2):
                    tile = FC[2 + n, c, 2 * u + X]
                    tile = tile + pltpu.roll(tile, 127, 1)
                    sums.append(take(tile + pltpu.roll(tile, 7, 0), index))
                merged = jnp.where(lane % 8 < 4, sums[0], sums[1])
                for i in range(4):
                    moved = pltpu.roll(merged, (8 - i) % 8, 0) if u == 0 else pltpu.roll(merged, 4 - i, 0)
                    if result is None:
                        result = moved
                    else:
                        result = jnp.where(sub == 4 * u + i, moved, result)
            means[5 * n + c] = result * 0.125
        return carry

    lax.fori_loop(0, 5, x_body, 0)
    lax.fori_loop(0, 5, body, 0)


def make_deltas(layers, parted, means, items):
    for f in range(2):
        for t in range(2):
            item = f * 16 + 8 * t
            for c in range(5):
                for h in range(2):
                    r = 4 * f + 2 * t + h
                    delta = layers[20 + c, r : r + 1, :] - means[20 + c, r : r + 1, :]
                    if c < 4:
                        row = 2 * (c % 2) + h
                        items[item, c // 2, row : row + 1, :] = delta
                    else:
                        items[item, 2, h : h + 1, :] = delta
                        items[item, 2, 2 + h : 3 + h, :] = delta
    for n in range(4):
        a, s = 1 + n // 2, n % 2
        codes = []
        for c in range(5):
            fine = means[5 * n + c]
            codes.append([])
            for k in range(4):
                o = s * BIT_OF[a] + (k // 2) * TANGENT[a][0] + (k % 2) * 4
                moved = pltpu.roll(fine, (128 - 8 * o) % 128, 1)
                codes[c].append(parted[n, c, k] - moved)
        store_rims(items, (2 + n) * 16, codes, (0, 8))


def take_mixed(N, mixed):
    def body(c, carry):
        for t in range(2):
            for X in range(2):
                for h in range(2):
                    N[8 * t, c, X, h] = mixed[t, c, X, h]
        return carry

    lax.fori_loop(0, 5, body, 0)


def apply_corrections(recv, where, which, row_mask, change, N):
    sub = iota(0)

    def x_body(q, carry):
        for s in range(2):
            scale = RATIO if s else -RATIO
            item = s * 16 + q
            e = where[item]
            k = which[item]
            tile = recv[e, 4]
            last = jnp.where(k == 1, tile[2:4], tile[0:2])
            tile = rim_tile(recv, e, k)
            for c in range(5):
                for h in range(2):
                    row = tile[2 * c + h : 2 * c + h + 1] if c < 4 else last[h : h + 1]
                    row = jnp.broadcast_to(scale * row, (8, 128))
                    N[q, c, s, h] = N[q, c, s, h] + jnp.where(sub == 7 * s, row, 0.0)
        return carry

    lax.fori_loop(0, 16, x_body, 0)

    for n in range(4):
        scale = RATIO if n % 2 else -RATIO
        first = (2 + n) * 16
        tiles = turn([rim_tile(recv, where[first + q], which[first + q]) for q in range(16)])
        for m in range(16):
            change[n, m // 4, m % 4] = scale * tiles[m]
        tiles = []
        for t in range(2):
            rows = unsqueeze(
                [recv[where[first + 8 * t + j], 4] for j in range(8)],
                row_mask[4 + 2 * n + t] > 0.5,
            )
            tiles += [rows[j] for j in range(8)]
        tiles = last_tiles(turn(tiles))
        for m in range(4):
            change[n, 4, m] = scale * tiles[m]

    def body(X, carry):
        for c in range(5):
            c1, c2 = ORDER[1].index(c), ORDER[2].index(c)
            for h in range(2):
                tiles = []
                for y in range(8):
                    for z in range(2):
                        row = jnp.broadcast_to(
                            change[2 + z, c2, 2 * h + X, y : y + 1, :], (8, 128)
                        )
                        tile = jnp.where(sub == 7 * z, row, 0.0)
                        if y == 7 * h:
                            tile = tile + change[h, c1, 2 * z + X]
                        tiles.append(tile)
                tiles = turn(tiles)
                for q in range(16):
                    N[q, c, X, h] = N[q, c, X, h] + tiles[q]
        return carry

    lax.fori_loop(0, 2, body, 0)


def step_kernel(
    devices,
    perm,
    slots,
    where,
    which,
    fluid_hbm,
    row_mask,
    lane_mask,
    out,
    N,
    V,
    D,
    G,
    FC,
    change,
    items1,
    items2,
    items3,
    send1,
    recv1,
    send2,
    recv2,
    send3,
    recv3,
    early_out,
    early_in,
    faces_out,
    faces_in,
    mixed_out,
    mixed_in,
    late,
    means,
    send_sems,
    recv_sems,
    pair_send,
    pair_recv,
    ready,
    fluid,
    load_sem,
):
    level = lax.axis_index("level")
    me = lax.axis_index("blk")
    other = 1 - level
    barrier = pltpu.get_barrier_semaphore()

    def start_all(send, recv, n, target):
        for dz, dx, dy in send_order():
            d = dz * 16 + dx * 4 + dy - 1
            pltpu.make_async_remote_copy(
                src_ref=send.at[d],
                dst_ref=recv.at[d],
                send_sem=send_sems.at[n],
                recv_sem=recv_sems.at[n],
                device_id=(target, far[dz] + mid[dx] + near[dy]),
                device_id_type=MESH,
            ).start()

    def whole(send, recv, n):
        return pltpu.make_async_remote_copy(
            src_ref=send,
            dst_ref=recv,
            send_sem=send_sems.at[n],
            recv_sem=recv_sems.at[n],
            device_id=(level, lax.rem(me + 1, devices)),
            device_id_type=MESH,
        )

    def to_pair(source, target, n):
        return pltpu.make_async_remote_copy(
            src_ref=source,
            dst_ref=target,
            send_sem=pair_send.at[n],
            recv_sem=pair_recv.at[n],
            device_id=(other, me),
            device_id_type=MESH,
        )

    def greet(semaphore, peers):
        for peer in peers:
            pl.semaphore_signal(
                semaphore, inc=1, device_id=(level, peer), device_id_type=MESH
            )

    far = [lax.rem(me // 16 + i, 8) * 16 for i in range(8)]
    mid = [lax.rem(me // 4 % 4 + i, 4) * 4 for i in range(4)]
    near = [lax.rem(me % 4 + i, 4) for i in range(4)]
    line = [far[i] + mid[0] + near[0] for i in range(1, 8)]
    plane = [far[0] + mid[i] + near[j] for i in range(4) for j in range(4) if i or j]

    pl.semaphore_signal(barrier, inc=1, device_id=(other, me), device_id_type=MESH)

    @pl.when(level == 0)
    def _():
        greet(barrier, line + plane)

    copy = pltpu.make_async_copy(fluid_hbm, fluid, load_sem)
    copy.start()
    copy.wait()
    make_views(N, V, fluid, perm)

    @pl.when(level == 0)
    def _():
        pl.semaphore_wait(barrier, 23)
        greet(ready, line)
        make_slabs(V, items1)
        pack_slabs(items1, slots, send1)
        pl.semaphore_wait(ready, 7)
        start_all(send1, recv1, 0, 0)

    @pl.when(level == 1)
    def _():
        pl.semaphore_wait(barrier, 1)

        def clear(n, carry):
            for g in range(3):
                items3[n, g] = jnp.zeros((4, 128), F32)
            return carry

        lax.fori_loop(0, 96, clear, 0)

    inner_sweep(V, D)

    @pl.when(level == 0)
    def _():
        whole(send1, recv1, 0).wait_recv()
        collect_slabs(recv1, where, which, row_mask, lane_mask, G)
        parent_layers(lambda f, c, k: G[f, c, 1 - f % 2, k], early_out)
        to_pair(early_out, early_in, 0).start()

    @pl.when(level == 1)
    def _():
        sibling_ghosts(V, G)
        to_pair(early_out, early_in, 0).wait_recv()
        coarse_ghosts(early_in, G)

    outer_sweep(V, G, D, FC, True)
    update(N, D)
    make_views(N, V)

    @pl.when(level == 0)
    def _():
        make_rims(V, items2)
        pack_rims(items2, slots, send2)
        start_all(send2, recv2, 1, 1)
        parent_layers(lambda f, c, k: FC[f, c, k], faces_out)
        to_pair(faces_out, faces_in, 1).start()
        to_pair(mixed_out, mixed_in, 2).wait_recv()
        take_mixed(N, mixed_in)
        whole(send3, recv3, 2).wait_recv()
        apply_corrections(recv3, where, which, row_mask, change, N)

    @pl.when(level == 1)
    def _():
        inner_sweep(V, D)
        sibling_ghosts(V, G)
        to_pair(faces_out, faces_in, 1).wait_recv()
        part_layers(faces_in, change)
        whole(send2, recv2, 1).wait_recv()
        late_rims(recv2, where, which, row_mask, late)
        coarse_ghosts(early_in, G, late)
        outer_sweep(V, G, D, FC, False)
        restrict_faces(FC, means)
        make_deltas(faces_in, change, means, items3)
        pack_rims(items3, slots, send3)
        start_all(send3, recv3, 2, 0)
        update(N, D)
        restrict_cells(N, mixed_out)
        to_pair(mixed_out, mixed_in, 2).start()

    store_state(N, out)

    @pl.when(level == 0)
    def _():
        whole(send1, recv1, 0).wait_send()
        whole(send2, recv2, 1).wait_send()
        to_pair(early_out, early_in, 0).wait_send()
        to_pair(faces_out, faces_in, 1).wait_send()

    @pl.when(level == 1)
    def _():
        whole(send3, recv3, 2).wait_send()
        to_pair(mixed_out, mixed_in, 2).wait_send()


def place_kernel(back, source, out):
    def body(b, carry):
        out[0, b] = source[back[b]]
        return carry

    lax.fori_loop(0, out.shape[1], body, 0)


def tables(neighbours, parents, level, me, count, devices):
    rows = lax.dynamic_slice_in_dim(neighbours, me * count, count, 0)
    family = lax.dynamic_slice_in_dim(parents, me * count, count, 0)
    ids = jnp.arange(count, dtype=jnp.int32)
    owner = family[:, 0] - me * count
    owns = owner[:, None] == ids[None, :]
    is_parent = jnp.any(owns, axis=0)
    earlier = ids[None, :] < ids[:, None]
    parent_rank = jnp.sum(is_parent[None, :] & earlier, axis=1, dtype=jnp.int32)
    rest_rank = ids - parent_rank
    coarse_place = jnp.where(
        is_parent, 8 * parent_rank, jnp.where(rest_rank < 7, 1 + rest_rank, 2 + rest_rank)
    )
    fine_place = 8 * jnp.sum(jnp.where(owns, parent_rank[None, :], 0), axis=1) + family[:, 1]
    place = jnp.where(level == 0, coarse_place, fine_place).astype(jnp.int32)

    def inverse(position):
        return jnp.sum(
            jnp.where(position[None, :] == ids[:, None], ids[None, :], 0), axis=1, dtype=jnp.int32
        )

    coarse_perm = inverse(coarse_place)
    chosen = coarse_perm[:, None] == ids[None, :]
    ordered = jnp.sum(jnp.where(chosen[:, :, None], rows[None], 0), axis=1, dtype=jnp.int32)
    ordered = ordered.T.reshape(-1)
    faces = jnp.repeat(jnp.arange(6, dtype=jnp.int32), count)
    target = ordered // count
    own_id = jnp.tile(coarse_perm, 6) * 6 + faces
    their_id = ordered % count * 6 + faces + 1 - 2 * (faces % 2)
    key = jnp.where(me < target, own_id, their_id)
    which = jnp.sum(
        (target[:, None] == target[None, :]) & (key[None, :] < key[:, None]),
        axis=1,
        dtype=jnp.int32,
    )
    far, mid, near = target // 16 - me // 16, target // 4 % 4 - me // 4 % 4, target % 4 - me % 4
    to = (far % 8) * 16 + (mid % 4) * 4 + near % 4 - 1
    come = (-far % 8) * 16 + (-mid % 4) * 4 + (-near) % 4 - 1
    item_ids = jnp.arange(6 * count, dtype=jnp.int32)
    slot_ids = jnp.arange(2 * devices, dtype=jnp.int32)
    slots = jnp.sum(
        jnp.where((2 * to + which)[None, :] == slot_ids[:, None], item_ids[None, :], 0),
        axis=1,
        dtype=jnp.int32,
    )
    second = which.astype(F32).reshape(6, count)
    late = jnp.stack([second[2:, 0], second[2:, 0], second[2:, 8], second[2:, 8]])
    rows = jnp.concatenate([second.reshape(12, 8), late.reshape(2, 8)])
    row_mask = jnp.broadcast_to(rows[:, :, None], (14, 8, 128))
    lane_mask = jnp.broadcast_to(jnp.repeat(second[2:], 8, axis=1)[:, None, :], (4, 8, 128))
    return inverse(place), place, slots, come, which, row_mask, lane_mask


def local(fluid_state, neighbours, parents):
    level = lax.axis_index("level")
    me = lax.axis_index("blk")
    devices = lax.axis_size("blk")
    count = fluid_state.shape[1]
    perm, place, slots, where, which, row_mask, lane_mask = tables(
        neighbours, parents, level, me, count, devices
    )
    smem = pl.BlockSpec(memory_space=pltpu.SMEM)
    vmem = pl.BlockSpec(memory_space=pltpu.VMEM)
    peers = devices - 1

    def step(*refs):
        step_kernel(devices, *refs)

    result = pl.pallas_call(
        step,
        out_shape=jax.ShapeDtypeStruct(fluid_state.shape[1:], F32),
        in_specs=[smem] * 4 + [pl.BlockSpec(memory_space=pl.ANY)] + [vmem] * 2,
        out_specs=vmem,
        scratch_shapes=[
            pltpu.VMEM((16, 5, 2, 2, 8, 128), F32),
            pltpu.VMEM((3, 5, 16, 4, 8, 128), F32),
            pltpu.VMEM((3, 5, 16, 4, 8, 128), F32),
            pltpu.VMEM((6, 5, 2, 4, 8, 128), F32),
            pltpu.VMEM((6, 5, 4, 8, 128), F32),
            pltpu.VMEM((4, 5, 4, 8, 128), F32),
            pltpu.VMEM((96, 3, 8, 128), F32),
            pltpu.VMEM((96, 3, 4, 128), F32),
            pltpu.VMEM((96, 3, 4, 128), F32),
            pltpu.VMEM((peers, 5, 8, 128), F32),
            pltpu.VMEM((peers, 5, 8, 128), F32),
            pltpu.VMEM((peers, 5, 4, 128), F32),
            pltpu.VMEM((peers, 5, 4, 128), F32),
            pltpu.VMEM((peers, 5, 4, 128), F32),
            pltpu.VMEM((peers, 5, 4, 128), F32),
            pltpu.VMEM((25, 8, 128), F32),
            pltpu.VMEM((25, 8, 128), F32),
            pltpu.VMEM((25, 8, 128), F32),
            pltpu.VMEM((25, 8, 128), F32),
            pltpu.VMEM((2, 5, 2, 2, 8, 128), F32),
            pltpu.VMEM((2, 5, 2, 2, 8, 128), F32),
            pltpu.VMEM((25, 8, 128), F32),
            pltpu.VMEM((25, 8, 128), F32),
            pltpu.SemaphoreType.DMA((3,)),
            pltpu.SemaphoreType.DMA((3,)),
            pltpu.SemaphoreType.DMA((3,)),
            pltpu.SemaphoreType.DMA((3,)),
            pltpu.SemaphoreType.REGULAR,
            pltpu.VMEM(fluid_state.shape, F32),
            pltpu.SemaphoreType.DMA,
        ],
        compiler_params=pltpu.CompilerParams(
            collective_id=0, has_side_effects=True, vmem_limit_bytes=60 * 1024 * 1024
        ),
    )(perm, slots, where, which, fluid_state, row_mask, lane_mask)
    return pl.pallas_call(
        place_kernel,
        out_shape=jax.ShapeDtypeStruct(fluid_state.shape, F32),
        in_specs=[smem, vmem],
        out_specs=vmem,
    )(place, result)


def solution(mesh):
    return jax.shard_map(
        local,
        mesh=mesh,
        in_specs=(P("level", "blk", None, None, None), P(), P()),
        out_specs=P("level", "blk", None, None, None),
        check_vma=False,
    )
```

```python
import jax
import jax.numpy as jnp
from jax import lax
from jax.experimental import pallas as pl
from jax.experimental.pallas import tpu as pltpu
from jax.sharding import PartitionSpec as P

GAMMA = 1.4
RATIO = 0.12
MESH = pl.DeviceIdType.MESH
ORDER = ((0, 1, 2, 3, 4), (0, 2, 1, 3, 4), (0, 3, 1, 2, 4))
BIT_OF = (4, 2, 1)
TANGENT = ((2, 1), (1, 4), (2, 4))
F32 = jnp.float32


def send_order():
    offsets = [(z, x, y) for z in range(8) for x in range(4) for y in range(4)][1:]
    mixed = [offsets[(53 * k + 26) % 127] for k in range(127)]
    return sorted(mixed, key=lambda o: -(min(o[0], 8 - o[0]) + min(o[1], 4 - o[1]) + min(o[2], 4 - o[2])))


def iota(axis):
    return lax.broadcasted_iota(jnp.int32, (8, 128), axis)


def take(tile, index):
    return jnp.take_along_axis(tile, index, axis=1, mode="promise_in_bounds")


def flip8(tiles):
    return jnp.swapaxes(jnp.stack(tiles), 0, 1)


def turn(tiles):
    whole = jnp.concatenate(tiles, axis=0).T
    return [whole[8 * i : 8 * i + 8] for i in range(16)]


def halves(tile):
    lane = iota(1)
    other = pltpu.roll(tile, 64, 1)
    return jnp.where(lane < 64, tile, other), jnp.where(lane < 64, other, tile)


def join(low, high, second):
    lane = iota(1)
    low = jnp.where(second, pltpu.roll(low, 64, 1), low)
    high = jnp.where(second, high, pltpu.roll(high, 64, 1))
    return jnp.where(lane < 64, low, high)


def prim(q):
    inverse = 1.0 / q[0]
    speed = q[1] * inverse
    kinetic = (q[1] * q[1] + q[2] * q[2] + q[3] * q[3]) * inverse
    return inverse, speed, (GAMMA - 1.0) * (q[4] - 0.5 * kinetic)


def flux_of(q, speed, pressure):
    return [q[1], q[1] * speed + pressure, q[2] * speed, q[3] * speed, (q[4] + pressure) * speed]


def half_step(below, here, above, low_wanted=True, high_wanted=True):
    low, high = [], []
    for u0, u1, u2 in zip(below, here, above):
        a = u1 - u0
        b = u2 - u1
        slope = jnp.maximum(jnp.minimum(a, b), 0.0) + jnp.minimum(jnp.maximum(a, b), 0.0)
        low.append(u1 - 0.5 * slope)
        high.append(u1 + 0.5 * slope)
    _, speed, pressure = prim(low)
    flux_low = flux_of(low, speed, pressure)
    _, speed, pressure = prim(high)
    flux_high = flux_of(high, speed, pressure)
    change = [0.5 * RATIO * (a - b) for a, b in zip(flux_low, flux_high)]
    low = [a + b for a, b in zip(low, change)] if low_wanted else None
    high = [a + b for a, b in zip(high, change)] if high_wanted else None
    return low, high


def with_sound(q):
    inverse, speed, pressure = prim(q)
    return q, inverse, speed, pressure, jnp.sqrt(GAMMA * pressure * inverse)


def contact_flux(low, high):
    ql, il, ul, pl_, cl = with_sound(low)
    qh, ih, uh, ph, ch = with_sound(high)
    slowest = jnp.minimum(ul - cl, uh - ch)
    fastest = jnp.maximum(ul + cl, uh + ch)
    mass_l = ql[0] * (slowest - ul)
    mass_h = qh[0] * (fastest - uh)
    contact = (ph - pl_ + ul * mass_l - uh * mass_h) / (mass_l - mass_h)
    lower = jnp.logical_or(slowest >= 0.0, contact >= 0.0)
    q = [jnp.where(lower, a, b) for a, b in zip(ql, qh)]
    inverse = jnp.where(lower, il, ih)
    speed = jnp.where(lower, ul, uh)
    pressure = jnp.where(lower, pl_, ph)
    mass = jnp.where(lower, mass_l, mass_h)
    wave = jnp.where(lower, slowest, fastest)
    outside = jnp.logical_or(slowest >= 0.0, jnp.logical_and(contact < 0.0, fastest <= 0.0))
    flux = flux_of(q, speed, pressure)
    over = 1.0 / (wave - contact)
    factor = mass * over
    scaled = factor * inverse
    gap = contact - speed
    star = [
        factor,
        factor * contact,
        scaled * q[2],
        scaled * q[3],
        scaled * q[4] + gap * (factor * contact + pressure * over),
    ]
    return [jnp.where(outside, f, f + wave * (s - u)) for f, s, u in zip(flux, star, q)]


def cells(V, a, i, ch):
    return [V[a, c, i, ch] for c in range(5)]


def ghost(G, a, s, layer, ch):
    return [G[2 * a + s, c, layer, ch] for c in range(5)]


def inner_sweep(V, D):
    def body(n, carry):
        a = n // 4
        ch = n % 4
        states = [cells(V, a, i, ch) for i in range(3)]
        _, high = half_step(*states)
        previous = None
        for i in range(2, 15):
            states = [states[1], states[2], cells(V, a, i + 1, ch)]
            low, next_high = half_step(*states)
            flux = contact_flux(high, low)
            for c in range(5):
                D[a, c, i - 1, ch] = flux[c] if previous is None else flux[c] - previous[c]
            high, previous = next_high, flux
        for c in range(5):
            D[a, c, 14, ch] = -previous[c]
        return carry

    lax.fori_loop(0, 12, body, 0)


def outer_sweep(V, G, D, FC, first):
    def body(n, carry):
        a = n // 4
        ch = n % 4
        u = [cells(V, a, i, ch) for i in range(3)]
        g = [ghost(G, a, 0, layer, ch) for layer in range(2)]
        _, r_ghost = half_step(g[0], g[1], u[0], low_wanted=False)
        l0, r0 = half_step(g[1], u[0], u[1])
        l1, _ = half_step(u[0], u[1], u[2], high_wanted=False)
        f0 = contact_flux(r_ghost, l0)
        f1 = contact_flux(r0, l1)
        for c in range(5):
            D[a, c, 0, ch] = f1[c] - f0[c]
            D[a, c, 1, ch] = D[a, c, 1, ch] - f1[c]
            FC[2 * a, c, ch] = f0[c] if first else FC[2 * a, c, ch] + f0[c]
        u = [cells(V, a, i, ch) for i in (13, 14, 15)]
        g = [ghost(G, a, 1, layer, ch) for layer in range(2)]
        _, r0 = half_step(u[0], u[1], u[2], low_wanted=False)
        l1, r1 = half_step(u[1], u[2], g[0])
        l2, _ = half_step(u[2], g[0], g[1], high_wanted=False)
        f0 = contact_flux(r0, l1)
        f1 = contact_flux(r1, l2)
        for c in range(5):
            D[a, c, 14, ch] = D[a, c, 14, ch] + f0[c]
            D[a, c, 15, ch] = f1[c] - f0[c]
            FC[2 * a + 1, c, ch] = f1[c] if first else FC[2 * a + 1, c, ch] + f1[c]
        return carry

    lax.fori_loop(0, 12, body, 0)


def update(N, D):
    def body(n, carry):
        X = n // 2
        h = n % 2
        for c in range(5):
            c1, c2 = ORDER[1].index(c), ORDER[2].index(c)
            tiles = [None] * 16
            for z in range(2):
                rows = flip8([D[2, c2, 8 * z + i, 2 * h + X] for i in range(8)])
                for y in range(8):
                    tiles[2 * y + z] = D[1, c1, 8 * h + y, 2 * z + X] + rows[y]
            tiles = turn(tiles)
            for t in range(2):
                rows = flip8([D[0, c, 8 * X + i, 2 * h + t] for i in range(8)])
                for j in range(8):
                    q = 8 * t + j
                    N[q, c, X, h] = N[q, c, X, h] - RATIO * (tiles[q] + rows[j])
        return carry

    lax.fori_loop(0, 4, body, 0)


def make_views(N, V, fluid=None, perm=None):
    def body(n, carry):
        X = n // 2
        h = n % 2
        for c in range(5):
            c1, c2 = ORDER[1].index(c), ORDER[2].index(c)
            tiles = []
            for q in range(16):
                if fluid is None:
                    tiles.append(N[q, c, X, h])
                else:
                    rows = pl.ds(pl.multiple_of(8 * X, 8), 8)
                    lanes = pl.ds(pl.multiple_of(128 * h, 128), 128)
                    tiles.append(fluid[0, perm[q], c, rows, lanes])
                    N[q, c, X, h] = tiles[q]
            for t in range(2):
                rows = flip8(tiles[8 * t : 8 * t + 8])
                for i in range(8):
                    V[0, c, 8 * X + i, 2 * h + t] = rows[i]
            tiles = turn(tiles)
            for z in range(2):
                for y in range(8):
                    V[1, c1, 8 * h + y, 2 * z + X] = tiles[2 * y + z]
                rows = flip8([tiles[2 * y + z] for y in range(8)])
                for i in range(8):
                    V[2, c2, 8 * z + i, 2 * h + X] = rows[i]
        return carry

    lax.fori_loop(0, 4, body, 0)


def store_state(N, out):
    def body(q, carry):
        for c in range(5):
            for X in range(2):
                for h in range(2):
                    out[q, c, 8 * X : 8 * X + 8, 128 * h : 128 * h + 128] = N[q, c, X, h]
        return carry

    lax.fori_loop(0, 16, body, 0)


def make_slabs(V, items):
    def x_body(n, carry):
        s = n // 2
        t = n % 2
        codes = [
            [V[0, c, 14 * s + layer, 2 * h + t] for layer in range(2) for h in range(2)]
            for c in range(5)
        ]
        last = [half for tile in codes[4] for half in halves(tile)]
        for g, tiles in enumerate((codes[0] + codes[1], codes[2] + codes[3], last)):
            rows = flip8(tiles)
            for j in range(8):
                items[s * 16 + 8 * t + j, g] = rows[j]
        return carry

    def body(n, carry):
        a = 1 + n // 2
        s = n % 2
        codes = [
            [V[a, c, 14 * s + layer, k] for layer in range(2) for k in range(4)] for c in range(5)
        ]
        for g, tiles in enumerate((codes[0] + codes[1], codes[2] + codes[3], codes[4] * 2)):
            tiles = turn(tiles)
            for q in range(16):
                items[(2 + n) * 16 + q, g] = tiles[q]
        return carry

    lax.fori_loop(0, 4, x_body, 0)
    lax.fori_loop(0, 4, body, 0)


def squeeze(tiles):
    group = iota(1) // 32
    rows = flip8(tiles)
    pair = []
    for r in range(2):
        row = rows[4 * r]
        for g in range(1, 4):
            row = jnp.where(group == g, rows[4 * r + g], row)
        pair.append(row)
    return flip8(pair * 4)


def unsqueeze(tiles, second):
    rows = flip8([jnp.concatenate([tile, tile], axis=0) for tile in tiles])
    pair = [jnp.where(second, rows[2 + r], rows[r]) for r in range(2)]
    return flip8([pair[0]] * 4 + [pair[1]] * 4)


def last_tiles(tiles):
    lane = iota(1)
    result = tiles[0:4]
    for g in range(1, 4):
        result = [jnp.where(lane % 4 == g, tiles[4 * g + m], result[m]) for m in range(4)]
    return result


def make_rims(V, items):
    def x_body(n, carry):
        s = n // 2
        t = n % 2
        codes = [V[0, c, 15 * s, 2 * h + t] for c in range(5) for h in range(2)]
        rows = flip8(codes[:8])
        last = flip8(codes[8:] * 4)
        for j in range(8):
            item = s * 16 + 8 * t + j
            items[item, 0] = rows[j, 0:4]
            items[item, 1] = rows[j, 4:8]
            items[item, 2] = last[j, 0:4]
        return carry

    def body(n, carry):
        a = 1 + n // 2
        s = n % 2
        codes = [[V[a, c, 15 * s, k] for k in range(4)] for c in range(5)]
        store_rims(items, (2 + n) * 16, codes, range(16))
        return carry

    lax.fori_loop(0, 4, x_body, 0)
    lax.fori_loop(0, 4, body, 0)


def store_rims(items, first, codes, blocks):
    tiles = turn(codes[0] + codes[1] + codes[2] + codes[3])
    last = turn(codes[4] * 4)
    for t in range(2):
        pairs = squeeze(last[8 * t : 8 * t + 8])
        for j in range(8):
            q = 8 * t + j
            if q in blocks:
                items[first + q, 0] = tiles[q][0:4]
                items[first + q, 1] = tiles[q][4:8]
                items[first + q, 2] = pairs[j, 0:4]


def rim_tile(recv, e, k):
    return jnp.concatenate([recv[e, 2 * k], recv[e, 2 * k + 1]], axis=0)


def pack_all(one, count):
    def body(n, carry):
        for i in range(4):
            one(4 * n + i)
        return carry

    lax.fori_loop(0, count // 4, body, 0)
    for d in range(count // 4 * 4, count):
        one(d)


def pack_slabs(items, slots, send):
    def one(d):
        lane = iota(1)
        i0 = slots[2 * d]
        i1 = slots[2 * d + 1]
        for g in range(2):
            send[d, g] = items[i0, g]
            send[d, 2 + g] = items[i1, g]
        send[d, 4] = jnp.where(lane < 64, items[i0, 2], items[i1, 2])

    pack_all(one, send.shape[0])


def pack_rims(items, slots, send):
    def one(d):
        first = lax.broadcasted_iota(jnp.int32, (4, 128), 0) < 2
        i0 = slots[2 * d]
        i1 = slots[2 * d + 1]
        for g in range(2):
            send[d, g] = items[i0, g]
            send[d, 2 + g] = items[i1, g]
        send[d, 4] = jnp.where(first, items[i0, 2], items[i1, 2])

    pack_all(one, send.shape[0])


def collect_slabs(recv, where, which, row_mask, lane_mask, G):
    def x_body(n, carry):
        s = n // 2
        t = n % 2
        second = row_mask[n] > 0.5
        first = s * 16 + 8 * t
        for g in range(2):
            rows = flip8([recv[where[first + j], 2 * which[first + j] + g] for j in range(8)])
            for m in range(8):
                c, layer, h = 2 * g + m // 4, m // 2 % 2, m % 2
                G[s, c, layer, 2 * h + t] = rows[m]
        rows = flip8([recv[where[first + j], 4] for j in range(8)])
        for layer in range(2):
            for h in range(2):
                m = 2 * layer + h
                G[s, 4, layer, 2 * h + t] = join(rows[2 * m], rows[2 * m + 1], second)
        return carry

    def body(n, carry):
        second = lane_mask[n] > 0.5
        first = (2 + n) * 16
        for g in range(2):
            tiles = turn([recv[where[first + q], 2 * which[first + q] + g] for q in range(16)])
            for m in range(16):
                G[2 + n, 2 * g + m // 8, m // 4 % 2, m % 4] = tiles[m]
        tiles = turn([recv[where[first + q], 4] for q in range(16)])
        for m in range(8):
            G[2 + n, 4, m // 4, m % 4] = jnp.where(second, tiles[8 + m], tiles[m])
        return carry

    lax.fori_loop(0, 4, x_body, 0)
    lax.fori_loop(0, 4, body, 0)


def make_masks(which, row_mask, lane_mask):
    def value(item):
        return which[item].astype(F32)

    def row_body(n, carry):
        mask = jnp.zeros((8, 128), F32)
        for j in range(8):
            mask = jnp.where(iota(0) == j, value(8 * n + j), mask)
        row_mask[n] = mask
        return carry

    def lane_body(n, carry):
        mask = jnp.zeros((8, 128), F32)
        for q in range(16):
            mask = jnp.where(iota(1) // 8 == q, value((2 + n) * 16 + q), mask)
        lane_mask[n] = mask
        return carry

    lax.fori_loop(0, 12, row_body, 0)
    lax.fori_loop(0, 4, lane_body, 0)
    for t in range(2):
        mask = jnp.zeros((8, 128), F32)
        for j in range(8):
            mask = jnp.where(iota(0) == j, value((2 + j % 4) * 16 + 8 * t), mask)
        row_mask[12 + t] = mask


def parent_layers(read, out):
    face = iota(1) // 8 % 8

    def body(c, carry):
        for k in range(4):
            tile = read(2, c, k)
            for n in range(1, 4):
                tile = jnp.where(face == n, pltpu.roll(read(2 + n, c, k), 8 * n, 1), tile)
            out[4 * c + k] = tile
        for f in range(2):
            for t in range(2):
                for h in range(2):
                    r = 4 * f + 2 * t + h
                    out[20 + c, r : r + 1, :] = read(f, c, 2 * h + t)[0:1]
        return carry

    lax.fori_loop(0, 5, body, 0)


def part_layers(layers, out):
    def body(c, carry):
        for n in range(4):
            for k in range(4):
                out[n, c, k] = pltpu.roll(layers[4 * c + k], (128 - 8 * n) % 128, 1)
        return carry

    lax.fori_loop(0, 5, body, 0)


def late_rims(recv, where, which, row_mask, rims):
    for f in range(2):
        for t in range(2):
            item = f * 16 + 8 * t
            r = 4 * f + 2 * t
            tile = rim_tile(recv, where[item], which[item])
            for c in range(4):
                rims[20 + c, r : r + 2, :] = tile[2 * c : 2 * c + 2]
            tile = recv[where[item], 4]
            rims[24, r : r + 2, :] = jnp.where(which[item] == 1, tile[2:4], tile[0:2])
    items = [f * 16 + 8 * t for t in range(2) for _ in range(2) for f in range(2, 6)]
    tiles = turn([rim_tile(recv, where[i], which[i]) for i in items])
    for m in range(16):
        rims[m] = tiles[m]
    tiles = []
    for t in range(2):
        rows = unsqueeze(
            [recv[where[i], 4] for i in items[8 * t : 8 * t + 8]], row_mask[12 + t] > 0.5
        )
        tiles += [rows[j] for j in range(8)]
    tiles = last_tiles(turn(tiles))
    for m in range(4):
        rims[16 + m] = tiles[m]


def spread_rows(tile, u):
    sub = iota(0)
    result = pltpu.roll(tile, 4, 0) if u else tile
    base = result
    for r in range(1, 5):
        result = jnp.where((sub + 1) // 2 == r, pltpu.roll(base, r, 0), result)
    return result


def sibling_ghosts(V, G):
    def x_body(c, carry):
        for f in range(2):
            for layer in range(2):
                for k in range(4):
                    near = V[0, c, (layer if f else 14 + layer), k]
                    G[f, c, layer, k] = pltpu.roll(near, 4, 0)
        return carry

    def body(c, carry):
        for f in range(2, 6):
            a, s = f // 2, f % 2
            by = (128 - 8 * BIT_OF[a]) if s else 8 * BIT_OF[a]
            for layer in range(2):
                for k in range(4):
                    near = V[a, c, (layer if s else 14 + layer), k]
                    G[f, c, layer, k] = pltpu.roll(near, by, 1)
        return carry

    lax.fori_loop(0, 5, x_body, 0)
    lax.fori_loop(0, 5, body, 0)


def coarse_ghosts(rims, G, late=None):
    lane = iota(1)
    sub = iota(0)

    def rim(*index):
        value = rims[index]
        return value if late is None else 0.5 * (value + late[index])

    def x_body(c, carry):
        first = (sub // 2) % 2 == 1
        second = sub % 2
        for f in range(2):
            outer = (sub // 4) % 2 == f
            for t in range(2):
                r = 4 * f + 2 * t
                row = [
                    jnp.broadcast_to(rim(20 + c, pl.ds(r + h, 1), slice(None)), (8, 128))
                    for h in range(2)
                ]
                source = jnp.where(first, row[1], row[0])
                for h in range(2):
                    index = (4 * h + lane // 32) * 16 + 8 * second + (lane % 16) // 2
                    coarse = take(source, index)
                    for layer in range(2):
                        k = 2 * h + t
                        G[f, c, layer, k] = jnp.where(outer, coarse, G[f, c, layer, k])
        return carry

    octant = lane // 8 % 8

    def body(c, carry):
        source = [rim(4 * c + k) for k in range(4)]
        second = octant // 4 == 1
        for f in range(2, 6):
            a, s = f // 2, f % 2
            outer = octant // BIT_OF[a] % 2 == s
            first = octant // TANGENT[a][0] % 2 == 1
            for X in range(2):
                index = (lane // 64 * 8 + f - 2) * 8 + 4 * X + lane % 8 // 2
                four = [take(tile, index) for tile in source]
                low = jnp.where(second, four[1], four[0])
                high = jnp.where(second, four[3], four[2])
                chosen = jnp.where(first, high, low)
                for u in range(2):
                    coarse = spread_rows(chosen, u)
                    for layer in range(2):
                        k = 2 * u + X
                        G[f, c, layer, k] = jnp.where(outer, coarse, G[f, c, layer, k])
        return carry

    lax.fori_loop(0, 5, x_body, 0)
    lax.fori_loop(0, 5, body, 0)


def lane_pairs(low, high):
    even = iota(1) % 2 == 0
    return jnp.where(even, low + pltpu.roll(low, 127, 1), high + pltpu.roll(high, 1, 1))


def pair_sums(low, high):
    lane = iota(1)
    index = (lane // 16 % 4) * 32 + 2 * (lane % 8) + lane // 64
    pairs = lane_pairs(low, high)
    merged = take(pairs + pltpu.roll(pairs, 112, 1), index)
    return jnp.where(lane % 16 < 8, merged, pltpu.roll(merged, 7, 0))


def restrict_cells(N, mixed):
    def body(n, carry):
        t = n % 2
        c = n // 2
        merged = []
        for X in range(2):
            rows = [flip8([N[8 * t + j, c, X, h] for j in range(8)]) for h in range(2)]
            for x in range(4):
                low, high = [rows[h][2 * x] + rows[h][2 * x + 1] for h in range(2)]
                merged.append(pair_sums(low, high) * 0.125)
        rows = flip8(merged)
        for X in range(2):
            for h in range(2):
                mixed[t, c, X, h] = rows[4 * X + 2 * h]
        return carry

    lax.fori_loop(0, 10, body, 0)


def restrict_faces(FC, means):
    lane = iota(1)
    sub = iota(0)

    def body(c, carry):
        index = lane // 8 * 8 + 2 * (lane % 4) + lane // 4 % 2
        for n in range(4):
            result = None
            for u in range(2):
                pairs = lane_pairs(FC[2 + n, c, 2 * u], FC[2 + n, c, 2 * u + 1])
                merged = take(pairs + pltpu.roll(pairs, 7, 0), index)
                for i in range(4):
                    moved = pltpu.roll(merged, ((4 if u else 8) - i) % 8, 0)
                    result = moved if result is None else jnp.where(sub == 4 * u + i, moved, result)
            means[5 * n + c] = result * 0.125
        for f in range(2):
            for t in range(2):
                merged = pair_sums(FC[f, c, t], FC[f, c, 2 + t]) * 0.125
                for h in range(2):
                    o = 4 * f + 2 * h
                    r = 4 * f + 2 * t + h
                    means[20 + c, r : r + 1, :] = merged[o : o + 1]
        return carry

    lax.fori_loop(0, 5, body, 0)


def make_deltas(layers, parted, means, items):
    for f in range(2):
        for t in range(2):
            item = f * 16 + 8 * t
            for c in range(5):
                for h in range(2):
                    r = 4 * f + 2 * t + h
                    delta = layers[20 + c, r : r + 1, :] - means[20 + c, r : r + 1, :]
                    if c < 4:
                        row = 2 * (c % 2) + h
                        items[item, c // 2, row : row + 1, :] = delta
                    else:
                        items[item, 2, h : h + 1, :] = delta
                        items[item, 2, 2 + h : 3 + h, :] = delta
    for n in range(4):
        a, s = 1 + n // 2, n % 2
        codes = []
        for c in range(5):
            fine = means[5 * n + c]
            codes.append([])
            for k in range(4):
                o = s * BIT_OF[a] + (k // 2) * TANGENT[a][0] + (k % 2) * 4
                moved = pltpu.roll(fine, (128 - 8 * o) % 128, 1)
                codes[c].append(parted[n, c, k] - moved)
        store_rims(items, (2 + n) * 16, codes, (0, 8))


def take_mixed(N, mixed):
    def body(c, carry):
        for t in range(2):
            for X in range(2):
                for h in range(2):
                    N[8 * t, c, X, h] = mixed[t, c, X, h]
        return carry

    lax.fori_loop(0, 5, body, 0)


def apply_corrections(recv, where, which, row_mask, change, N):
    sub = iota(0)

    def x_body(q, carry):
        for s in range(2):
            scale = RATIO if s else -RATIO
            item = s * 16 + q
            e = where[item]
            k = which[item]
            tile = recv[e, 4]
            last = jnp.where(k == 1, tile[2:4], tile[0:2])
            tile = rim_tile(recv, e, k)
            for c in range(5):
                for h in range(2):
                    row = tile[2 * c + h : 2 * c + h + 1] if c < 4 else last[h : h + 1]
                    row = jnp.broadcast_to(scale * row, (8, 128))
                    N[q, c, s, h] = N[q, c, s, h] + jnp.where(sub == 7 * s, row, 0.0)
        return carry

    lax.fori_loop(0, 16, x_body, 0)

    for n in range(4):
        scale = RATIO if n % 2 else -RATIO
        first = (2 + n) * 16
        tiles = turn([rim_tile(recv, where[first + q], which[first + q]) for q in range(16)])
        for m in range(16):
            change[n, m // 4, m % 4] = scale * tiles[m]
        tiles = []
        for t in range(2):
            rows = unsqueeze(
                [recv[where[first + 8 * t + j], 4] for j in range(8)],
                row_mask[4 + 2 * n + t] > 0.5,
            )
            tiles += [rows[j] for j in range(8)]
        tiles = last_tiles(turn(tiles))
        for m in range(4):
            change[n, 4, m] = scale * tiles[m]

    def body(X, carry):
        for c in range(5):
            c1, c2 = ORDER[1].index(c), ORDER[2].index(c)
            for h in range(2):
                tiles = []
                for y in range(8):
                    for z in range(2):
                        row = jnp.broadcast_to(
                            change[2 + z, c2, 2 * h + X, y : y + 1, :], (8, 128)
                        )
                        tile = jnp.where(sub == 7 * z, row, 0.0)
                        if y == 7 * h:
                            tile = tile + change[h, c1, 2 * z + X]
                        tiles.append(tile)
                tiles = turn(tiles)
                for q in range(16):
                    N[q, c, X, h] = N[q, c, X, h] + tiles[q]
        return carry

    lax.fori_loop(0, 2, body, 0)


def step_kernel(
    devices,
    perm,
    slots,
    where,
    which,
    fluid_hbm,
    out,
    N,
    V,
    D,
    G,
    FC,
    change,
    items1,
    items2,
    items3,
    send1,
    recv1,
    send2,
    recv2,
    send3,
    recv3,
    early_out,
    early_in,
    faces_out,
    faces_in,
    mixed_out,
    mixed_in,
    late,
    means,
    send_sems,
    recv_sems,
    pair_send,
    pair_recv,
    ready,
    row_mask,
    lane_mask,
    fluid,
    load_sem,
):
    level = lax.axis_index("level")
    me = lax.axis_index("blk")
    other = 1 - level
    barrier = pltpu.get_barrier_semaphore()

    def start_all(send, recv, n, target):
        for dz, dx, dy in send_order():
            d = dz * 16 + dx * 4 + dy - 1
            pltpu.make_async_remote_copy(
                src_ref=send.at[d],
                dst_ref=recv.at[d],
                send_sem=send_sems.at[n],
                recv_sem=recv_sems.at[n],
                device_id=(target, far[dz] + mid[dx] + near[dy]),
                device_id_type=MESH,
            ).start()

    def whole(send, recv, n):
        return pltpu.make_async_remote_copy(
            src_ref=send,
            dst_ref=recv,
            send_sem=send_sems.at[n],
            recv_sem=recv_sems.at[n],
            device_id=(level, lax.rem(me + 1, devices)),
            device_id_type=MESH,
        )

    def to_pair(source, target, n):
        return pltpu.make_async_remote_copy(
            src_ref=source,
            dst_ref=target,
            send_sem=pair_send.at[n],
            recv_sem=pair_recv.at[n],
            device_id=(other, me),
            device_id_type=MESH,
        )

    def greet(semaphore, peers):
        for peer in peers:
            pl.semaphore_signal(
                semaphore, inc=1, device_id=(level, peer), device_id_type=MESH
            )

    far = [lax.rem(me // 16 + i, 8) * 16 for i in range(8)]
    mid = [lax.rem(me // 4 % 4 + i, 4) * 4 for i in range(4)]
    near = [lax.rem(me % 4 + i, 4) for i in range(4)]
    line = [far[i] + mid[0] + near[0] for i in range(1, 8)]
    plane = [far[0] + mid[i] + near[j] for i in range(4) for j in range(4) if i or j]

    pl.semaphore_signal(barrier, inc=1, device_id=(other, me), device_id_type=MESH)

    @pl.when(level == 0)
    def _():
        greet(barrier, line + plane)

    copy = pltpu.make_async_copy(fluid_hbm, fluid, load_sem)
    copy.start()
    copy.wait()
    make_views(N, V, fluid, perm)

    @pl.when(level == 0)
    def _():
        pl.semaphore_wait(barrier, 23)
        greet(ready, line)
        make_slabs(V, items1)
        pack_slabs(items1, slots, send1)
        pl.semaphore_wait(ready, 7)
        start_all(send1, recv1, 0, 0)

    @pl.when(level == 1)
    def _():
        pl.semaphore_wait(barrier, 1)

        def clear(n, carry):
            for g in range(3):
                items3[n, g] = jnp.zeros((4, 128), F32)
            return carry

        lax.fori_loop(0, 96, clear, 0)

    inner_sweep(V, D)
    make_masks(which, row_mask, lane_mask)

    @pl.when(level == 0)
    def _():
        whole(send1, recv1, 0).wait_recv()
        collect_slabs(recv1, where, which, row_mask, lane_mask, G)

    @pl.when(level == 1)
    def _():
        sibling_ghosts(V, G)
        to_pair(early_out, early_in, 0).wait_recv()
        coarse_ghosts(early_in, G)

    outer_sweep(V, G, D, FC, True)
    update(N, D)
    make_views(N, V)

    @pl.when(level == 0)
    def _():
        make_rims(V, items2)
        pack_rims(items2, slots, send2)
        parent_layers(lambda f, c, k: G[f, c, 1 - f % 2, k], early_out)
        to_pair(early_out, early_in, 0).start()
        start_all(send2, recv2, 1, 1)
        parent_layers(lambda f, c, k: FC[f, c, k], faces_out)
        to_pair(faces_out, faces_in, 1).start()
        to_pair(mixed_out, mixed_in, 2).wait_recv()
        take_mixed(N, mixed_in)
        whole(send3, recv3, 2).wait_recv()
        apply_corrections(recv3, where, which, row_mask, change, N)

    @pl.when(level == 1)
    def _():
        inner_sweep(V, D)
        sibling_ghosts(V, G)
        to_pair(faces_out, faces_in, 1).wait_recv()
        part_layers(faces_in, change)
        whole(send2, recv2, 1).wait_recv()
        late_rims(recv2, where, which, row_mask, late)
        coarse_ghosts(early_in, G, late)
        outer_sweep(V, G, D, FC, False)
        restrict_faces(FC, means)
        make_deltas(faces_in, change, means, items3)
        pack_rims(items3, slots, send3)
        start_all(send3, recv3, 2, 0)
        update(N, D)
        restrict_cells(N, mixed_out)
        to_pair(mixed_out, mixed_in, 2).start()

    store_state(N, out)

    @pl.when(level == 0)
    def _():
        whole(send1, recv1, 0).wait_send()
        whole(send2, recv2, 1).wait_send()
        to_pair(early_out, early_in, 0).wait_send()
        to_pair(faces_out, faces_in, 1).wait_send()

    @pl.when(level == 1)
    def _():
        whole(send3, recv3, 2).wait_send()
        to_pair(mixed_out, mixed_in, 2).wait_send()


def place_kernel(back, source, out, sems):
    copies = [
        pltpu.make_async_copy(source.at[back[b]], out.at[0, b], sems.at[b])
        for b in range(out.shape[1])
    ]
    for copy in copies:
        copy.start()
    for copy in copies:
        copy.wait()


def tables(neighbours, parents, level, me, count, devices):
    rows = lax.dynamic_slice_in_dim(neighbours, me * count, count, 0)
    family = lax.dynamic_slice_in_dim(parents, me * count, count, 0)
    ids = jnp.arange(count, dtype=jnp.int32)
    owner = family[:, 0] - me * count
    owns = owner[:, None] == ids[None, :]
    is_parent = jnp.any(owns, axis=0)
    earlier = ids[None, :] < ids[:, None]
    parent_rank = jnp.sum(is_parent[None, :] & earlier, axis=1, dtype=jnp.int32)
    rest_rank = ids - parent_rank
    coarse_place = jnp.where(
        is_parent, 8 * parent_rank, jnp.where(rest_rank < 7, 1 + rest_rank, 2 + rest_rank)
    )
    fine_place = 8 * jnp.sum(jnp.where(owns, parent_rank[None, :], 0), axis=1) + family[:, 1]
    place = jnp.where(level == 0, coarse_place, fine_place).astype(jnp.int32)

    def inverse(position):
        return jnp.sum(
            jnp.where(position[None, :] == ids[:, None], ids[None, :], 0), axis=1, dtype=jnp.int32
        )

    coarse_perm = inverse(coarse_place)
    chosen = coarse_perm[:, None] == ids[None, :]
    ordered = jnp.sum(jnp.where(chosen[:, :, None], rows[None], 0), axis=1, dtype=jnp.int32)
    ordered = ordered.T.reshape(-1)
    faces = jnp.repeat(jnp.arange(6, dtype=jnp.int32), count)
    target = ordered // count
    own_id = jnp.tile(coarse_perm, 6) * 6 + faces
    their_id = ordered % count * 6 + faces + 1 - 2 * (faces % 2)
    key = jnp.where(me < target, own_id, their_id)
    which = jnp.sum(
        (target[:, None] == target[None, :]) & (key[None, :] < key[:, None]),
        axis=1,
        dtype=jnp.int32,
    )
    far, mid, near = target // 16 - me // 16, target // 4 % 4 - me // 4 % 4, target % 4 - me % 4
    to = (far % 8) * 16 + (mid % 4) * 4 + near % 4 - 1
    come = (-far % 8) * 16 + (-mid % 4) * 4 + (-near) % 4 - 1
    item_ids = jnp.arange(6 * count, dtype=jnp.int32)
    slot_ids = jnp.arange(2 * devices, dtype=jnp.int32)
    slots = jnp.sum(
        jnp.where((2 * to + which)[None, :] == slot_ids[:, None], item_ids[None, :], 0),
        axis=1,
        dtype=jnp.int32,
    )
    return inverse(place), place, slots, come, which


def local(fluid_state, neighbours, parents):
    level = lax.axis_index("level")
    me = lax.axis_index("blk")
    devices = lax.axis_size("blk")
    count = fluid_state.shape[1]
    perm, place, slots, where, which = tables(
        neighbours, parents, level, me, count, devices
    )
    smem = pl.BlockSpec(memory_space=pltpu.SMEM)
    vmem = pl.BlockSpec(memory_space=pltpu.VMEM)
    peers = devices - 1

    def step(*refs):
        step_kernel(devices, *refs)

    result = pl.pallas_call(
        step,
        out_shape=jax.ShapeDtypeStruct(fluid_state.shape[1:], F32),
        in_specs=[smem] * 4 + [pl.BlockSpec(memory_space=pltpu.HBM)],
        out_specs=vmem,
        scratch_shapes=[
            pltpu.VMEM((16, 5, 2, 2, 8, 128), F32),
            pltpu.VMEM((3, 5, 16, 4, 8, 128), F32),
            pltpu.VMEM((3, 5, 16, 4, 8, 128), F32),
            pltpu.VMEM((6, 5, 2, 4, 8, 128), F32),
            pltpu.VMEM((6, 5, 4, 8, 128), F32),
            pltpu.VMEM((4, 5, 4, 8, 128), F32),
            pltpu.VMEM((96, 3, 8, 128), F32),
            pltpu.VMEM((96, 3, 4, 128), F32),
            pltpu.VMEM((96, 3, 4, 128), F32),
            pltpu.VMEM((peers, 5, 8, 128), F32),
            pltpu.VMEM((peers, 5, 8, 128), F32),
            pltpu.VMEM((peers, 5, 4, 128), F32),
            pltpu.VMEM((peers, 5, 4, 128), F32),
            pltpu.VMEM((peers, 5, 4, 128), F32),
            pltpu.VMEM((peers, 5, 4, 128), F32),
            pltpu.VMEM((25, 8, 128), F32),
            pltpu.VMEM((25, 8, 128), F32),
            pltpu.VMEM((25, 8, 128), F32),
            pltpu.VMEM((25, 8, 128), F32),
            pltpu.VMEM((2, 5, 2, 2, 8, 128), F32),
            pltpu.VMEM((2, 5, 2, 2, 8, 128), F32),
            pltpu.VMEM((25, 8, 128), F32),
            pltpu.VMEM((25, 8, 128), F32),
            pltpu.SemaphoreType.DMA((3,)),
            pltpu.SemaphoreType.DMA((3,)),
            pltpu.SemaphoreType.DMA((3,)),
            pltpu.SemaphoreType.DMA((3,)),
            pltpu.SemaphoreType.REGULAR,
            pltpu.VMEM((14, 8, 128), F32),
            pltpu.VMEM((4, 8, 128), F32),
            pltpu.VMEM(fluid_state.shape, F32),
            pltpu.SemaphoreType.DMA,
        ],
        compiler_params=pltpu.CompilerParams(
            collective_id=0, has_side_effects=True, vmem_limit_bytes=34 * 1024 * 1024
        ),
    )(perm, slots, where, which, fluid_state)
    return pl.pallas_call(
        place_kernel,
        out_shape=jax.ShapeDtypeStruct(fluid_state.shape, F32),
        in_specs=[smem, vmem],
        out_specs=pl.BlockSpec(memory_space=pl.ANY),
        scratch_shapes=[pltpu.SemaphoreType.DMA((count,))],
        compiler_params=pltpu.CompilerParams(vmem_limit_bytes=8 * 1024 * 1024),
    )(place, result)


def solution(mesh):
    return jax.shard_map(
        local,
        mesh=mesh,
        in_specs=(P("level", "blk", None, None, None), P(), P()),
        out_specs=P("level", "blk", None, None, None),
        check_vma=False,
    )
```

```python
import jax
import jax.numpy as jnp
from jax import lax
from jax.experimental import pallas as pl
from jax.experimental.pallas import tpu as pltpu
from jax.sharding import PartitionSpec as P

GAMMA = 1.4
RATIO = 0.12
MESH = pl.DeviceIdType.MESH
ORDER = ((0, 1, 2, 3, 4), (0, 2, 1, 3, 4), (0, 3, 1, 2, 4))
BIT_OF = (4, 2, 1)
TANGENT = ((2, 1), (1, 4), (2, 4))
F32 = jnp.float32


def send_order():
    offsets = [(z, x, y) for z in range(8) for x in range(4) for y in range(4)][1:]
    mixed = [offsets[(53 * k + 26) % 127] for k in range(127)]
    return sorted(mixed, key=lambda o: -(min(o[0], 8 - o[0]) + min(o[1], 4 - o[1]) + min(o[2], 4 - o[2])))


def iota(axis):
    return lax.broadcasted_iota(jnp.int32, (8, 128), axis)


def in_one(count, first, second):
    lax.fori_loop(0, count, lambda n, carry: second(n, first(n, carry)), 0)


def take(tile, index):
    return jnp.take_along_axis(tile, index, axis=1, mode="promise_in_bounds")


def flip8(tiles):
    return jnp.swapaxes(jnp.stack(tiles), 0, 1)


def turn(tiles):
    whole = jnp.concatenate(tiles, axis=0).T
    return [whole[8 * i : 8 * i + 8] for i in range(16)]


def halves(tile):
    lane = iota(1)
    other = pltpu.roll(tile, 64, 1)
    return jnp.where(lane < 64, tile, other), jnp.where(lane < 64, other, tile)


def join(low, high, second):
    lane = iota(1)
    low = jnp.where(second, pltpu.roll(low, 64, 1), low)
    high = jnp.where(second, high, pltpu.roll(high, 64, 1))
    return jnp.where(lane < 64, low, high)


def prim(q):
    inverse = 1.0 / q[0]
    speed = q[1] * inverse
    kinetic = (q[1] * q[1] + q[2] * q[2] + q[3] * q[3]) * inverse
    return inverse, speed, (GAMMA - 1.0) * (q[4] - 0.5 * kinetic)


def flux_of(q, speed, pressure):
    return [q[1], q[1] * speed + pressure, q[2] * speed, q[3] * speed, (q[4] + pressure) * speed]


def half_step(below, here, above, low_wanted=True, high_wanted=True):
    low, high = [], []
    for u0, u1, u2 in zip(below, here, above):
        a = u1 - u0
        b = u2 - u1
        slope = jnp.maximum(jnp.minimum(a, b), 0.0) + jnp.minimum(jnp.maximum(a, b), 0.0)
        low.append(u1 - 0.5 * slope)
        high.append(u1 + 0.5 * slope)
    _, speed, pressure = prim(low)
    flux_low = flux_of(low, speed, pressure)
    _, speed, pressure = prim(high)
    flux_high = flux_of(high, speed, pressure)
    change = [0.5 * RATIO * (a - b) for a, b in zip(flux_low, flux_high)]
    low = [a + b for a, b in zip(low, change)] if low_wanted else None
    high = [a + b for a, b in zip(high, change)] if high_wanted else None
    return low, high


def with_sound(q):
    inverse, speed, pressure = prim(q)
    return q, inverse, speed, pressure, jnp.sqrt(GAMMA * pressure * inverse)


def contact_flux(low, high):
    ql, il, ul, pl_, cl = with_sound(low)
    qh, ih, uh, ph, ch = with_sound(high)
    slowest = jnp.minimum(ul - cl, uh - ch)
    fastest = jnp.maximum(ul + cl, uh + ch)
    mass_l = ql[0] * (slowest - ul)
    mass_h = qh[0] * (fastest - uh)
    contact = (ph - pl_ + ul * mass_l - uh * mass_h) / (mass_l - mass_h)
    lower = jnp.logical_or(slowest >= 0.0, contact >= 0.0)
    q = [jnp.where(lower, a, b) for a, b in zip(ql, qh)]
    inverse = jnp.where(lower, il, ih)
    speed = jnp.where(lower, ul, uh)
    pressure = jnp.where(lower, pl_, ph)
    mass = jnp.where(lower, mass_l, mass_h)
    wave = jnp.where(lower, slowest, fastest)
    outside = jnp.logical_or(slowest >= 0.0, jnp.logical_and(contact < 0.0, fastest <= 0.0))
    flux = flux_of(q, speed, pressure)
    over = 1.0 / (wave - contact)
    factor = mass * over
    scaled = factor * inverse
    gap = contact - speed
    star = [
        factor,
        factor * contact,
        scaled * q[2],
        scaled * q[3],
        scaled * q[4] + gap * (factor * contact + pressure * over),
    ]
    return [jnp.where(outside, f, f + wave * (s - u)) for f, s, u in zip(flux, star, q)]


def cells(V, a, i, ch):
    return [V[a, c, i, ch] for c in range(5)]


def ghost(G, a, s, layer, ch):
    return [G[2 * a + s, c, layer, ch] for c in range(5)]


def inner_sweep(V, D):
    def body(n, carry):
        a = n // 4
        ch = n % 4
        states = [cells(V, a, i, ch) for i in range(3)]
        _, high = half_step(*states)
        previous = None
        for i in range(2, 15):
            states = [states[1], states[2], cells(V, a, i + 1, ch)]
            low, next_high = half_step(*states)
            flux = contact_flux(high, low)
            for c in range(5):
                D[a, c, i - 1, ch] = flux[c] if previous is None else flux[c] - previous[c]
            high, previous = next_high, flux
        for c in range(5):
            D[a, c, 14, ch] = -previous[c]
        return carry

    lax.fori_loop(0, 12, body, 0)


def outer_sweep(V, G, D, FC=None):
    def body(n, carry):
        a = n // 4
        ch = n % 4
        u = [cells(V, a, i, ch) for i in range(3)]
        g = [ghost(G, a, 0, layer, ch) for layer in range(2)]
        _, r_ghost = half_step(g[0], g[1], u[0], low_wanted=False)
        l0, r0 = half_step(g[1], u[0], u[1])
        l1, _ = half_step(u[0], u[1], u[2], high_wanted=False)
        f0 = contact_flux(r_ghost, l0)
        f1 = contact_flux(r0, l1)
        for c in range(5):
            D[a, c, 0, ch] = f1[c] - f0[c]
            D[a, c, 1, ch] = D[a, c, 1, ch] - f1[c]
            if FC is not None:
                FC[2 * a, c, ch] = f0[c]
        u = [cells(V, a, i, ch) for i in (13, 14, 15)]
        g = [ghost(G, a, 1, layer, ch) for layer in range(2)]
        _, r0 = half_step(u[0], u[1], u[2], low_wanted=False)
        l1, r1 = half_step(u[1], u[2], g[0])
        l2, _ = half_step(u[2], g[0], g[1], high_wanted=False)
        f0 = contact_flux(r0, l1)
        f1 = contact_flux(r1, l2)
        for c in range(5):
            D[a, c, 14, ch] = D[a, c, 14, ch] + f0[c]
            D[a, c, 15, ch] = f1[c] - f0[c]
            if FC is not None:
                FC[2 * a + 1, c, ch] = f1[c]
        return carry

    lax.fori_loop(0, 12, body, 0)


def edge_faces(V, G, FC):
    def body(n, carry):
        a = n // 4
        ch = n % 4
        u = [cells(V, a, i, ch) for i in range(2)]
        g = [ghost(G, a, 0, layer, ch) for layer in range(2)]
        _, high = half_step(g[0], g[1], u[0], low_wanted=False)
        low, _ = half_step(g[1], u[0], u[1], high_wanted=False)
        first = contact_flux(high, low)
        u = [cells(V, a, i, ch) for i in (14, 15)]
        g = [ghost(G, a, 1, layer, ch) for layer in range(2)]
        _, high = half_step(u[0], u[1], g[0], low_wanted=False)
        low, _ = half_step(u[1], g[0], g[1], high_wanted=False)
        last = contact_flux(high, low)
        for c in range(5):
            FC[2 * a, c, ch] = FC[2 * a, c, ch] + first[c]
            FC[2 * a + 1, c, ch] = FC[2 * a + 1, c, ch] + last[c]
        return carry

    lax.fori_loop(0, 12, body, 0)


def update(N, D):
    def body(n, carry):
        X = n // 2
        h = n % 2
        for c in range(5):
            c1, c2 = ORDER[1].index(c), ORDER[2].index(c)
            tiles = [None] * 16
            for z in range(2):
                rows = flip8([D[2, c2, 8 * z + i, 2 * h + X] for i in range(8)])
                for y in range(8):
                    tiles[2 * y + z] = D[1, c1, 8 * h + y, 2 * z + X] + rows[y]
            tiles = turn(tiles)
            for t in range(2):
                rows = flip8([D[0, c, 8 * X + i, 2 * h + t] for i in range(8)])
                for j in range(8):
                    q = 8 * t + j
                    N[q, c, X, h] = N[q, c, X, h] - RATIO * (tiles[q] + rows[j])
        return carry

    lax.fori_loop(0, 4, body, 0)


def make_views(N, V, fluid=None, perm=None):
    def body(n, carry):
        X = n // 2
        h = n % 2
        for c in range(5):
            c1, c2 = ORDER[1].index(c), ORDER[2].index(c)
            tiles = []
            for q in range(16):
                if fluid is None:
                    tiles.append(N[q, c, X, h])
                else:
                    rows = pl.ds(pl.multiple_of(8 * X, 8), 8)
                    lanes = pl.ds(pl.multiple_of(128 * h, 128), 128)
                    tiles.append(fluid[0, perm[q], c, rows, lanes])
                    N[q, c, X, h] = tiles[q]
            for t in range(2):
                rows = flip8(tiles[8 * t : 8 * t + 8])
                for i in range(8):
                    V[0, c, 8 * X + i, 2 * h + t] = rows[i]
            tiles = turn(tiles)
            for z in range(2):
                for y in range(8):
                    V[1, c1, 8 * h + y, 2 * z + X] = tiles[2 * y + z]
                rows = flip8([tiles[2 * y + z] for y in range(8)])
                for i in range(8):
                    V[2, c2, 8 * z + i, 2 * h + X] = rows[i]
        return carry

    lax.fori_loop(0, 4, body, 0)


def store_state(N, out):
    def body(q, carry):
        for c in range(5):
            for X in range(2):
                for h in range(2):
                    out[q, c, 8 * X : 8 * X + 8, 128 * h : 128 * h + 128] = N[q, c, X, h]
        return carry

    lax.fori_loop(0, 16, body, 0)


def make_slabs(V, items):
    def x_body(n, carry):
        s = n // 2
        t = n % 2
        codes = [
            [V[0, c, 14 * s + layer, 2 * h + t] for layer in range(2) for h in range(2)]
            for c in range(5)
        ]
        last = [half for tile in codes[4] for half in halves(tile)]
        for g, tiles in enumerate((codes[0] + codes[1], codes[2] + codes[3], last)):
            rows = flip8(tiles)
            for j in range(8):
                items[s * 16 + 8 * t + j, g] = rows[j]
        return carry

    def body(n, carry):
        a = 1 + n // 2
        s = n % 2
        codes = [
            [V[a, c, 14 * s + layer, k] for layer in range(2) for k in range(4)] for c in range(5)
        ]
        for g, tiles in enumerate((codes[0] + codes[1], codes[2] + codes[3], codes[4] * 2)):
            tiles = turn(tiles)
            for q in range(16):
                items[(2 + n) * 16 + q, g] = tiles[q]
        return carry

    in_one(4, x_body, body)


def squeeze(tiles):
    group = iota(1) // 32
    rows = flip8(tiles)
    pair = []
    for r in range(2):
        row = rows[4 * r]
        for g in range(1, 4):
            row = jnp.where(group == g, rows[4 * r + g], row)
        pair.append(row)
    return flip8(pair * 4)


def unsqueeze(tiles, second):
    rows = flip8([jnp.concatenate([tile, tile], axis=0) for tile in tiles])
    pair = [jnp.where(second, rows[2 + r], rows[r]) for r in range(2)]
    return flip8([pair[0]] * 4 + [pair[1]] * 4)


def last_tiles(tiles):
    lane = iota(1)
    result = tiles[0:4]
    for g in range(1, 4):
        result = [jnp.where(lane % 4 == g, tiles[4 * g + m], result[m]) for m in range(4)]
    return result


def make_rims(V, items):
    def x_body(n, carry):
        s = n // 2
        t = n % 2
        codes = [V[0, c, 15 * s, 2 * h + t] for c in range(5) for h in range(2)]
        rows = flip8(codes[:8])
        last = flip8(codes[8:] * 4)
        for j in range(8):
            item = s * 16 + 8 * t + j
            items[item, 0] = rows[j, 0:4]
            items[item, 1] = rows[j, 4:8]
            items[item, 2] = last[j, 0:4]
        return carry

    def body(n, carry):
        a = 1 + n // 2
        s = n % 2
        codes = [[V[a, c, 15 * s, k] for k in range(4)] for c in range(5)]
        store_rims(items, (2 + n) * 16, codes, range(16))
        return carry

    in_one(4, x_body, body)


def store_rims(items, first, codes, blocks):
    tiles = turn(codes[0] + codes[1] + codes[2] + codes[3])
    last = turn(codes[4] * 4)
    for t in range(2):
        pairs = squeeze(last[8 * t : 8 * t + 8])
        for j in range(8):
            q = 8 * t + j
            if q in blocks:
                items[first + q, 0] = tiles[q][0:4]
                items[first + q, 1] = tiles[q][4:8]
                items[first + q, 2] = pairs[j, 0:4]


def rim_tile(recv, e, k):
    return jnp.concatenate([recv[e, 2 * k], recv[e, 2 * k + 1]], axis=0)


def pack_all(one, count):
    def body(n, carry):
        for i in range(4):
            one(4 * n + i)
        return carry

    lax.fori_loop(0, count // 4, body, 0)
    for d in range(count // 4 * 4, count):
        one(d)


def pack_slabs(items, slots, send):
    def one(d):
        lane = iota(1)
        i0 = slots[2 * d]
        i1 = slots[2 * d + 1]
        for g in range(2):
            send[d, g] = items[i0, g]
            send[d, 2 + g] = items[i1, g]
        send[d, 4] = jnp.where(lane < 64, items[i0, 2], items[i1, 2])

    pack_all(one, send.shape[0])


def pack_rims(items, slots, send):
    def one(d):
        first = lax.broadcasted_iota(jnp.int32, (4, 128), 0) < 2
        i0 = slots[2 * d]
        i1 = slots[2 * d + 1]
        for g in range(2):
            send[d, g] = items[i0, g]
            send[d, 2 + g] = items[i1, g]
        send[d, 4] = jnp.where(first, items[i0, 2], items[i1, 2])

    pack_all(one, send.shape[0])


def collect_slabs(recv, where, which, row_mask, lane_mask, G):
    def x_body(n, carry):
        s = n // 2
        t = n % 2
        second = row_mask[n] > 0.5
        first = s * 16 + 8 * t
        for g in range(2):
            rows = flip8([recv[where[first + j], 2 * which[first + j] + g] for j in range(8)])
            for m in range(8):
                c, layer, h = 2 * g + m // 4, m // 2 % 2, m % 2
                G[s, c, layer, 2 * h + t] = rows[m]
        rows = flip8([recv[where[first + j], 4] for j in range(8)])
        for layer in range(2):
            for h in range(2):
                m = 2 * layer + h
                G[s, 4, layer, 2 * h + t] = join(rows[2 * m], rows[2 * m + 1], second)
        return carry

    def body(n, carry):
        second = lane_mask[n] > 0.5
        first = (2 + n) * 16
        for g in range(2):
            tiles = turn([recv[where[first + q], 2 * which[first + q] + g] for q in range(16)])
            for m in range(16):
                G[2 + n, 2 * g + m // 8, m // 4 % 2, m % 4] = tiles[m]
        tiles = turn([recv[where[first + q], 4] for q in range(16)])
        for m in range(8):
            G[2 + n, 4, m // 4, m % 4] = jnp.where(second, tiles[8 + m], tiles[m])
        return carry

    in_one(4, x_body, body)


def make_masks(which, row_mask, lane_mask):
    def value(item):
        return which[item].astype(F32)

    def row_body(n, carry):
        mask = jnp.zeros((8, 128), F32)
        for j in range(8):
            mask = jnp.where(iota(0) == j, value(8 * n + j), mask)
        row_mask[n] = mask
        return carry

    def lane_body(n, carry):
        mask = jnp.zeros((8, 128), F32)
        for q in range(16):
            mask = jnp.where(iota(1) // 8 == q, value((2 + n) * 16 + q), mask)
        lane_mask[n] = mask
        return carry

    lax.fori_loop(0, 12, row_body, 0)
    lax.fori_loop(0, 4, lane_body, 0)
    for t in range(2):
        mask = jnp.zeros((8, 128), F32)
        for j in range(8):
            mask = jnp.where(iota(0) == j, value((2 + j % 4) * 16 + 8 * t), mask)
        row_mask[12 + t] = mask


def parent_layers(read, out):
    face = iota(1) // 8 % 8

    def body(c, carry):
        for k in range(4):
            tile = read(2, c, k)
            for n in range(1, 4):
                tile = jnp.where(face == n, pltpu.roll(read(2 + n, c, k), 8 * n, 1), tile)
            out[4 * c + k] = tile
        for f in range(2):
            for t in range(2):
                for h in range(2):
                    r = 4 * f + 2 * t + h
                    out[20 + c, r : r + 1, :] = read(f, c, 2 * h + t)[0:1]
        return carry

    lax.fori_loop(0, 5, body, 0)


def part_layers(layers, out):
    def body(c, carry):
        for n in range(4):
            for k in range(4):
                out[n, c, k] = pltpu.roll(layers[4 * c + k], (128 - 8 * n) % 128, 1)
        return carry

    lax.fori_loop(0, 5, body, 0)


def late_rims(recv, where, which, row_mask, rims):
    for f in range(2):
        for t in range(2):
            item = f * 16 + 8 * t
            r = 4 * f + 2 * t
            tile = rim_tile(recv, where[item], which[item])
            for c in range(4):
                rims[20 + c, r : r + 2, :] = tile[2 * c : 2 * c + 2]
            tile = recv[where[item], 4]
            rims[24, r : r + 2, :] = jnp.where(which[item] == 1, tile[2:4], tile[0:2])
    items = [f * 16 + 8 * t for t in range(2) for _ in range(2) for f in range(2, 6)]
    tiles = turn([rim_tile(recv, where[i], which[i]) for i in items])
    for m in range(16):
        rims[m] = tiles[m]
    tiles = []
    for t in range(2):
        rows = unsqueeze(
            [recv[where[i], 4] for i in items[8 * t : 8 * t + 8]], row_mask[12 + t] > 0.5
        )
        tiles += [rows[j] for j in range(8)]
    tiles = last_tiles(turn(tiles))
    for m in range(4):
        rims[16 + m] = tiles[m]


def spread_rows(tile, u):
    sub = iota(0)
    result = pltpu.roll(tile, 4, 0) if u else tile
    base = result
    for r in range(1, 5):
        result = jnp.where((sub + 1) // 2 == r, pltpu.roll(base, r, 0), result)
    return result


def sibling_ghosts(V, G):
    def x_body(c, carry):
        for f in range(2):
            for layer in range(2):
                for k in range(4):
                    near = V[0, c, (layer if f else 14 + layer), k]
                    G[f, c, layer, k] = pltpu.roll(near, 4, 0)
        return carry

    def body(c, carry):
        for f in range(2, 6):
            a, s = f // 2, f % 2
            by = (128 - 8 * BIT_OF[a]) if s else 8 * BIT_OF[a]
            for layer in range(2):
                for k in range(4):
                    near = V[a, c, (layer if s else 14 + layer), k]
                    G[f, c, layer, k] = pltpu.roll(near, by, 1)
        return carry

    in_one(5, x_body, body)


def coarse_ghosts(rims, G, late=None):
    lane = iota(1)
    sub = iota(0)

    def rim(*index):
        value = rims[index]
        return value if late is None else 0.5 * (value + late[index])

    def x_body(c, carry):
        first = (sub // 2) % 2 == 1
        second = sub % 2
        for f in range(2):
            outer = (sub // 4) % 2 == f
            for t in range(2):
                r = 4 * f + 2 * t
                row = [
                    jnp.broadcast_to(rim(20 + c, pl.ds(r + h, 1), slice(None)), (8, 128))
                    for h in range(2)
                ]
                source = jnp.where(first, row[1], row[0])
                for h in range(2):
                    index = (4 * h + lane // 32) * 16 + 8 * second + (lane % 16) // 2
                    coarse = take(source, index)
                    for layer in range(2):
                        k = 2 * h + t
                        G[f, c, layer, k] = jnp.where(outer, coarse, G[f, c, layer, k])
        return carry

    octant = lane // 8 % 8

    def body(c, carry):
        source = [rim(4 * c + k) for k in range(4)]
        second = octant // 4 == 1
        for f in range(2, 6):
            a, s = f // 2, f % 2
            outer = octant // BIT_OF[a] % 2 == s
            first = octant // TANGENT[a][0] % 2 == 1
            for X in range(2):
                index = (lane // 64 * 8 + f - 2) * 8 + 4 * X + lane % 8 // 2
                four = [take(tile, index) for tile in source]
                low = jnp.where(second, four[1], four[0])
                high = jnp.where(second, four[3], four[2])
                chosen = jnp.where(first, high, low)
                for u in range(2):
                    coarse = spread_rows(chosen, u)
                    for layer in range(2):
                        k = 2 * u + X
                        G[f, c, layer, k] = jnp.where(outer, coarse, G[f, c, layer, k])
        return carry

    in_one(5, x_body, body)


def lane_pairs(low, high):
    even = iota(1) % 2 == 0
    return jnp.where(even, low + pltpu.roll(low, 127, 1), high + pltpu.roll(high, 1, 1))


def pair_sums(low, high):
    lane = iota(1)
    index = (lane // 16 % 4) * 32 + 2 * (lane % 8) + lane // 64
    pairs = lane_pairs(low, high)
    merged = take(pairs + pltpu.roll(pairs, 112, 1), index)
    return jnp.where(lane % 16 < 8, merged, pltpu.roll(merged, 7, 0))


def restrict_cells(N, mixed):
    def body(n, carry):
        t = n % 2
        c = n // 2
        merged = []
        for X in range(2):
            rows = [flip8([N[8 * t + j, c, X, h] for j in range(8)]) for h in range(2)]
            for x in range(4):
                low, high = [rows[h][2 * x] + rows[h][2 * x + 1] for h in range(2)]
                merged.append(pair_sums(low, high) * 0.125)
        rows = flip8(merged)
        for X in range(2):
            for h in range(2):
                mixed[t, c, X, h] = rows[4 * X + 2 * h]
        return carry

    lax.fori_loop(0, 10, body, 0)


def restrict_faces(FC, means):
    lane = iota(1)
    sub = iota(0)

    def body(c, carry):
        index = lane // 8 * 8 + 2 * (lane % 4) + lane // 4 % 2
        for n in range(4):
            result = None
            for u in range(2):
                pairs = lane_pairs(FC[2 + n, c, 2 * u], FC[2 + n, c, 2 * u + 1])
                merged = take(pairs + pltpu.roll(pairs, 7, 0), index)
                for i in range(4):
                    moved = pltpu.roll(merged, ((4 if u else 8) - i) % 8, 0)
                    result = moved if result is None else jnp.where(sub == 4 * u + i, moved, result)
            means[5 * n + c] = result * 0.125
        for f in range(2):
            for t in range(2):
                merged = pair_sums(FC[f, c, t], FC[f, c, 2 + t]) * 0.125
                for h in range(2):
                    o = 4 * f + 2 * h
                    r = 4 * f + 2 * t + h
                    means[20 + c, r : r + 1, :] = merged[o : o + 1]
        return carry

    lax.fori_loop(0, 5, body, 0)


def make_deltas(layers, parted, means, items):
    for f in range(2):
        for t in range(2):
            item = f * 16 + 8 * t
            for c in range(5):
                for h in range(2):
                    r = 4 * f + 2 * t + h
                    delta = layers[20 + c, r : r + 1, :] - means[20 + c, r : r + 1, :]
                    if c < 4:
                        row = 2 * (c % 2) + h
                        items[item, c // 2, row : row + 1, :] = delta
                    else:
                        items[item, 2, h : h + 1, :] = delta
                        items[item, 2, 2 + h : 3 + h, :] = delta
    for n in range(4):
        a, s = 1 + n // 2, n % 2
        codes = []
        for c in range(5):
            fine = means[5 * n + c]
            codes.append([])
            for k in range(4):
                o = s * BIT_OF[a] + (k // 2) * TANGENT[a][0] + (k % 2) * 4
                moved = pltpu.roll(fine, (128 - 8 * o) % 128, 1)
                codes[c].append(parted[n, c, k] - moved)
        store_rims(items, (2 + n) * 16, codes, (0, 8))


def take_mixed(N, mixed):
    def body(c, carry):
        for t in range(2):
            for X in range(2):
                for h in range(2):
                    N[8 * t, c, X, h] = mixed[t, c, X, h]
        return carry

    lax.fori_loop(0, 5, body, 0)


def apply_corrections(recv, where, which, row_mask, change, N):
    sub = iota(0)

    def x_body(q, carry):
        for s in range(2):
            scale = RATIO if s else -RATIO
            item = s * 16 + q
            e = where[item]
            k = which[item]
            tile = recv[e, 4]
            last = jnp.where(k == 1, tile[2:4], tile[0:2])
            tile = rim_tile(recv, e, k)
            for c in range(5):
                for h in range(2):
                    row = tile[2 * c + h : 2 * c + h + 1] if c < 4 else last[h : h + 1]
                    row = jnp.broadcast_to(scale * row, (8, 128))
                    N[q, c, s, h] = N[q, c, s, h] + jnp.where(sub == 7 * s, row, 0.0)
        return carry

    lax.fori_loop(0, 16, x_body, 0)

    for n in range(4):
        scale = RATIO if n % 2 else -RATIO
        first = (2 + n) * 16
        tiles = turn([rim_tile(recv, where[first + q], which[first + q]) for q in range(16)])
        for m in range(16):
            change[n, m // 4, m % 4] = scale * tiles[m]
        tiles = []
        for t in range(2):
            rows = unsqueeze(
                [recv[where[first + 8 * t + j], 4] for j in range(8)],
                row_mask[4 + 2 * n + t] > 0.5,
            )
            tiles += [rows[j] for j in range(8)]
        tiles = last_tiles(turn(tiles))
        for m in range(4):
            change[n, 4, m] = scale * tiles[m]

    def body(X, carry):
        for c in range(5):
            c1, c2 = ORDER[1].index(c), ORDER[2].index(c)
            for h in range(2):
                tiles = []
                for y in range(8):
                    for z in range(2):
                        row = jnp.broadcast_to(
                            change[2 + z, c2, 2 * h + X, y : y + 1, :], (8, 128)
                        )
                        tile = jnp.where(sub == 7 * z, row, 0.0)
                        if y == 7 * h:
                            tile = tile + change[h, c1, 2 * z + X]
                        tiles.append(tile)
                tiles = turn(tiles)
                for q in range(16):
                    N[q, c, X, h] = N[q, c, X, h] + tiles[q]
        return carry

    lax.fori_loop(0, 2, body, 0)


def step_kernel(
    devices,
    perm,
    slots,
    where,
    which,
    fluid_hbm,
    out,
    N,
    V,
    D,
    G,
    FC,
    change,
    items1,
    items2,
    items3,
    send1,
    recv1,
    send2,
    recv2,
    send3,
    recv3,
    early_out,
    early_in,
    faces_out,
    faces_in,
    mixed_out,
    mixed_in,
    late,
    means,
    send_sems,
    recv_sems,
    pair_send,
    pair_recv,
    ready,
    row_mask,
    lane_mask,
    fluid,
    load_sem,
):
    level = lax.axis_index("level")
    me = lax.axis_index("blk")
    other = 1 - level
    barrier = pltpu.get_barrier_semaphore()

    def start_all(send, recv, n, target):
        for dz, dx, dy in send_order():
            d = dz * 16 + dx * 4 + dy - 1
            pltpu.make_async_remote_copy(
                src_ref=send.at[d],
                dst_ref=recv.at[d],
                send_sem=send_sems.at[n],
                recv_sem=recv_sems.at[n],
                device_id=(target, far[dz] + mid[dx] + near[dy]),
                device_id_type=MESH,
            ).start()

    def whole(send, recv, n):
        return pltpu.make_async_remote_copy(
            src_ref=send,
            dst_ref=recv,
            send_sem=send_sems.at[n],
            recv_sem=recv_sems.at[n],
            device_id=(level, lax.rem(me + 1, devices)),
            device_id_type=MESH,
        )

    def to_pair(source, target, n):
        return pltpu.make_async_remote_copy(
            src_ref=source,
            dst_ref=target,
            send_sem=pair_send.at[n],
            recv_sem=pair_recv.at[n],
            device_id=(other, me),
            device_id_type=MESH,
        )

    def greet(semaphore, peers):
        for peer in peers:
            pl.semaphore_signal(
                semaphore, inc=1, device_id=(level, peer), device_id_type=MESH
            )

    far = [lax.rem(me // 16 + i, 8) * 16 for i in range(8)]
    mid = [lax.rem(me // 4 % 4 + i, 4) * 4 for i in range(4)]
    near = [lax.rem(me % 4 + i, 4) for i in range(4)]
    line = [far[i] + mid[0] + near[0] for i in range(1, 8)]
    plane = [far[0] + mid[i] + near[j] for i in range(4) for j in range(4) if i or j]

    pl.semaphore_signal(barrier, inc=1, device_id=(other, me), device_id_type=MESH)

    @pl.when(level == 0)
    def _():
        greet(barrier, line + plane)

    copy = pltpu.make_async_copy(fluid_hbm, fluid, load_sem)
    copy.start()
    copy.wait()
    make_views(N, V, fluid, perm)

    @pl.when(level == 0)
    def _():
        pl.semaphore_wait(barrier, 23)
        greet(ready, line)
        make_slabs(V, items1)
        pack_slabs(items1, slots, send1)
        pl.semaphore_wait(ready, 7)
        start_all(send1, recv1, 0, 0)

    @pl.when(level == 1)
    def _():
        pl.semaphore_wait(barrier, 1)

        def clear(n, carry):
            for g in range(3):
                items3[n, g] = jnp.zeros((4, 128), F32)
            return carry

        lax.fori_loop(0, 96, clear, 0)

    inner_sweep(V, D)
    make_masks(which, row_mask, lane_mask)

    @pl.when(level == 0)
    def _():
        whole(send1, recv1, 0).wait_recv()
        collect_slabs(recv1, where, which, row_mask, lane_mask, G)

    @pl.when(level == 1)
    def _():
        sibling_ghosts(V, G)
        to_pair(early_out, early_in, 0).wait_recv()
        coarse_ghosts(early_in, G)

    outer_sweep(V, G, D, FC)
    update(N, D)
    make_views(N, V)

    @pl.when(level == 0)
    def _():
        make_rims(V, items2)
        pack_rims(items2, slots, send2)
        parent_layers(lambda f, c, k: G[f, c, 1 - f % 2, k], early_out)
        to_pair(early_out, early_in, 0).start()
        start_all(send2, recv2, 1, 1)
        parent_layers(lambda f, c, k: FC[f, c, k], faces_out)
        to_pair(faces_out, faces_in, 1).start()
        to_pair(mixed_out, mixed_in, 2).wait_recv()
        take_mixed(N, mixed_in)
        whole(send3, recv3, 2).wait_recv()
        apply_corrections(recv3, where, which, row_mask, change, N)

    @pl.when(level == 1)
    def _():
        inner_sweep(V, D)
        sibling_ghosts(V, G)
        to_pair(faces_out, faces_in, 1).wait_recv()
        part_layers(faces_in, change)
        whole(send2, recv2, 1).wait_recv()
        late_rims(recv2, where, which, row_mask, late)
        coarse_ghosts(early_in, G, late)
        edge_faces(V, G, FC)
        restrict_faces(FC, means)
        make_deltas(faces_in, change, means, items3)
        pack_rims(items3, slots, send3)
        start_all(send3, recv3, 2, 0)
        outer_sweep(V, G, D)
        update(N, D)
        restrict_cells(N, mixed_out)
        to_pair(mixed_out, mixed_in, 2).start()

    store_state(N, out)

    @pl.when(level == 0)
    def _():
        whole(send1, recv1, 0).wait_send()
        whole(send2, recv2, 1).wait_send()
        to_pair(early_out, early_in, 0).wait_send()
        to_pair(faces_out, faces_in, 1).wait_send()

    @pl.when(level == 1)
    def _():
        whole(send3, recv3, 2).wait_send()
        to_pair(mixed_out, mixed_in, 2).wait_send()


def place_kernel(back, source, out, sems):
    copies = [
        pltpu.make_async_copy(source.at[back[b]], out.at[0, b], sems.at[b])
        for b in range(out.shape[1])
    ]
    for copy in copies:
        copy.start()
    for copy in copies:
        copy.wait()


def tables(neighbours, parents, level, me, count, devices):
    rows = lax.dynamic_slice_in_dim(neighbours, me * count, count, 0)
    family = lax.dynamic_slice_in_dim(parents, me * count, count, 0)
    ids = jnp.arange(count, dtype=jnp.int32)
    owner = family[:, 0] - me * count
    owns = owner[:, None] == ids[None, :]
    is_parent = jnp.any(owns, axis=0)
    earlier = ids[None, :] < ids[:, None]
    parent_rank = jnp.sum(is_parent[None, :] & earlier, axis=1, dtype=jnp.int32)
    rest_rank = ids - parent_rank
    coarse_place = jnp.where(
        is_parent, 8 * parent_rank, jnp.where(rest_rank < 7, 1 + rest_rank, 2 + rest_rank)
    )
    fine_place = 8 * jnp.sum(jnp.where(owns, parent_rank[None, :], 0), axis=1) + family[:, 1]
    place = jnp.where(level == 0, coarse_place, fine_place).astype(jnp.int32)

    def inverse(position):
        return jnp.sum(
            jnp.where(position[None, :] == ids[:, None], ids[None, :], 0), axis=1, dtype=jnp.int32
        )

    coarse_perm = inverse(coarse_place)
    chosen = coarse_perm[:, None] == ids[None, :]
    ordered = jnp.sum(jnp.where(chosen[:, :, None], rows[None], 0), axis=1, dtype=jnp.int32)
    ordered = ordered.T.reshape(-1)
    faces = jnp.repeat(jnp.arange(6, dtype=jnp.int32), count)
    target = ordered // count
    own_id = jnp.tile(coarse_perm, 6) * 6 + faces
    their_id = ordered % count * 6 + faces + 1 - 2 * (faces % 2)
    key = jnp.where(me < target, own_id, their_id)
    which = jnp.sum(
        (target[:, None] == target[None, :]) & (key[None, :] < key[:, None]),
        axis=1,
        dtype=jnp.int32,
    )
    far, mid, near = target // 16 - me // 16, target // 4 % 4 - me // 4 % 4, target % 4 - me % 4
    to = (far % 8) * 16 + (mid % 4) * 4 + near % 4 - 1
    come = (-far % 8) * 16 + (-mid % 4) * 4 + (-near) % 4 - 1
    item_ids = jnp.arange(6 * count, dtype=jnp.int32)
    slot_ids = jnp.arange(2 * devices, dtype=jnp.int32)
    slots = jnp.sum(
        jnp.where((2 * to + which)[None, :] == slot_ids[:, None], item_ids[None, :], 0),
        axis=1,
        dtype=jnp.int32,
    )
    return inverse(place), place, slots, come, which


def local(fluid_state, neighbours, parents):
    level = lax.axis_index("level")
    me = lax.axis_index("blk")
    devices = lax.axis_size("blk")
    count = fluid_state.shape[1]
    perm, place, slots, where, which = tables(
        neighbours, parents, level, me, count, devices
    )
    smem = pl.BlockSpec(memory_space=pltpu.SMEM)
    vmem = pl.BlockSpec(memory_space=pltpu.VMEM)
    peers = devices - 1

    def step(*refs):
        step_kernel(devices, *refs)

    result = pl.pallas_call(
        step,
        out_shape=jax.ShapeDtypeStruct(fluid_state.shape[1:], F32),
        in_specs=[smem] * 4 + [pl.BlockSpec(memory_space=pltpu.HBM)],
        out_specs=vmem,
        scratch_shapes=[
            pltpu.VMEM((16, 5, 2, 2, 8, 128), F32),
            pltpu.VMEM((3, 5, 16, 4, 8, 128), F32),
            pltpu.VMEM((3, 5, 16, 4, 8, 128), F32),
            pltpu.VMEM((6, 5, 2, 4, 8, 128), F32),
            pltpu.VMEM((6, 5, 4, 8, 128), F32),
            pltpu.VMEM((4, 5, 4, 8, 128), F32),
            pltpu.VMEM((96, 3, 8, 128), F32),
            pltpu.VMEM((96, 3, 4, 128), F32),
            pltpu.VMEM((96, 3, 4, 128), F32),
            pltpu.VMEM((peers, 5, 8, 128), F32),
            pltpu.VMEM((peers, 5, 8, 128), F32),
            pltpu.VMEM((peers, 5, 4, 128), F32),
            pltpu.VMEM((peers, 5, 4, 128), F32),
            pltpu.VMEM((peers, 5, 4, 128), F32),
            pltpu.VMEM((peers, 5, 4, 128), F32),
            pltpu.VMEM((25, 8, 128), F32),
            pltpu.VMEM((25, 8, 128), F32),
            pltpu.VMEM((25, 8, 128), F32),
            pltpu.VMEM((25, 8, 128), F32),
            pltpu.VMEM((2, 5, 2, 2, 8, 128), F32),
            pltpu.VMEM((2, 5, 2, 2, 8, 128), F32),
            pltpu.VMEM((25, 8, 128), F32),
            pltpu.VMEM((25, 8, 128), F32),
            pltpu.SemaphoreType.DMA((3,)),
            pltpu.SemaphoreType.DMA((3,)),
            pltpu.SemaphoreType.DMA((3,)),
            pltpu.SemaphoreType.DMA((3,)),
            pltpu.SemaphoreType.REGULAR,
            pltpu.VMEM((14, 8, 128), F32),
            pltpu.VMEM((4, 8, 128), F32),
            pltpu.VMEM(fluid_state.shape, F32),
            pltpu.SemaphoreType.DMA,
        ],
        compiler_params=pltpu.CompilerParams(
            collective_id=0, has_side_effects=True, vmem_limit_bytes=34 * 1024 * 1024
        ),
    )(perm, slots, where, which, fluid_state)
    return pl.pallas_call(
        place_kernel,
        out_shape=jax.ShapeDtypeStruct(fluid_state.shape, F32),
        in_specs=[smem, vmem],
        out_specs=pl.BlockSpec(memory_space=pl.ANY),
        scratch_shapes=[pltpu.SemaphoreType.DMA((count,))],
        compiler_params=pltpu.CompilerParams(vmem_limit_bytes=8 * 1024 * 1024),
    )(place, result)


def solution(mesh):
    return jax.shard_map(
        local,
        mesh=mesh,
        in_specs=(P("level", "blk", None, None, None), P(), P()),
        out_specs=P("level", "blk", None, None, None),
        check_vma=False,
    )
```

```python
import jax
import jax.numpy as jnp
from jax import lax
from jax.experimental import pallas as pl
from jax.experimental.pallas import tpu as pltpu
from jax.sharding import PartitionSpec as P

GAMMA = 1.4
RATIO = 0.12
MESH = pl.DeviceIdType.MESH
ORDER = ((0, 1, 2, 3, 4), (0, 2, 1, 3, 4), (0, 3, 1, 2, 4))
BIT_OF = (4, 2, 1)
TANGENT = ((2, 1), (1, 4), (2, 4))
F32 = jnp.float32


def send_order():
    offsets = [(z, x, y) for z in range(8) for x in range(4) for y in range(4)][1:]
    mixed = [offsets[(53 * k + 26) % 127] for k in range(127)]
    return sorted(mixed, key=lambda o: -(min(o[0], 8 - o[0]) + min(o[1], 4 - o[1]) + min(o[2], 4 - o[2])))


def iota(axis):
    return lax.broadcasted_iota(jnp.int32, (8, 128), axis)


def in_one(count, first, second):
    lax.fori_loop(0, count, lambda n, carry: second(n, first(n, carry)), 0)


def take(tile, index):
    return jnp.take_along_axis(tile, index, axis=1, mode="promise_in_bounds")


def flip8(tiles):
    return jnp.swapaxes(jnp.stack(tiles), 0, 1)


def turn(tiles):
    whole = jnp.concatenate(tiles, axis=0).T
    return [whole[8 * i : 8 * i + 8] for i in range(16)]


def halves(tile):
    lane = iota(1)
    other = pltpu.roll(tile, 64, 1)
    return jnp.where(lane < 64, tile, other), jnp.where(lane < 64, other, tile)


def join(low, high, second):
    lane = iota(1)
    low = jnp.where(second, pltpu.roll(low, 64, 1), low)
    high = jnp.where(second, high, pltpu.roll(high, 64, 1))
    return jnp.where(lane < 64, low, high)


def prim(q):
    inverse = 1.0 / q[0]
    speed = q[1] * inverse
    kinetic = (q[1] * q[1] + q[2] * q[2] + q[3] * q[3]) * inverse
    return inverse, speed, (GAMMA - 1.0) * (q[4] - 0.5 * kinetic)


def flux_of(q, speed, pressure):
    return [q[1], q[1] * speed + pressure, q[2] * speed, q[3] * speed, (q[4] + pressure) * speed]


def half_step(below, here, above, low_wanted=True, high_wanted=True):
    low, high = [], []
    for u0, u1, u2 in zip(below, here, above):
        a = u1 - u0
        b = u2 - u1
        slope = jnp.maximum(jnp.minimum(a, b), 0.0) + jnp.minimum(jnp.maximum(a, b), 0.0)
        low.append(u1 - 0.5 * slope)
        high.append(u1 + 0.5 * slope)
    _, speed, pressure = prim(low)
    flux_low = flux_of(low, speed, pressure)
    _, speed, pressure = prim(high)
    flux_high = flux_of(high, speed, pressure)
    change = [0.5 * RATIO * (a - b) for a, b in zip(flux_low, flux_high)]
    low = [a + b for a, b in zip(low, change)] if low_wanted else None
    high = [a + b for a, b in zip(high, change)] if high_wanted else None
    return low, high


def with_sound(q):
    inverse, speed, pressure = prim(q)
    return q, inverse, speed, pressure, jnp.sqrt(GAMMA * pressure * inverse)


def contact_flux(low, high):
    ql, il, ul, pl_, cl = with_sound(low)
    qh, ih, uh, ph, ch = with_sound(high)
    slowest = jnp.minimum(ul - cl, uh - ch)
    fastest = jnp.maximum(ul + cl, uh + ch)
    mass_l = ql[0] * (slowest - ul)
    mass_h = qh[0] * (fastest - uh)
    contact = (ph - pl_ + ul * mass_l - uh * mass_h) / (mass_l - mass_h)
    lower = jnp.logical_or(slowest >= 0.0, contact >= 0.0)
    q = [jnp.where(lower, a, b) for a, b in zip(ql, qh)]
    inverse = jnp.where(lower, il, ih)
    speed = jnp.where(lower, ul, uh)
    pressure = jnp.where(lower, pl_, ph)
    mass = jnp.where(lower, mass_l, mass_h)
    wave = jnp.where(lower, slowest, fastest)
    outside = jnp.logical_or(slowest >= 0.0, jnp.logical_and(contact < 0.0, fastest <= 0.0))
    flux = flux_of(q, speed, pressure)
    over = 1.0 / (wave - contact)
    factor = mass * over
    scaled = factor * inverse
    gap = contact - speed
    star = [
        factor,
        factor * contact,
        scaled * q[2],
        scaled * q[3],
        scaled * q[4] + gap * (factor * contact + pressure * over),
    ]
    return [jnp.where(outside, f, f + wave * (s - u)) for f, s, u in zip(flux, star, q)]


def cells(V, a, i, ch):
    return [V[a, c, i, ch] for c in range(5)]


def ghost(G, a, s, layer, ch):
    return [G[2 * a + s, c, layer, ch] for c in range(5)]


def inner_sweep(V, D):
    def body(n, carry):
        a = n // 4
        ch = n % 4
        states = [cells(V, a, i, ch) for i in range(3)]
        _, high = half_step(*states)
        previous = None
        for i in range(2, 15):
            states = [states[1], states[2], cells(V, a, i + 1, ch)]
            low, next_high = half_step(*states)
            flux = contact_flux(high, low)
            for c in range(5):
                D[a, c, i - 1, ch] = flux[c] if previous is None else flux[c] - previous[c]
            high, previous = next_high, flux
        for c in range(5):
            D[a, c, 14, ch] = -previous[c]
        return carry

    lax.fori_loop(0, 12, body, 0)


def outer_sweep(V, G, D, FC=None):
    def body(n, carry):
        a = n // 4
        ch = n % 4
        u = [cells(V, a, i, ch) for i in range(3)]
        g = [ghost(G, a, 0, layer, ch) for layer in range(2)]
        _, r_ghost = half_step(g[0], g[1], u[0], low_wanted=False)
        l0, r0 = half_step(g[1], u[0], u[1])
        l1, _ = half_step(u[0], u[1], u[2], high_wanted=False)
        f0 = contact_flux(r_ghost, l0)
        f1 = contact_flux(r0, l1)
        for c in range(5):
            D[a, c, 0, ch] = f1[c] - f0[c]
            D[a, c, 1, ch] = D[a, c, 1, ch] - f1[c]
            if FC is not None:
                FC[2 * a, c, ch] = f0[c]
        u = [cells(V, a, i, ch) for i in (13, 14, 15)]
        g = [ghost(G, a, 1, layer, ch) for layer in range(2)]
        _, r0 = half_step(u[0], u[1], u[2], low_wanted=False)
        l1, r1 = half_step(u[1], u[2], g[0])
        l2, _ = half_step(u[2], g[0], g[1], high_wanted=False)
        f0 = contact_flux(r0, l1)
        f1 = contact_flux(r1, l2)
        for c in range(5):
            D[a, c, 14, ch] = D[a, c, 14, ch] + f0[c]
            D[a, c, 15, ch] = f1[c] - f0[c]
            if FC is not None:
                FC[2 * a + 1, c, ch] = f1[c]
        return carry

    lax.fori_loop(0, 12, body, 0)


def edge_faces(V, G, FC):
    def body(n, carry):
        a = n // 4
        ch = n % 4
        u = [cells(V, a, i, ch) for i in range(2)]
        g = [ghost(G, a, 0, layer, ch) for layer in range(2)]
        _, high = half_step(g[0], g[1], u[0], low_wanted=False)
        low, _ = half_step(g[1], u[0], u[1], high_wanted=False)
        first = contact_flux(high, low)
        u = [cells(V, a, i, ch) for i in (14, 15)]
        g = [ghost(G, a, 1, layer, ch) for layer in range(2)]
        _, high = half_step(u[0], u[1], g[0], low_wanted=False)
        low, _ = half_step(u[1], g[0], g[1], high_wanted=False)
        last = contact_flux(high, low)
        for c in range(5):
            FC[2 * a, c, ch] = FC[2 * a, c, ch] + first[c]
            FC[2 * a + 1, c, ch] = FC[2 * a + 1, c, ch] + last[c]
        return carry

    lax.fori_loop(0, 12, body, 0)


def update(N, D, V=None):
    def body(n, carry):
        X = n // 2
        h = n % 2
        for c in range(5):
            c1, c2 = ORDER[1].index(c), ORDER[2].index(c)
            tiles = [None] * 16
            for z in range(2):
                rows = flip8([D[2, c2, 8 * z + i, 2 * h + X] for i in range(8)])
                for y in range(8):
                    tiles[2 * y + z] = D[1, c1, 8 * h + y, 2 * z + X] + rows[y]
            tiles = turn(tiles)
            for t in range(2):
                rows = flip8([D[0, c, 8 * X + i, 2 * h + t] for i in range(8)])
                for j in range(8):
                    q = 8 * t + j
                    tiles[q] = N[q, c, X, h] - RATIO * (tiles[q] + rows[j])
                    N[q, c, X, h] = tiles[q]
            if V is not None:
                view_tiles(tiles, V, c, X, h)
        return carry

    lax.fori_loop(0, 4, body, 0)


def view_tiles(tiles, V, c, X, h):
    c1, c2 = ORDER[1].index(c), ORDER[2].index(c)
    for t in range(2):
        rows = flip8(tiles[8 * t : 8 * t + 8])
        for i in range(8):
            V[0, c, 8 * X + i, 2 * h + t] = rows[i]
    tiles = turn(tiles)
    for z in range(2):
        for y in range(8):
            V[1, c1, 8 * h + y, 2 * z + X] = tiles[2 * y + z]
        rows = flip8([tiles[2 * y + z] for y in range(8)])
        for i in range(8):
            V[2, c2, 8 * z + i, 2 * h + X] = rows[i]


def load_views(N, V, fluid, perm):
    def body(n, carry):
        X = n // 2
        h = n % 2
        rows = pl.ds(pl.multiple_of(8 * X, 8), 8)
        lanes = pl.ds(pl.multiple_of(128 * h, 128), 128)
        for c in range(5):
            tiles = [fluid[0, perm[q], c, rows, lanes] for q in range(16)]
            for q in range(16):
                N[q, c, X, h] = tiles[q]
            view_tiles(tiles, V, c, X, h)
        return carry

    lax.fori_loop(0, 4, body, 0)


def store_state(N, out):
    def body(q, carry):
        for c in range(5):
            for X in range(2):
                for h in range(2):
                    out[q, c, 8 * X : 8 * X + 8, 128 * h : 128 * h + 128] = N[q, c, X, h]
        return carry

    lax.fori_loop(0, 16, body, 0)


def make_slabs(V, items):
    def x_body(n, carry):
        s = n // 2
        t = n % 2
        codes = [
            [V[0, c, 14 * s + layer, 2 * h + t] for layer in range(2) for h in range(2)]
            for c in range(5)
        ]
        last = [half for tile in codes[4] for half in halves(tile)]
        for g, tiles in enumerate((codes[0] + codes[1], codes[2] + codes[3], last)):
            rows = flip8(tiles)
            for j in range(8):
                items[s * 16 + 8 * t + j, g] = rows[j]
        return carry

    def body(n, carry):
        a = 1 + n // 2
        s = n % 2
        codes = [
            [V[a, c, 14 * s + layer, k] for layer in range(2) for k in range(4)] for c in range(5)
        ]
        for g, tiles in enumerate((codes[0] + codes[1], codes[2] + codes[3], codes[4] * 2)):
            tiles = turn(tiles)
            for q in range(16):
                items[(2 + n) * 16 + q, g] = tiles[q]
        return carry

    in_one(4, x_body, body)


def squeeze(tiles):
    group = iota(1) // 32
    rows = flip8(tiles)
    pair = []
    for r in range(2):
        row = rows[4 * r]
        for g in range(1, 4):
            row = jnp.where(group == g, rows[4 * r + g], row)
        pair.append(row)
    return flip8(pair * 4)


def unsqueeze(tiles, second):
    rows = flip8([jnp.concatenate([tile, tile], axis=0) for tile in tiles])
    pair = [jnp.where(second, rows[2 + r], rows[r]) for r in range(2)]
    return flip8([pair[0]] * 4 + [pair[1]] * 4)


def last_tiles(tiles):
    lane = iota(1)
    result = tiles[0:4]
    for g in range(1, 4):
        result = [jnp.where(lane % 4 == g, tiles[4 * g + m], result[m]) for m in range(4)]
    return result


def make_rims(V, items):
    def x_body(n, carry):
        s = n // 2
        t = n % 2
        codes = [V[0, c, 15 * s, 2 * h + t] for c in range(5) for h in range(2)]
        rows = flip8(codes[:8])
        last = flip8(codes[8:] * 4)
        for j in range(8):
            item = s * 16 + 8 * t + j
            items[item, 0] = rows[j, 0:4]
            items[item, 1] = rows[j, 4:8]
            items[item, 2] = last[j, 0:4]
        return carry

    def body(n, carry):
        a = 1 + n // 2
        s = n % 2
        codes = [[V[a, c, 15 * s, k] for k in range(4)] for c in range(5)]
        store_rims(items, (2 + n) * 16, codes, range(16))
        return carry

    in_one(4, x_body, body)


def store_rims(items, first, codes, blocks):
    tiles = turn(codes[0] + codes[1] + codes[2] + codes[3])
    last = turn(codes[4] * 4)
    for t in range(2):
        pairs = squeeze(last[8 * t : 8 * t + 8])
        for j in range(8):
            q = 8 * t + j
            if q in blocks:
                items[first + q, 0] = tiles[q][0:4]
                items[first + q, 1] = tiles[q][4:8]
                items[first + q, 2] = pairs[j, 0:4]


def rim_tile(recv, e, k):
    return jnp.concatenate([recv[e, 2 * k], recv[e, 2 * k + 1]], axis=0)


def pack_all(one, count):
    def body(n, carry):
        for i in range(4):
            one(4 * n + i)
        return carry

    lax.fori_loop(0, count // 4, body, 0)
    for d in range(count // 4 * 4, count):
        one(d)


def pack_slabs(items, slots, send):
    def one(d):
        lane = iota(1)
        i0 = slots[2 * d]
        i1 = slots[2 * d + 1]
        for g in range(2):
            send[d, g] = items[i0, g]
            send[d, 2 + g] = items[i1, g]
        send[d, 4] = jnp.where(lane < 64, items[i0, 2], items[i1, 2])

    pack_all(one, send.shape[0])


def pack_rims(items, slots, send):
    def one(d):
        first = lax.broadcasted_iota(jnp.int32, (4, 128), 0) < 2
        i0 = slots[2 * d]
        i1 = slots[2 * d + 1]
        for g in range(2):
            send[d, g] = items[i0, g]
            send[d, 2 + g] = items[i1, g]
        send[d, 4] = jnp.where(first, items[i0, 2], items[i1, 2])

    pack_all(one, send.shape[0])


def collect_slabs(recv, where, which, row_mask, lane_mask, G):
    def x_body(n, carry):
        s = n // 2
        t = n % 2
        second = row_mask[n] > 0.5
        first = s * 16 + 8 * t
        for g in range(2):
            rows = flip8([recv[where[first + j], 2 * which[first + j] + g] for j in range(8)])
            for m in range(8):
                c, layer, h = 2 * g + m // 4, m // 2 % 2, m % 2
                G[s, c, layer, 2 * h + t] = rows[m]
        rows = flip8([recv[where[first + j], 4] for j in range(8)])
        for layer in range(2):
            for h in range(2):
                m = 2 * layer + h
                G[s, 4, layer, 2 * h + t] = join(rows[2 * m], rows[2 * m + 1], second)
        return carry

    def body(n, carry):
        second = lane_mask[n] > 0.5
        first = (2 + n) * 16
        for g in range(2):
            tiles = turn([recv[where[first + q], 2 * which[first + q] + g] for q in range(16)])
            for m in range(16):
                G[2 + n, 2 * g + m // 8, m // 4 % 2, m % 4] = tiles[m]
        tiles = turn([recv[where[first + q], 4] for q in range(16)])
        for m in range(8):
            G[2 + n, 4, m // 4, m % 4] = jnp.where(second, tiles[8 + m], tiles[m])
        return carry

    in_one(4, x_body, body)


def make_masks(which, row_mask, lane_mask):
    def value(item):
        return which[item].astype(F32)

    def row_body(n, carry):
        mask = jnp.zeros((8, 128), F32)
        for j in range(8):
            mask = jnp.where(iota(0) == j, value(8 * n + j), mask)
        row_mask[n] = mask
        return carry

    def lane_body(n, carry):
        mask = jnp.zeros((8, 128), F32)
        for q in range(16):
            mask = jnp.where(iota(1) // 8 == q, value((2 + n) * 16 + q), mask)
        lane_mask[n] = mask
        return carry

    lax.fori_loop(0, 12, row_body, 0)
    lax.fori_loop(0, 4, lane_body, 0)
    for t in range(2):
        mask = jnp.zeros((8, 128), F32)
        for j in range(8):
            mask = jnp.where(iota(0) == j, value((2 + j % 4) * 16 + 8 * t), mask)
        row_mask[12 + t] = mask


def parent_layers(read, out):
    face = iota(1) // 8 % 8

    def body(c, carry):
        for k in range(4):
            tile = read(2, c, k)
            for n in range(1, 4):
                tile = jnp.where(face == n, pltpu.roll(read(2 + n, c, k), 8 * n, 1), tile)
            out[4 * c + k] = tile
        for f in range(2):
            for t in range(2):
                for h in range(2):
                    r = 4 * f + 2 * t + h
                    out[20 + c, r : r + 1, :] = read(f, c, 2 * h + t)[0:1]
        return carry

    lax.fori_loop(0, 5, body, 0)


def part_layers(layers, out):
    def body(c, carry):
        for n in range(4):
            for k in range(4):
                out[n, c, k] = pltpu.roll(layers[4 * c + k], (128 - 8 * n) % 128, 1)
        return carry

    lax.fori_loop(0, 5, body, 0)


def late_rims(recv, where, which, row_mask, rims):
    for f in range(2):
        for t in range(2):
            item = f * 16 + 8 * t
            r = 4 * f + 2 * t
            tile = rim_tile(recv, where[item], which[item])
            for c in range(4):
                rims[20 + c, r : r + 2, :] = tile[2 * c : 2 * c + 2]
            tile = recv[where[item], 4]
            rims[24, r : r + 2, :] = jnp.where(which[item] == 1, tile[2:4], tile[0:2])
    items = [f * 16 + 8 * t for t in range(2) for _ in range(2) for f in range(2, 6)]
    tiles = turn([rim_tile(recv, where[i], which[i]) for i in items])
    for m in range(16):
        rims[m] = tiles[m]
    tiles = []
    for t in range(2):
        rows = unsqueeze(
            [recv[where[i], 4] for i in items[8 * t : 8 * t + 8]], row_mask[12 + t] > 0.5
        )
        tiles += [rows[j] for j in range(8)]
    tiles = last_tiles(turn(tiles))
    for m in range(4):
        rims[16 + m] = tiles[m]


def spread_rows(tile, u):
    sub = iota(0)
    result = pltpu.roll(tile, 4, 0) if u else tile
    base = result
    for r in range(1, 5):
        result = jnp.where((sub + 1) // 2 == r, pltpu.roll(base, r, 0), result)
    return result


def sibling_ghosts(V, G):
    def x_body(c, carry):
        for f in range(2):
            for layer in range(2):
                for k in range(4):
                    near = V[0, c, (layer if f else 14 + layer), k]
                    G[f, c, layer, k] = pltpu.roll(near, 4, 0)
        return carry

    def body(c, carry):
        for f in range(2, 6):
            a, s = f // 2, f % 2
            by = (128 - 8 * BIT_OF[a]) if s else 8 * BIT_OF[a]
            for layer in range(2):
                for k in range(4):
                    near = V[a, c, (layer if s else 14 + layer), k]
                    G[f, c, layer, k] = pltpu.roll(near, by, 1)
        return carry

    in_one(5, x_body, body)


def coarse_ghosts(rims, G, late=None):
    lane = iota(1)
    sub = iota(0)

    def rim(*index):
        value = rims[index]
        return value if late is None else 0.5 * (value + late[index])

    def x_body(c, carry):
        first = (sub // 2) % 2 == 1
        second = sub % 2
        for f in range(2):
            outer = (sub // 4) % 2 == f
            for t in range(2):
                r = 4 * f + 2 * t
                row = [
                    jnp.broadcast_to(rim(20 + c, pl.ds(r + h, 1), slice(None)), (8, 128))
                    for h in range(2)
                ]
                source = jnp.where(first, row[1], row[0])
                for h in range(2):
                    index = (4 * h + lane // 32) * 16 + 8 * second + (lane % 16) // 2
                    coarse = take(source, index)
                    for layer in range(2):
                        k = 2 * h + t
                        G[f, c, layer, k] = jnp.where(outer, coarse, G[f, c, layer, k])
        return carry

    octant = lane // 8 % 8

    def body(c, carry):
        source = [rim(4 * c + k) for k in range(4)]
        second = octant // 4 == 1
        for f in range(2, 6):
            a, s = f // 2, f % 2
            outer = octant // BIT_OF[a] % 2 == s
            first = octant // TANGENT[a][0] % 2 == 1
            for X in range(2):
                index = (lane // 64 * 8 + f - 2) * 8 + 4 * X + lane % 8 // 2
                four = [take(tile, index) for tile in source]
                low = jnp.where(second, four[1], four[0])
                high = jnp.where(second, four[3], four[2])
                chosen = jnp.where(first, high, low)
                for u in range(2):
                    coarse = spread_rows(chosen, u)
                    for layer in range(2):
                        k = 2 * u + X
                        G[f, c, layer, k] = jnp.where(outer, coarse, G[f, c, layer, k])
        return carry

    in_one(5, x_body, body)


def lane_pairs(low, high):
    even = iota(1) % 2 == 0
    return jnp.where(even, low + pltpu.roll(low, 127, 1), high + pltpu.roll(high, 1, 1))


def pair_sums(low, high):
    lane = iota(1)
    index = (lane // 16 % 4) * 32 + 2 * (lane % 8) + lane // 64
    pairs = lane_pairs(low, high)
    merged = take(pairs + pltpu.roll(pairs, 112, 1), index)
    return jnp.where(lane % 16 < 8, merged, pltpu.roll(merged, 7, 0))


def restrict_cells(N, mixed):
    def body(n, carry):
        t = n % 2
        c = n // 2
        merged = []
        for X in range(2):
            rows = [flip8([N[8 * t + j, c, X, h] for j in range(8)]) for h in range(2)]
            for x in range(4):
                low, high = [rows[h][2 * x] + rows[h][2 * x + 1] for h in range(2)]
                merged.append(pair_sums(low, high) * 0.125)
        rows = flip8(merged)
        for X in range(2):
            for h in range(2):
                mixed[t, c, X, h] = rows[4 * X + 2 * h]
        return carry

    lax.fori_loop(0, 10, body, 0)


def restrict_faces(FC, means):
    lane = iota(1)
    sub = iota(0)

    def body(c, carry):
        index = lane // 8 * 8 + 2 * (lane % 4) + lane // 4 % 2
        for n in range(4):
            result = None
            for u in range(2):
                pairs = lane_pairs(FC[2 + n, c, 2 * u], FC[2 + n, c, 2 * u + 1])
                merged = take(pairs + pltpu.roll(pairs, 7, 0), index)
                for i in range(4):
                    moved = pltpu.roll(merged, ((4 if u else 8) - i) % 8, 0)
                    result = moved if result is None else jnp.where(sub == 4 * u + i, moved, result)
            means[5 * n + c] = result * 0.125
        for f in range(2):
            for t in range(2):
                merged = pair_sums(FC[f, c, t], FC[f, c, 2 + t]) * 0.125
                for h in range(2):
                    o = 4 * f + 2 * h
                    r = 4 * f + 2 * t + h
                    means[20 + c, r : r + 1, :] = merged[o : o + 1]
        return carry

    lax.fori_loop(0, 5, body, 0)


def make_deltas(layers, parted, means, items):
    for f in range(2):
        for t in range(2):
            item = f * 16 + 8 * t
            for c in range(5):
                for h in range(2):
                    r = 4 * f + 2 * t + h
                    delta = layers[20 + c, r : r + 1, :] - means[20 + c, r : r + 1, :]
                    if c < 4:
                        row = 2 * (c % 2) + h
                        items[item, c // 2, row : row + 1, :] = delta
                    else:
                        items[item, 2, h : h + 1, :] = delta
                        items[item, 2, 2 + h : 3 + h, :] = delta
    for n in range(4):
        a, s = 1 + n // 2, n % 2
        codes = []
        for c in range(5):
            fine = means[5 * n + c]
            codes.append([])
            for k in range(4):
                o = s * BIT_OF[a] + (k // 2) * TANGENT[a][0] + (k % 2) * 4
                moved = pltpu.roll(fine, (128 - 8 * o) % 128, 1)
                codes[c].append(parted[n, c, k] - moved)
        store_rims(items, (2 + n) * 16, codes, (0, 8))


def take_mixed(N, mixed):
    def body(c, carry):
        for t in range(2):
            for X in range(2):
                for h in range(2):
                    N[8 * t, c, X, h] = mixed[t, c, X, h]
        return carry

    lax.fori_loop(0, 5, body, 0)


def apply_corrections(recv, where, which, row_mask, change, N):
    sub = iota(0)

    def x_body(q, carry):
        for s in range(2):
            scale = RATIO if s else -RATIO
            item = s * 16 + q
            e = where[item]
            k = which[item]
            tile = recv[e, 4]
            last = jnp.where(k == 1, tile[2:4], tile[0:2])
            tile = rim_tile(recv, e, k)
            for c in range(5):
                for h in range(2):
                    row = tile[2 * c + h : 2 * c + h + 1] if c < 4 else last[h : h + 1]
                    row = jnp.broadcast_to(scale * row, (8, 128))
                    N[q, c, s, h] = N[q, c, s, h] + jnp.where(sub == 7 * s, row, 0.0)
        return carry

    lax.fori_loop(0, 16, x_body, 0)

    for n in range(4):
        scale = RATIO if n % 2 else -RATIO
        first = (2 + n) * 16
        tiles = turn([rim_tile(recv, where[first + q], which[first + q]) for q in range(16)])
        for m in range(16):
            change[n, m // 4, m % 4] = scale * tiles[m]
        tiles = []
        for t in range(2):
            rows = unsqueeze(
                [recv[where[first + 8 * t + j], 4] for j in range(8)],
                row_mask[4 + 2 * n + t] > 0.5,
            )
            tiles += [rows[j] for j in range(8)]
        tiles = last_tiles(turn(tiles))
        for m in range(4):
            change[n, 4, m] = scale * tiles[m]

    def body(X, carry):
        for c in range(5):
            c1, c2 = ORDER[1].index(c), ORDER[2].index(c)
            for h in range(2):
                tiles = []
                for y in range(8):
                    for z in range(2):
                        row = jnp.broadcast_to(
                            change[2 + z, c2, 2 * h + X, y : y + 1, :], (8, 128)
                        )
                        tile = jnp.where(sub == 7 * z, row, 0.0)
                        if y == 7 * h:
                            tile = tile + change[h, c1, 2 * z + X]
                        tiles.append(tile)
                tiles = turn(tiles)
                for q in range(16):
                    N[q, c, X, h] = N[q, c, X, h] + tiles[q]
        return carry

    lax.fori_loop(0, 2, body, 0)


def step_kernel(
    devices,
    perm,
    slots,
    where,
    which,
    fluid,
    out,
    N,
    V,
    D,
    G,
    FC,
    change,
    items1,
    items2,
    items3,
    send1,
    recv1,
    send2,
    recv2,
    send3,
    recv3,
    early_out,
    early_in,
    faces_out,
    faces_in,
    mixed_out,
    mixed_in,
    late,
    means,
    send_sems,
    recv_sems,
    pair_send,
    pair_recv,
    ready,
    row_mask,
    lane_mask,
):
    level = lax.axis_index("level")
    me = lax.axis_index("blk")
    other = 1 - level
    barrier = pltpu.get_barrier_semaphore()

    def start_all(send, recv, n, target):
        for dz, dx, dy in send_order():
            d = dz * 16 + dx * 4 + dy - 1
            pltpu.make_async_remote_copy(
                src_ref=send.at[d],
                dst_ref=recv.at[d],
                send_sem=send_sems.at[n],
                recv_sem=recv_sems.at[n],
                device_id=(target, far[dz] + mid[dx] + near[dy]),
                device_id_type=MESH,
            ).start()

    def whole(send, recv, n):
        return pltpu.make_async_remote_copy(
            src_ref=send,
            dst_ref=recv,
            send_sem=send_sems.at[n],
            recv_sem=recv_sems.at[n],
            device_id=(level, lax.rem(me + 1, devices)),
            device_id_type=MESH,
        )

    def to_pair(source, target, n):
        return pltpu.make_async_remote_copy(
            src_ref=source,
            dst_ref=target,
            send_sem=pair_send.at[n],
            recv_sem=pair_recv.at[n],
            device_id=(other, me),
            device_id_type=MESH,
        )

    def greet(semaphore, peers):
        for peer in peers:
            pl.semaphore_signal(
                semaphore, inc=1, device_id=(level, peer), device_id_type=MESH
            )

    far = [lax.rem(me // 16 + i, 8) * 16 for i in range(8)]
    mid = [lax.rem(me // 4 % 4 + i, 4) * 4 for i in range(4)]
    near = [lax.rem(me % 4 + i, 4) for i in range(4)]
    line = [far[i] + mid[0] + near[0] for i in range(1, 8)]
    plane = [far[0] + mid[i] + near[j] for i in range(4) for j in range(4) if i or j]

    pl.semaphore_signal(barrier, inc=1, device_id=(other, me), device_id_type=MESH)

    @pl.when(level == 0)
    def _():
        greet(barrier, line + plane)

    load_views(N, V, fluid, perm)

    @pl.when(level == 0)
    def _():
        pl.semaphore_wait(barrier, 23)
        greet(ready, line)
        make_slabs(V, items1)
        pack_slabs(items1, slots, send1)
        pl.semaphore_wait(ready, 7)
        start_all(send1, recv1, 0, 0)

    @pl.when(level == 1)
    def _():
        pl.semaphore_wait(barrier, 1)

        def clear(n, carry):
            for g in range(3):
                items3[n, g] = jnp.zeros((4, 128), F32)
            return carry

        lax.fori_loop(0, 96, clear, 0)

    inner_sweep(V, D)
    make_masks(which, row_mask, lane_mask)

    @pl.when(level == 0)
    def _():
        whole(send1, recv1, 0).wait_recv()
        collect_slabs(recv1, where, which, row_mask, lane_mask, G)

    @pl.when(level == 1)
    def _():
        sibling_ghosts(V, G)
        to_pair(early_out, early_in, 0).wait_recv()
        coarse_ghosts(early_in, G)

    outer_sweep(V, G, D, FC)
    update(N, D, V)

    @pl.when(level == 0)
    def _():
        make_rims(V, items2)
        pack_rims(items2, slots, send2)
        start_all(send2, recv2, 1, 1)
        parent_layers(lambda f, c, k: G[f, c, 1 - f % 2, k], early_out)
        to_pair(early_out, early_in, 0).start()
        parent_layers(lambda f, c, k: FC[f, c, k], faces_out)
        to_pair(faces_out, faces_in, 1).start()
        to_pair(mixed_out, mixed_in, 2).wait_recv()
        take_mixed(N, mixed_in)
        whole(send3, recv3, 2).wait_recv()
        apply_corrections(recv3, where, which, row_mask, change, N)

    @pl.when(level == 1)
    def _():
        inner_sweep(V, D)
        sibling_ghosts(V, G)
        to_pair(faces_out, faces_in, 1).wait_recv()
        part_layers(faces_in, change)
        whole(send2, recv2, 1).wait_recv()
        late_rims(recv2, where, which, row_mask, late)
        coarse_ghosts(early_in, G, late)
        edge_faces(V, G, FC)
        restrict_faces(FC, means)
        make_deltas(faces_in, change, means, items3)
        pack_rims(items3, slots, send3)
        start_all(send3, recv3, 2, 0)
        outer_sweep(V, G, D)
        update(N, D)
        restrict_cells(N, mixed_out)
        to_pair(mixed_out, mixed_in, 2).start()

    store_state(N, out)

    @pl.when(level == 0)
    def _():
        whole(send1, recv1, 0).wait_send()
        whole(send2, recv2, 1).wait_send()
        to_pair(early_out, early_in, 0).wait_send()
        to_pair(faces_out, faces_in, 1).wait_send()

    @pl.when(level == 1)
    def _():
        whole(send3, recv3, 2).wait_send()
        to_pair(mixed_out, mixed_in, 2).wait_send()


def place_kernel(back, source, out, sems):
    copies = [
        pltpu.make_async_copy(source.at[back[b]], out.at[0, b], sems.at[b])
        for b in range(out.shape[1])
    ]
    for copy in copies:
        copy.start()
    for copy in copies:
        copy.wait()


def tables(neighbours, parents, level, me, count, devices):
    rows = lax.dynamic_slice_in_dim(neighbours, me * count, count, 0)
    family = lax.dynamic_slice_in_dim(parents, me * count, count, 0)
    ids = jnp.arange(count, dtype=jnp.int32)
    owner = family[:, 0] - me * count
    owns = owner[:, None] == ids[None, :]
    is_parent = jnp.any(owns, axis=0)
    earlier = ids[None, :] < ids[:, None]
    parent_rank = jnp.sum(is_parent[None, :] & earlier, axis=1, dtype=jnp.int32)
    rest_rank = ids - parent_rank
    coarse_place = jnp.where(
        is_parent, 8 * parent_rank, jnp.where(rest_rank < 7, 1 + rest_rank, 2 + rest_rank)
    )
    fine_place = 8 * jnp.sum(jnp.where(owns, parent_rank[None, :], 0), axis=1) + family[:, 1]
    place = jnp.where(level == 0, coarse_place, fine_place).astype(jnp.int32)

    def inverse(position):
        return jnp.sum(
            jnp.where(position[None, :] == ids[:, None], ids[None, :], 0), axis=1, dtype=jnp.int32
        )

    coarse_perm = inverse(coarse_place)
    chosen = coarse_perm[:, None] == ids[None, :]
    ordered = jnp.sum(jnp.where(chosen[:, :, None], rows[None], 0), axis=1, dtype=jnp.int32)
    ordered = ordered.T.reshape(-1)
    faces = jnp.repeat(jnp.arange(6, dtype=jnp.int32), count)
    target = ordered // count
    own_id = jnp.tile(coarse_perm, 6) * 6 + faces
    their_id = ordered % count * 6 + faces + 1 - 2 * (faces % 2)
    key = jnp.where(me < target, own_id, their_id)
    which = jnp.sum(
        (target[:, None] == target[None, :]) & (key[None, :] < key[:, None]),
        axis=1,
        dtype=jnp.int32,
    )
    far, mid, near = target // 16 - me // 16, target // 4 % 4 - me // 4 % 4, target % 4 - me % 4
    to = (far % 8) * 16 + (mid % 4) * 4 + near % 4 - 1
    come = (-far % 8) * 16 + (-mid % 4) * 4 + (-near) % 4 - 1
    item_ids = jnp.arange(6 * count, dtype=jnp.int32)
    slot_ids = jnp.arange(2 * devices, dtype=jnp.int32)
    slots = jnp.sum(
        jnp.where((2 * to + which)[None, :] == slot_ids[:, None], item_ids[None, :], 0),
        axis=1,
        dtype=jnp.int32,
    )
    return inverse(place), place, slots, come, which


def local(fluid_state, neighbours, parents):
    level = lax.axis_index("level")
    me = lax.axis_index("blk")
    devices = lax.axis_size("blk")
    count = fluid_state.shape[1]
    perm, place, slots, where, which = tables(
        neighbours, parents, level, me, count, devices
    )
    smem = pl.BlockSpec(memory_space=pltpu.SMEM)
    vmem = pl.BlockSpec(memory_space=pltpu.VMEM)
    peers = devices - 1

    def step(*refs):
        step_kernel(devices, *refs)

    result = pl.pallas_call(
        step,
        out_shape=jax.ShapeDtypeStruct(fluid_state.shape[1:], F32),
        in_specs=[smem] * 4 + [vmem],
        out_specs=vmem,
        scratch_shapes=[
            pltpu.VMEM((16, 5, 2, 2, 8, 128), F32),
            pltpu.VMEM((3, 5, 16, 4, 8, 128), F32),
            pltpu.VMEM((3, 5, 16, 4, 8, 128), F32),
            pltpu.VMEM((6, 5, 2, 4, 8, 128), F32),
            pltpu.VMEM((6, 5, 4, 8, 128), F32),
            pltpu.VMEM((4, 5, 4, 8, 128), F32),
            pltpu.VMEM((96, 3, 8, 128), F32),
            pltpu.VMEM((96, 3, 4, 128), F32),
            pltpu.VMEM((96, 3, 4, 128), F32),
            pltpu.VMEM((peers, 5, 8, 128), F32),
            pltpu.VMEM((peers, 5, 8, 128), F32),
            pltpu.VMEM((peers, 5, 4, 128), F32),
            pltpu.VMEM((peers, 5, 4, 128), F32),
            pltpu.VMEM((peers, 5, 4, 128), F32),
            pltpu.VMEM((peers, 5, 4, 128), F32),
            pltpu.VMEM((25, 8, 128), F32),
            pltpu.VMEM((25, 8, 128), F32),
            pltpu.VMEM((25, 8, 128), F32),
            pltpu.VMEM((25, 8, 128), F32),
            pltpu.VMEM((2, 5, 2, 2, 8, 128), F32),
            pltpu.VMEM((2, 5, 2, 2, 8, 128), F32),
            pltpu.VMEM((25, 8, 128), F32),
            pltpu.VMEM((25, 8, 128), F32),
            pltpu.SemaphoreType.DMA((3,)),
            pltpu.SemaphoreType.DMA((3,)),
            pltpu.SemaphoreType.DMA((3,)),
            pltpu.SemaphoreType.DMA((3,)),
            pltpu.SemaphoreType.REGULAR,
            pltpu.VMEM((14, 8, 128), F32),
            pltpu.VMEM((4, 8, 128), F32),
        ],
        compiler_params=pltpu.CompilerParams(
            collective_id=0, has_side_effects=True, vmem_limit_bytes=34 * 1024 * 1024
        ),
    )(perm, slots, where, which, fluid_state)
    return pl.pallas_call(
        place_kernel,
        out_shape=jax.ShapeDtypeStruct(fluid_state.shape, F32),
        in_specs=[smem, vmem],
        out_specs=pl.BlockSpec(memory_space=pl.ANY),
        scratch_shapes=[pltpu.SemaphoreType.DMA((count,))],
        compiler_params=pltpu.CompilerParams(vmem_limit_bytes=8 * 1024 * 1024),
    )(place, result)


def solution(mesh):
    return jax.shard_map(
        local,
        mesh=mesh,
        in_specs=(P("level", "blk", None, None, None), P(), P()),
        out_specs=P("level", "blk", None, None, None),
        check_vma=False,
    )
```
